256 devices in a mesh: frag: 64 (over z, y, core), tile: 4 (over x).
Axes of the slice: x: 4, y: 4, z: 8, core: 2. Of those that a mesh axis runs over, the one named last changes fastest.
Arguments:
- core_fock: float32 [512, 256, 256], P('frag', 'tile'), as said below
- intersection: float32 [512, 256, 256], P('frag', 'tile'), as said below
- gamma_tile: float32 [512, 256, 256], P('frag', 'tile'), may hold values from -0.375 to 0.375
- charge_old: float32 [512, 256], P('frag'), may hold values from -6 to 6
- embed_old: float32 [512, 256], P('frag'), may hold values from -4 to 4
- core_pop: float32 [512, 256], P('frag'), may hold values from 0 to 1
- centres: float32 [512, 3, 256], P('frag'), may hold values from -10 to 10
- frag_sizes: int32 [512], P('frag'), may hold values from 20 to 256, as said below
- near_list: int32 [512, 8], P('frag'), may hold values from 0 to 511, as said below
- far_list: int32 [512, 8], P('frag'), may hold values from 0 to 511
Outputs:
- density: float32 [512, 256, 256], P('frag', 'tile')
- esp_matrix: float32 [512, 256, 256], P('frag', 'tile')
The draws below stay inside these ranges and needn't reach their ends.
Inputs may be any that keep to these rules, and one draw needn't show every extreme that they name: `frag_sizes`: each fragment uses at least 20 basis functions; some fragment uses exactly 256. near_list[f, k] is a fragment whose index differs from f by 1 to 8; the distance 8 occurs. `core_fock`: symmetric in its last two dimensions. `intersection`: symmetric in its last two dimensions.
All inputs are finite; a program needn't handle non-finite values.
Results may differ from the reference program's by a relative error of at most 0.0003.
Values sent between devices are 32-bit elements; how exact they have to be, the bound alone decides.
A program may use at most 64 MiB of HBM per device.

```python
import math
import jax
import jax.numpy as jnp
from jax import lax

BASIS = 256
NEAR = 8
FAR = 8
PC = 8
ITERS = 12
SPAN = 8
FRAGS = 512


def draw_core_fock(key, part):
    first, second = jax.random.split(jax.random.fold_in(key, 11))
    noise = jax.random.normal(first, (FRAGS, BASIS, BASIS), jnp.float32)
    symmetric = (noise + jnp.transpose(noise, (0, 2, 1))) * (0.5 / math.sqrt(BASIS))
    levels = jax.random.uniform(second, (FRAGS, BASIS), jnp.float32, -1.5, 1.5)
    result = symmetric + levels[:, :, None] * jnp.eye(BASIS, dtype=jnp.float32)[None]
    return result


def draw_intersection(key, part):
    noise = jax.random.normal(jax.random.fold_in(key, 23), (FRAGS, BASIS, BASIS), jnp.float32)
    symmetric = (noise + jnp.transpose(noise, (0, 2, 1))) * (0.2 / math.sqrt(BASIS))
    return jnp.eye(BASIS, dtype=jnp.float32)[None] + symmetric


def draw_frag_sizes(key, part):
    first, second = jax.random.split(jax.random.fold_in(key, 37))
    counts = jax.random.randint(first, (FRAGS,), 20, BASIS + 1)
    spot = jax.random.randint(second, (), 0, FRAGS)
    return counts.at[spot].set(BASIS).astype(jnp.int32)


def draw_near_list(key, part):
    first, second = jax.random.split(jax.random.fold_in(key, 41))
    offsets = jax.random.randint(first, (FRAGS, NEAR), 1, SPAN + 1)
    upward = jax.random.randint(second, (FRAGS, NEAR), 0, 2)
    anchor = jnp.arange(FRAGS, dtype=jnp.int32)[:, None]
    higher = anchor + offsets
    lower = anchor - offsets
    chosen = jnp.where(upward > 0, higher, lower)
    outside = (chosen < 0) | (chosen >= FRAGS)
    other = jnp.where(upward > 0, lower, higher)
    return jnp.where(outside, other, chosen).astype(jnp.int32)


def with_ends(array, stream_key, least, largest):
    extent = array.shape
    spot = [jax.random.randint(jax.random.fold_in(stream_key, axis), (), 0, extent[axis]) for axis in range(len(extent))]
    array = array.at[tuple(spot)].set(least)
    longest = extent.index(max(extent))
    spot[longest] = (spot[longest] + 1) % extent[longest]
    return array.at[tuple(spot)].set(largest)


def block_levels(key, dims, cuts, smallest, largest):
    factor_of, own = 1.0, jax.random.fold_in(key, 6)
    for position, parts in cuts:
        draws = jnp.exp(jax.random.uniform(jax.random.fold_in(own, position), (parts,), jnp.float32, smallest / len(cuts), largest / len(cuts)))
        factor_of = factor_of * jnp.repeat(draws, dims[position] // parts).reshape([-1 if axis == position else 1 for axis in range(len(dims))])
    return factor_of


def bell_draw(key, shape, scale, limit, pieces=(), kind=jnp.bfloat16):
    values = jax.random.normal(key, shape, jnp.float32) * scale
    if len(pieces) > 0:
        values = block_levels(key, shape, pieces, -0.22, 0.18) * values
    return jnp.clip(values, min=-limit, max=limit).astype(kind)


def setup_inputs(seed: int = 0) -> dict:
    streams_of = jax.random.split(jax.random.key(seed), 11)
    return {
        "core_fock": draw_core_fock(jax.random.fold_in(streams_of[10], 71), 0),
        "intersection": draw_intersection(jax.random.fold_in(streams_of[10], 71), 0),
        "gamma_tile": bell_draw(streams_of[2], (FRAGS, BASIS, BASIS), BASIS ** -0.5, 0.375, ((0, 64), (1, 4)), jnp.float32),
        "charge_old": bell_draw(streams_of[3], (FRAGS, BASIS), 1.0, 6.0, ((0, 64),), jnp.float32),
        "embed_old": bell_draw(streams_of[4], (FRAGS, BASIS), 0.5, 4.0, ((0, 64),), jnp.float32),
        "core_pop": jnp.clip(1.0 * jax.random.uniform(streams_of[5], (FRAGS, BASIS), jnp.float32) ** block_levels(streams_of[5], (FRAGS, BASIS), ((0, 64),), -0.2, 0.2), 0.0, 1.0),
        "centres": bell_draw(streams_of[6], (FRAGS, 3, BASIS), 2.0, 10.0, ((0, 64),), jnp.float32),
        "frag_sizes": draw_frag_sizes(jax.random.fold_in(streams_of[10], 71), 0),
        "near_list": draw_near_list(jax.random.fold_in(streams_of[10], 71), 0),
        "far_list": with_ends(jax.random.randint(streams_of[9], (FRAGS, FAR), 0, FRAGS), jax.random.fold_in(streams_of[9], 1), 0, FRAGS - 1).astype(jnp.int32),
    }


precise = lax.Precision.HIGHEST
screening = 0.25

def coulomb(centre_set, source):
    dist_sq = (centre_set[0][:, None] - source[1][None, :]) ** 2
    dist_sq = dist_sq + (centre_set[1][:, None] - source[2][None, :]) ** 2
    dist_sq = dist_sq + (centre_set[2][:, None] - source[3][None, :]) ** 2
    return lax.optimization_barrier(jnp.sum(source[0][None, :] * lax.rsqrt(dist_sq + 1.0), axis=1))

def purify(fock_matrix, frag_size):
    column_index = jnp.arange(BASIS, dtype=jnp.int32)
    active = (column_index < frag_size).astype(jnp.float32)
    masked = fock_matrix * active[:, None] * active[None, :]
    frob_norm = jnp.sqrt(jnp.sum(masked * masked) + 1e-06)
    identity = jnp.eye(BASIS, dtype=jnp.float32)
    sign_est = masked / frob_norm + identity * (1.0 - active)[:, None]
    for sweep_index in range(ITERS):
        squared = jnp.dot(sign_est, sign_est, precision=precise)
        sign_est = 1.5 * sign_est - 0.5 * jnp.dot(squared, sign_est, precision=precise)
    return 0.5 * (identity - sign_est)

def reference(core_fock, intersection, gamma_tile, charge_old, embed_old, core_pop, centres, frag_sizes, near_list, far_list):

    def one_fragment(inputs):
        core_one, over_one, gamma_one, charge_one, embed_one, size_one = inputs
        field = jnp.dot(gamma_one, charge_one, precision=precise) + embed_one
        fock_matrix = core_one + 0.5 * over_one * (field[:, None] + field[None, :])
        return purify(fock_matrix, size_one)
    density = lax.map(one_fragment, (core_fock, intersection, gamma_tile, charge_old, embed_old, frag_sizes))
    charges = lax.optimization_barrier(jnp.sum(density * intersection, axis=2)) - core_pop
    table = jnp.concatenate([charges[:, None, :], centres], axis=1)
    group = BASIS // PC
    block_charge = lax.optimization_barrier(jnp.sum(charges.reshape(FRAGS, PC, group), axis=2))
    block_place = lax.optimization_barrier(jnp.mean(centres.reshape(FRAGS, 3, PC, group), axis=3))
    blocks = jnp.concatenate([block_charge[:, None, :], block_place], axis=1)

    def potential_of(inputs):
        centre_set, near_ids, far_ids = inputs

        def add_near(summed, neighbour):
            return (summed + coulomb(centre_set, table[neighbour]), None)
        summed, unused = lax.scan(add_near, jnp.zeros((BASIS,), jnp.float32), near_ids)
        far_source = jnp.transpose(blocks[far_ids], (1, 0, 2)).reshape(4, -1)
        return screening * (summed + coulomb(centre_set, far_source))
    potential = lax.map(potential_of, (centres, near_list, far_list))
    esp_matrix = 0.5 * intersection * (potential[:, :, None] + potential[:, None, :])
    return (density, esp_matrix)
```

```python
import functools
import jax
import jax.numpy as jnp
from jax import lax
from jax.experimental import pallas as pl
from jax.experimental.pallas import tpu as pltpu
from jax.sharding import PartitionSpec as P

ITERS = 12
TILES = 4
ROWS = 64
BASIS = 256
PER = 8
OWN = 2
PC = 8
LIST = 8
PLANES = 8

f32 = jnp.float32
bf16 = jnp.bfloat16
HI = lax.Precision.HIGHEST
MESH = pl.DeviceIdType.MESH


def dot_nt(a, b):
    return lax.dot_general(a, b, (((1,), (1,)), ((), ())), precision=HI, preferred_element_type=f32)


def split(x):
    high = x.astype(bf16)
    return high, (x - high.astype(f32)).astype(bf16)


def dot3(a, b):
    (ah, al), (bh, bl) = a, b
    mul = functools.partial(jnp.dot, preferred_element_type=f32)
    return mul(ah, bh) + mul(ah, bl) + mul(al, bh)


def lanes(shape):
    return lax.broadcasted_iota(jnp.int32, shape, len(shape) - 1)


def turn(x):
    return pltpu.roll(x, ROWS, axis=1)


def kernel(
    planes,
    groups,
    core_hbm,
    over_hbm,
    gamma_hbm,
    charge_hbm,
    embed_hbm,
    pop_hbm,
    centre_hbm,
    size_sm,
    near_sm,
    far_hbm,
    density_out,
    esp_out,
    core_v,
    over_v,
    gamma_v,
    charge_v,
    embed_v,
    pop_v,
    far_v,
    core_r,
    over_r,
    send1,
    send2,
    send3,
    got1,
    got2,
    got3,
    field_s,
    field_g,
    near_c,
    all_c,
    place_t,
    col_b,
    kern_n,
    kern_f,
    est,
    over_f,
    dens_s,
    table,
    block_t,
    col_s,
    in_sem,
    raw_send,
    raw_recv,
    fld_send,
    fld_recv,
    nc_send,
    nc_recv,
    ac_send,
    ac_recv,
    pl_send,
    pl_recv,
    tb_send,
    tb_recv,
    bd_send,
    bd_recv,
    bk_send,
    bk_recv,
    dn_send,
    dn_recv,
    out_sem,
):
    plane_frags = groups * PER
    plane_peers = groups * TILES
    at_f = lax.axis_index("frag")
    at_t = lax.axis_index("tile")
    at_z = at_f // groups
    at_g = lax.rem(at_f, groups)
    at_p = at_g * TILES + at_t
    frag_devs = planes * groups

    def tile_peer(step):
        return (at_f, lax.rem(at_t + step, TILES))

    def frag_peer(step):
        return (lax.rem(at_f + frag_devs + step, frag_devs), at_t)

    def plane_peer(step):
        peer = lax.rem(at_p + step, plane_peers)
        return (at_z * groups + peer // TILES, lax.rem(peer, TILES))

    def group_peer(step):
        return (at_z * groups + lax.rem(at_g + step, groups), at_t)

    def z_peer(step):
        return (lax.rem(at_z + planes + step, planes) * groups + at_g, at_t)

    barrier = pltpu.get_barrier_semaphore()

    def greet(device):
        pl.semaphore_signal(barrier, inc=1, device_id=device, device_id_type=MESH)

    def greet_plane(step, carry):
        greet(plane_peer(step))
        return carry

    def greet_z(step, carry):
        greet(z_peer(step))
        return carry

    lax.fori_loop(1, plane_peers, greet_plane, 0)
    lax.fori_loop(1, planes, greet_z, 0)
    greet(frag_peer(1))
    greet(frag_peer(-1))

    loads = [
        pltpu.make_async_copy(src, dst, in_sem.at[n])
        for n, (src, dst) in enumerate(
            (
                (core_hbm, core_v),
                (over_hbm, over_v),
                (gamma_hbm, gamma_v),
                (charge_hbm, charge_v),
                (embed_hbm, embed_v),
                (pop_hbm, pop_v),
                (far_hbm, far_v),
                (centre_hbm, near_c.at[1]),
                (centre_hbm, all_c.at[at_g]),
            )
        )
    ]
    for load in loads:
        load.start()

    back = lax.rem(BASIS - ROWS * at_t, BASIS)
    forth = ROWS * at_t
    lane128 = lanes((ROWS, 128))
    low = lane128 < ROWS
    to_prev = lax.rem(at_t + 3, TILES)
    to_opp = lax.rem(at_t + 2, TILES)
    to_next = lax.rem(at_t + 1, TILES)
    for n, (array, turned) in enumerate(((core_v, core_r), (over_v, over_r))):
        loads[n].wait()
        for f in range(PER):
            turned[f] = pltpu.roll(array[f], back, axis=1)
        firsts, pairs = [], []
        for e in range(OWN):
            mine = turned[OWN * to_prev + e]
            send1[n, e] = turn(mine[:, :128])
            firsts.append(mine[:, 128:])
            mine = turned[OWN * to_next + e]
            send3[n, e] = jnp.where(low, turn(mine[:, 128:]), turn(mine[:, :128]))
            pairs.append(turned[OWN * to_opp + e][:, :128])
        send1[n, 2] = jnp.where(low, firsts[0], turn(firsts[1]))
        send2[n, 0] = jnp.where(low, pairs[0], turn(pairs[1]))

    pl.semaphore_wait(barrier, (plane_peers - 1) + (planes - 1) + 2)

    sends = []

    def push(src, dst, send_sem, recv_sem, device):
        copy = pltpu.make_async_remote_copy(
            src_ref=src,
            dst_ref=dst,
            send_sem=send_sem,
            recv_sem=recv_sem,
            device_id=device,
            device_id_type=MESH,
        )
        copy.start()
        sends.append(copy)
        return copy

    raw = [
        push(send2, got2, raw_send.at[1], raw_recv.at[1], tile_peer(2)),
        push(send1, got1, raw_send.at[0], raw_recv.at[0], tile_peer(3)),
        push(send3, got3, raw_send.at[2], raw_recv.at[2], tile_peer(1)),
    ]
    near = [
        push(centre_hbm, near_c.at[0], nc_send.at[0], nc_recv.at[0], frag_peer(1)),
        push(centre_hbm, near_c.at[2], nc_send.at[1], nc_recv.at[1], frag_peer(-1)),
    ]

    def spread_centres(step, carry):
        pltpu.make_async_remote_copy(
            src_ref=centre_hbm,
            dst_ref=all_c.at[at_g],
            send_sem=ac_send,
            recv_sem=ac_recv,
            device_id=group_peer(step),
            device_id_type=MESH,
        ).start()
        return carry

    lax.fori_loop(1, groups, spread_centres, 0)

    for n in (2, 3, 4):
        loads[n].wait()
    wide = (PER, PER * ROWS)
    prod = dot_nt(charge_v[...], gamma_v[...].reshape(PER * ROWS, BASIS))
    emb = pltpu.roll(embed_v[...], back, axis=1)[:, :128]
    emb = jnp.where(lanes((PER, 128)) < ROWS, emb, turn(emb))
    prod = prod + jnp.concatenate([emb] * 4, axis=1)
    same = lax.broadcasted_iota(jnp.int32, wide, 0) == lanes(wide) // ROWS
    fields = jnp.sum(jnp.where(same, prod, 0.0), axis=0, keepdims=True)
    for t in range(TILES):
        field_s[t] = fields[:, 128 * t : 128 * t + 128]
    fld = []
    for r in (2, 1, 3):
        dest = lax.rem(at_t + TILES - r, TILES)
        fld.append(
            push(field_s.at[dest], field_g.at[r], fld_send.at[r - 1], fld_recv.at[r - 1], (at_f, dest))
        )

    loads[7].wait()
    own = near_c[1].reshape(3 * PER, BASIS)
    cols = jnp.transpose(jnp.concatenate([own, jnp.zeros((128 - 3 * PER, BASIS), f32)], axis=0))
    for f in range(PER):
        for d in range(3):
            n = d * PER + f
            col_b[f, d] = jnp.broadcast_to(cols[:, n : n + 1], (BASIS, 128))
    for copy in near:
        copy.wait_recv()
    near_first = at_f * PER - PER

    def pair(n, carry):
        f = n // LIST
        other = jnp.clip(near_sm[f, lax.rem(n, LIST)] - near_first, 0, 3 * PER - 1)
        slot = other // PER
        row = other - slot * PER
        src = [near_c[slot, d, pl.ds(row, 1), :] for d in range(3)]
        for r in range(4):
            rows = slice(64 * r, 64 * r + 64)
            for h in range(2):
                cut = slice(128 * h, 128 * h + 128)
                dist = 1.0
                for d in range(3):
                    diff = col_b[f, d, rows, :] - src[d][:, cut]
                    dist = dist + diff * diff
                kern_n[n, rows, cut] = lax.rsqrt(dist)
        return carry

    lax.fori_loop(0, PER * LIST, pair, 0)

    loads[8].wait()
    pltpu.make_async_copy(
        all_c.at[pl.ds(0, groups - 1)], all_c.at[pl.ds(0, groups - 1)], ac_recv
    ).wait()
    runs = lax.broadcasted_iota(jnp.int32, (PC, BASIS), 0) == lanes((PC, BASIS)) // (BASIS // PC)
    sum_run = runs.astype(f32)
    mean_run = sum_run * (PC / BASIS)
    pad = jnp.zeros((PC, 128 - plane_frags), f32)
    for d in range(3):
        places = dot_nt(mean_run, all_c[:, d].reshape(plane_frags, BASIS))
        place_t[at_z, d] = jnp.concatenate([places, pad], axis=1)

    def spread_places(step, carry):
        pltpu.make_async_remote_copy(
            src_ref=place_t.at[at_z],
            dst_ref=place_t.at[at_z],
            send_sem=pl_send,
            recv_sem=pl_recv,
            device_id=z_peer(step),
            device_id_type=MESH,
        ).start()
        return carry

    lax.fori_loop(1, planes, spread_places, 0)

    fld_rows = [field_s[at_t]]
    for copy in fld:
        copy.wait_recv()
    for r in (1, 2, 3):
        fld_rows.append(field_g[r])
    for copy in raw:
        copy.wait_recv()
    full_lanes = lanes((1, BASIS))
    low1 = lanes((1, 128)) < ROWS
    zero = jnp.zeros((ROWS, 128), f32)

    def halves(n, turned, e):
        top = turned[OWN * at_t + e]
        top = jnp.where(lanes((ROWS, BASIS)) < ROWS, 0.5 * top, top)
        one = got1[n, e]
        tail = got1[n, 2]
        tail = turn(tail) if e == 0 else tail
        opp = got2[n, 0]
        opp = opp if e == 0 else turn(opp)
        last = got3[n, e]
        return jnp.concatenate(
            [
                top,
                jnp.concatenate([jnp.where(low, 0.0, 0.5 * one), jnp.where(low, one, tail)], axis=1),
                jnp.concatenate([zero, jnp.where(low, 0.5 * opp, 0.0)], axis=1),
                jnp.concatenate([zero, jnp.where(low, last, 0.5 * last)], axis=1),
            ],
            axis=0,
        )

    square = (BASIS, BASIS)
    row_at = lax.broadcasted_iota(jnp.int32, square, 0)
    col_at = lanes(square)
    eye = (row_at == col_at).astype(f32)
    for e in range(OWN):
        half = halves(1, over_r, e)
        over = half + jnp.transpose(half)
        over_f[e] = over
        if e == 0:
            field = [jnp.where(low1, fld_rows[0], turn(fld_rows[1])), jnp.where(low1, fld_rows[2], turn(fld_rows[3]))]
        else:
            field = [jnp.where(low1, turn(fld_rows[0]), fld_rows[1]), jnp.where(low1, turn(fld_rows[2]), fld_rows[3])]
        field = jnp.concatenate(field, axis=1)
        half = halves(0, core_r, e) + 0.5 * over * field
        fock = half + jnp.transpose(half)
        size = size_sm[OWN * at_t + e]
        row_in = lax.rem(row_at + ROWS * at_t, BASIS) < size
        col_in = lax.rem(col_at + ROWS * at_t, BASIS) < size
        fock = jnp.where(row_in & col_in, fock, 0.0)
        total = jnp.sum(jnp.sum(fock * fock, axis=0, keepdims=True), axis=1, keepdims=True)
        fock = fock / jnp.sqrt(total + 1e-06)
        est[e] = fock + jnp.where(row_in, 0.0, eye)

    def sweep(step, carry):
        parts = [split(est[e]) for e in range(OWN)]
        squares = [split(dot3(parts[e], parts[e])) for e in range(OWN)]
        for e in range(OWN):
            est[e] = 1.5 * est[e] - 0.5 * dot3(squares[e], parts[e])
        return carry

    lax.fori_loop(0, ITERS, sweep, 0)

    loads[5].wait()
    first = PER + at_g * PER + OWN * at_t
    for e in range(OWN):
        dens = 0.5 * (eye - est[e])
        charge = jnp.sum(dens * over_f[e], axis=0, keepdims=True)
        charge = pltpu.roll(jnp.broadcast_to(charge, (8, BASIS)), forth, axis=1)[0:1]
        charge = charge - pop_v[pl.ds(OWN * at_t + e, 1), :]
        table[first + e] = charge

    def spread_charges(step, carry):
        pltpu.make_async_remote_copy(
            src_ref=table.at[pl.ds(first, OWN)],
            dst_ref=table.at[pl.ds(first, OWN)],
            send_sem=tb_send,
            recv_sem=tb_recv,
            device_id=plane_peer(step),
            device_id_type=MESH,
        ).start()
        return carry

    lax.fori_loop(1, plane_peers, spread_charges, 0)

    for e in range(OWN):
        dens = pltpu.roll(0.5 * (eye - est[e]), forth, axis=1)
        for r in range(TILES):
            dens_s[r, e] = dens[ROWS * r : ROWS * r + ROWS]
    slot = density_out.at[pl.ds(OWN * at_t, OWN)]
    den = [push(dens_s.at[r], slot, dn_send.at[r - 1], dn_recv.at[r - 1], tile_peer(r)) for r in (2, 1, 3)]
    keep = pltpu.make_async_copy(dens_s.at[0], slot, out_sem.at[0])
    keep.start()

    loads[6].wait()
    far_list = far_v[...].astype(f32)
    diag = lax.broadcasted_iota(jnp.int32, (LIST, LIST), 0) == lanes((LIST, LIST))
    far_at = [
        jnp.sum(jnp.where(diag, jnp.broadcast_to(far_list[f : f + 1], (LIST, LIST)), 0.0), axis=1, keepdims=True)
        for f in range(PER)
    ]
    far_at = jnp.broadcast_to(jnp.concatenate(far_at, axis=0), (PER * LIST, 128))
    lane64 = lanes((PER * LIST, 128))
    picks = []
    for z in range(planes):
        entry = jnp.where(lane64 < plane_frags, lane64 + z * plane_frags, -1).astype(f32)
        picks.append((far_at == entry).astype(f32))
    pick = jnp.concatenate(picks, axis=1)
    pltpu.make_async_copy(
        place_t.at[pl.ds(0, planes - 1)], place_t.at[pl.ds(0, planes - 1)], pl_recv
    ).wait()
    far_place = [
        dot_nt(pick, jnp.concatenate([place_t[z, d] for z in range(planes)], axis=1)) for d in range(3)
    ]
    spots = [
        jnp.concatenate([jnp.broadcast_to(near_c[1, d, f : f + 1, :], (LIST, BASIS)) for f in range(PER)], axis=0)
        for d in range(3)
    ]
    for p in range(PC):
        dist = 1.0
        for d in range(3):
            diff = spots[d] - far_place[d][:, p : p + 1]
            dist = dist + diff * diff
        kern_f[p] = lax.rsqrt(dist)

    pltpu.make_async_copy(
        table.at[pl.ds(PER, plane_frags - OWN)], table.at[pl.ds(PER, plane_frags - OWN)], tb_recv
    ).wait()
    plane_charge = table[pl.ds(PER, plane_frags)].reshape(plane_frags, BASIS)
    block_t[at_z] = jnp.concatenate([dot_nt(sum_run, plane_charge), pad], axis=1)

    edge = [
        push(table.at[pl.ds(plane_frags, PER)], table.at[pl.ds(0, PER)], bd_send.at[0], bd_recv.at[0], z_peer(1)),
        push(table.at[pl.ds(PER, PER)], table.at[pl.ds(plane_frags + PER, PER)], bd_send.at[1], bd_recv.at[1], z_peer(-1)),
    ]

    def spread_blocks(step, carry):
        pltpu.make_async_remote_copy(
            src_ref=block_t.at[at_z],
            dst_ref=block_t.at[at_z],
            send_sem=bk_send,
            recv_sem=bk_recv,
            device_id=z_peer(step),
            device_id_type=MESH,
        ).start()
        return carry

    lax.fori_loop(1, planes, spread_blocks, 0)

    for copy in edge:
        copy.wait_recv()
    table_first = at_z * plane_frags - PER
    lane256 = lanes((BASIS, 128))
    near_cols = jnp.zeros((BASIS, 128), f32)

    def near_sum(f):
        acc = jnp.zeros((BASIS, 128), f32)
        for k in range(LIST):
            row = table[jnp.clip(near_sm[f, k] - table_first, 0, plane_frags + 2 * PER - 1)]
            acc = acc + kern_n[f * LIST + k, :, :128] * row[:, :128]
            acc = acc + kern_n[f * LIST + k, :, 128:] * row[:, 128:]
        return jnp.sum(acc, axis=1, keepdims=True)

    def near_step(f, cols):
        return jnp.where(lane256 == f, near_sum(f), cols)

    near_cols = lax.fori_loop(0, PER, near_step, near_cols)
    near_rows = jnp.transpose(near_cols)[:PER]

    pltpu.make_async_copy(
        block_t.at[pl.ds(0, planes - 1)], block_t.at[pl.ds(0, planes - 1)], bk_recv
    ).wait()
    far_charge = dot_nt(pick, jnp.concatenate([block_t[z] for z in range(planes)], axis=1))
    far_sum = jnp.zeros((PER * LIST, BASIS), f32)
    for p in range(PC):
        far_sum = far_sum + far_charge[:, p : p + 1] * kern_f[p]
    far_rows = jnp.sum(far_sum.reshape(PER, LIST, BASIS), axis=1)
    potential = 0.25 * (near_rows + far_rows)
    col_s[...] = jnp.transpose(jnp.concatenate([potential, jnp.zeros((128 - PER, BASIS), f32)], axis=0))
    mine = col_s[pl.ds(ROWS * at_t, ROWS), :]
    for f in range(PER):
        esp_out[f] = 0.5 * over_v[f] * (mine[:, f : f + 1] + potential[f : f + 1, :])

    for copy in den:
        copy.wait_recv()
    keep.wait()
    for copy in sends:
        copy.wait_send()
    for ref, count, sem in (
        (all_c, groups - 1, ac_send),
        (place_t, planes - 1, pl_send),
        (table, plane_frags - OWN, tb_send),
        (block_t, planes - 1, bk_send),
    ):
        pltpu.make_async_copy(ref.at[pl.ds(0, count)], ref.at[pl.ds(0, count)], sem).wait()


def per_device(
    planes,
    groups,
    core_fock,
    intersection,
    gamma_tile,
    charge_old,
    embed_old,
    core_pop,
    centres,
    frag_sizes,
    near_list,
    far_list,
):
    dma = pltpu.SemaphoreType.DMA
    anyspace = pl.BlockSpec(memory_space=pl.ANY)
    smem = pl.BlockSpec(memory_space=pltpu.SMEM)
    vmem = pl.BlockSpec(memory_space=pltpu.VMEM)
    own = (PER, ROWS, BASIS)
    pieces = (ROWS, 128)
    plane_frags = groups * PER
    return pl.pallas_call(
        functools.partial(kernel, planes, groups),
        out_shape=(jax.ShapeDtypeStruct(own, f32), jax.ShapeDtypeStruct(own, f32)),
        in_specs=[anyspace] * 7 + [smem, smem, anyspace],
        out_specs=(anyspace, vmem),
        scratch_shapes=[
            pltpu.VMEM(own, f32),
            pltpu.VMEM(own, f32),
            pltpu.VMEM(own, f32),
            pltpu.VMEM((PER, BASIS), f32),
            pltpu.VMEM((PER, BASIS), f32),
            pltpu.VMEM((PER, BASIS), f32),
            pltpu.VMEM((PER, LIST), jnp.int32),
            pltpu.VMEM(own, f32),
            pltpu.VMEM(own, f32),
            pltpu.VMEM((2, 3) + pieces, f32),
            pltpu.VMEM((2, 1) + pieces, f32),
            pltpu.VMEM((2, 2) + pieces, f32),
            pltpu.VMEM((2, 3) + pieces, f32),
            pltpu.VMEM((2, 1) + pieces, f32),
            pltpu.VMEM((2, 2) + pieces, f32),
            pltpu.VMEM((TILES, 1, 128), f32),
            pltpu.VMEM((TILES, 1, 128), f32),
            pltpu.VMEM((3, 3, PER, BASIS), f32),
            pltpu.VMEM((groups, 3, PER, BASIS), f32),
            pltpu.VMEM((planes, 3, PC, 128), f32),
            pltpu.VMEM((PER, 3, BASIS, 128), f32),
            pltpu.VMEM((PER * LIST, BASIS, BASIS), f32),
            pltpu.VMEM((PC, PER * LIST, BASIS), f32),
            pltpu.VMEM((OWN, BASIS, BASIS), f32),
            pltpu.VMEM((OWN, BASIS, BASIS), f32),
            pltpu.VMEM((TILES, OWN, ROWS, BASIS), f32),
            pltpu.VMEM((plane_frags + 2 * PER, 1, BASIS), f32),
            pltpu.VMEM((planes, PC, 128), f32),
            pltpu.VMEM((BASIS, 128), f32),
            dma((9,)),
            dma((3,)),
            dma((3,)),
            dma((3,)),
            dma((3,)),
            dma((2,)),
            dma((2,)),
            dma,
            dma,
            dma,
            dma,
            dma,
            dma,
            dma((2,)),
            dma((2,)),
            dma,
            dma,
            dma((3,)),
            dma((3,)),
            dma((1,)),
        ],
        compiler_params=pltpu.CompilerParams(
            collective_id=0, has_side_effects=True, vmem_limit_bytes=60 * 1024 * 1024
        ),
        name="scc_cycle",
    )(
        core_fock,
        intersection,
        gamma_tile,
        charge_old,
        embed_old,
        core_pop,
        jnp.transpose(centres, (1, 0, 2)),
        frag_sizes,
        near_list,
        far_list,
    )


def solution(mesh):
    groups = mesh.shape["frag"] // PLANES
    return build(mesh, PLANES, groups)


def build(mesh, planes, groups):
    in_specs = (
        P("frag", "tile", None),
        P("frag", "tile", None),
        P("frag", "tile", None),
        P("frag", None),
        P("frag", None),
        P("frag", None),
        P("frag", None, None),
        P("frag"),
        P("frag", None),
        P("frag", None),
    )
    out_specs = (P("frag", "tile", None), P("frag", "tile", None))
    return jax.shard_map(
        functools.partial(per_device, planes, groups),
        mesh=mesh,
        in_specs=in_specs,
        out_specs=out_specs,
        check_vma=False,
    )
```

```python
import functools
import jax
import jax.numpy as jnp
from jax import lax
from jax.experimental import pallas as pl
from jax.experimental.pallas import tpu as pltpu
from jax.sharding import PartitionSpec as P

ITERS = 12
TILES = 4
ROWS = 64
BASIS = 256
PER = 8
OWN = 2
PC = 8
LIST = 8
PLANES = 8
FIRST_PAIRS = 34
NEXT_PAIRS = 50

f32 = jnp.float32
bf16 = jnp.bfloat16
HI = lax.Precision.HIGHEST
MESH = pl.DeviceIdType.MESH


def dot_nt(a, b):
    return lax.dot_general(a, b, (((1,), (1,)), ((), ())), precision=HI, preferred_element_type=f32)


def split(x):
    high = x.astype(bf16)
    return high, (x - high.astype(f32)).astype(bf16)


def dot3(a, b):
    (ah, al), (bh, bl) = a, b
    mul = functools.partial(jnp.dot, preferred_element_type=f32)
    return mul(ah, bh) + mul(ah, bl) + mul(al, bh)


def pick_nt(sel, b):
    high = b.astype(bf16)
    rest = b - high.astype(f32)
    middle = rest.astype(bf16)
    least = (rest - middle.astype(f32)).astype(bf16)
    mul = functools.partial(
        lax.dot_general, dimension_numbers=(((1,), (1,)), ((), ())), preferred_element_type=f32
    )
    return mul(sel, high) + mul(sel, middle) + mul(sel, least)


def lanes(shape):
    return lax.broadcasted_iota(jnp.int32, shape, len(shape) - 1)


def turn(x):
    return pltpu.roll(x, ROWS, axis=1)


def kernel(
    planes,
    groups,
    core_hbm,
    over_hbm,
    gamma_hbm,
    charge_hbm,
    embed_hbm,
    pop_hbm,
    centre_hbm,
    size_sm,
    near_sm,
    far_hbm,
    density_out,
    esp_out,
    core_v,
    over_v,
    gamma_v,
    charge_v,
    embed_v,
    pop_v,
    far_v,
    core_r,
    over_r,
    send1,
    send2,
    send3,
    got1,
    got2,
    got3,
    field_s,
    field_g,
    near_c,
    all_c,
    place_t,
    col_b,
    kern_n,
    kern_f,
    est,
    over_f,
    dens_s,
    table,
    block_t,
    col_s,
    in_sem,
    raw_send,
    raw_recv,
    fld_send,
    fld_recv,
    nc_send,
    nc_recv,
    ac_send,
    ac_recv,
    pl_send,
    pl_recv,
    tb_send,
    tb_recv,
    bd_send,
    bd_recv,
    bk_send,
    bk_recv,
    dn_send,
    dn_recv,
    out_sem,
):
    plane_frags = groups * PER
    plane_peers = groups * TILES
    at_f = lax.axis_index("frag")
    at_t = lax.axis_index("tile")
    at_z = at_f // groups
    at_g = lax.rem(at_f, groups)
    frag_devs = planes * groups

    def tile_peer(step):
        return (at_f, lax.rem(at_t + step, TILES))

    def frag_peer(step):
        return (lax.rem(at_f + frag_devs + step, frag_devs), at_t)

    deep = groups // 2
    ring = lambda n, size: min(n, size - n)
    steps = [(dx, dy, dc) for dx in range(TILES) for dy in range(deep) for dc in range(2)][1:]
    steps.sort(key=lambda s: (-ring(s[0], TILES) - ring(s[1], deep), -s[2]))
    at_c = lax.rem(at_g, 2)
    peer_x = [lax.rem(at_t + dx, TILES) for dx in range(TILES)]
    peer_g = [
        [at_z * groups + 2 * lax.rem(at_g // 2 + dy, deep) + (1 - at_c if dc else at_c) for dc in range(2)]
        for dy in range(deep)
    ]
    plane_devices = [(peer_g[dy][dc], peer_x[dx]) for dx, dy, dc in steps]

    def group_peer(step):
        return (at_z * groups + lax.rem(at_g + step, groups), at_t)

    def z_peer(step):
        return (lax.rem(at_z + planes + step, planes) * groups + at_g, at_t)

    loads = [
        pltpu.make_async_copy(src, dst, in_sem.at[n])
        for n, (src, dst) in enumerate(
            (
                (core_hbm, core_v),
                (over_hbm, over_v),
                (gamma_hbm, gamma_v),
                (charge_hbm, charge_v),
                (embed_hbm, embed_v),
                (pop_hbm, pop_v),
                (far_hbm, far_v),
                (centre_hbm, near_c.at[1]),
                (centre_hbm, all_c.at[at_g]),
            )
        )
    ]
    for load in loads:
        load.start()

    barrier = pltpu.get_barrier_semaphore()

    def greet(device):
        pl.semaphore_signal(barrier, inc=1, device_id=device, device_id_type=MESH)

    z_steps = sorted(range(1, planes), key=lambda n: -ring(n, planes))
    z_devices = [z_peer(step) for step in z_steps]
    for device in z_devices + plane_devices:
        greet(device)
    greet(frag_peer(1))
    greet(frag_peer(-1))

    back = lax.rem(BASIS - ROWS * at_t, BASIS)
    forth = ROWS * at_t
    lane128 = lanes((ROWS, 128))
    low = lane128 < ROWS
    to_prev = lax.rem(at_t + 3, TILES)
    to_opp = lax.rem(at_t + 2, TILES)
    to_next = lax.rem(at_t + 1, TILES)
    for n, (array, turned) in enumerate(((core_v, core_r), (over_v, over_r))):
        loads[n].wait()
        for f in range(PER):
            turned[f] = pltpu.roll(array[f], back, axis=1)
        firsts, pairs = [], []
        for e in range(OWN):
            mine = turned[OWN * to_prev + e]
            send1[n, e] = turn(mine[:, :128])
            firsts.append(mine[:, 128:])
            mine = turned[OWN * to_next + e]
            send3[n, e] = jnp.where(low, turn(mine[:, 128:]), turn(mine[:, :128]))
            pairs.append(turned[OWN * to_opp + e][:, :128])
        send1[n, 2] = jnp.where(low, firsts[0], turn(firsts[1]))
        send2[n, 0] = jnp.where(low, pairs[0], turn(pairs[1]))

    pl.semaphore_wait(barrier, (plane_peers - 1) + (planes - 1) + 2)

    sends = []

    def push(src, dst, send_sem, recv_sem, device):
        copy = pltpu.make_async_remote_copy(
            src_ref=src,
            dst_ref=dst,
            send_sem=send_sem,
            recv_sem=recv_sem,
            device_id=device,
            device_id_type=MESH,
        )
        copy.start()
        sends.append(copy)
        return copy

    raw = [
        push(send2, got2, raw_send.at[1], raw_recv.at[1], tile_peer(2)),
        push(send1, got1, raw_send.at[0], raw_recv.at[0], tile_peer(3)),
        push(send3, got3, raw_send.at[2], raw_recv.at[2], tile_peer(1)),
    ]
    near = [
        push(centre_hbm, near_c.at[0], nc_send.at[0], nc_recv.at[0], frag_peer(1)),
        push(centre_hbm, near_c.at[2], nc_send.at[1], nc_recv.at[1], frag_peer(-1)),
    ]

    def spread_centres(step, carry):
        pltpu.make_async_remote_copy(
            src_ref=centre_hbm,
            dst_ref=all_c.at[at_g],
            send_sem=ac_send,
            recv_sem=ac_recv,
            device_id=group_peer(step),
            device_id_type=MESH,
        ).start()
        return carry

    lax.fori_loop(1, groups, spread_centres, 0)

    for n in (2, 3, 4):
        loads[n].wait()
    wide = (PER, PER * ROWS)
    prod = dot_nt(charge_v[...], gamma_v[...].reshape(PER * ROWS, BASIS))
    emb = pltpu.roll(embed_v[...], back, axis=1)[:, :128]
    emb = jnp.where(lanes((PER, 128)) < ROWS, emb, turn(emb))
    prod = prod + jnp.concatenate([emb] * 4, axis=1)
    same = lax.broadcasted_iota(jnp.int32, wide, 0) == lanes(wide) // ROWS
    fields = jnp.sum(jnp.where(same, prod, 0.0), axis=0, keepdims=True)
    for t in range(TILES):
        field_s[t] = fields[:, 128 * t : 128 * t + 128]
    fld = []
    for r in (2, 1, 3):
        dest = lax.rem(at_t + TILES - r, TILES)
        fld.append(
            push(field_s.at[dest], field_g.at[r], fld_send.at[r - 1], fld_recv.at[r - 1], (at_f, dest))
        )

    loads[7].wait()
    own = near_c[1].reshape(3 * PER, BASIS)
    cols = jnp.transpose(jnp.concatenate([own, jnp.zeros((128 - 3 * PER, BASIS), f32)], axis=0))
    for f in range(PER):
        for d in range(3):
            n = d * PER + f
            col_b[f, d] = jnp.broadcast_to(cols[:, n : n + 1], (BASIS, 128))
    for copy in near:
        copy.wait_recv()
    near_first = at_f * PER - PER

    def pair(n, carry):
        f = n // LIST
        other = jnp.clip(near_sm[f, lax.rem(n, LIST)] - near_first, 0, 3 * PER - 1)
        slot = other // PER
        row = other - slot * PER
        src = [near_c[slot, d, pl.ds(row, 1), :] for d in range(3)]
        for r in range(4):
            rows = slice(64 * r, 64 * r + 64)
            for h in range(2):
                cut = slice(128 * h, 128 * h + 128)
                dist = 1.0
                for d in range(3):
                    diff = col_b[f, d, rows, :] - src[d][:, cut]
                    dist = dist + diff * diff
                kern_n[n, rows, cut] = lax.rsqrt(dist)
        return carry

    lax.fori_loop(0, FIRST_PAIRS, pair, 0)

    loads[8].wait()
    pltpu.make_async_copy(
        all_c.at[pl.ds(0, groups - 1)], all_c.at[pl.ds(0, groups - 1)], ac_recv
    ).wait()
    runs = lax.broadcasted_iota(jnp.int32, (PC, BASIS), 0) == lanes((PC, BASIS)) // (BASIS // PC)
    mean_run = (runs.astype(f32) * (PC / BASIS)).astype(bf16)
    sum_run = runs.astype(f32).astype(bf16)
    pad = jnp.zeros((PC, 128 - plane_frags), f32)
    for d in range(3):
        places = pick_nt(mean_run, all_c[:, d].reshape(plane_frags, BASIS))
        place_t[at_z, d] = jnp.concatenate([places, pad], axis=1)

    def spread_places(step, carry):
        pltpu.make_async_remote_copy(
            src_ref=place_t.at[at_z],
            dst_ref=place_t.at[at_z],
            send_sem=pl_send,
            recv_sem=pl_recv,
            device_id=z_peer(step),
            device_id_type=MESH,
        ).start()
        return carry

    lax.fori_loop(1, planes, spread_places, 0)

    fld_rows = [field_s[at_t]]
    for copy in fld:
        copy.wait_recv()
    for r in (1, 2, 3):
        fld_rows.append(field_g[r])
    for copy in raw:
        copy.wait_recv()
    full_lanes = lanes((1, BASIS))
    low1 = lanes((1, 128)) < ROWS
    zero = jnp.zeros((ROWS, 128), f32)

    def halves(n, turned, e):
        top = turned[OWN * at_t + e]
        top = jnp.where(lanes((ROWS, BASIS)) < ROWS, 0.5 * top, top)
        one = got1[n, e]
        tail = got1[n, 2]
        tail = turn(tail) if e == 0 else tail
        opp = got2[n, 0]
        opp = opp if e == 0 else turn(opp)
        last = got3[n, e]
        return jnp.concatenate(
            [
                top,
                jnp.concatenate([jnp.where(low, 0.0, 0.5 * one), jnp.where(low, one, tail)], axis=1),
                jnp.concatenate([zero, jnp.where(low, 0.5 * opp, 0.0)], axis=1),
                jnp.concatenate([zero, jnp.where(low, last, 0.5 * last)], axis=1),
            ],
            axis=0,
        )

    square = (BASIS, BASIS)
    row_at = lax.broadcasted_iota(jnp.int32, square, 0)
    col_at = lanes(square)
    eye = (row_at == col_at).astype(f32)
    for e in range(OWN):
        half = halves(1, over_r, e)
        over = half + jnp.transpose(half)
        over_f[e] = over
        if e == 0:
            field = [jnp.where(low1, fld_rows[0], turn(fld_rows[1])), jnp.where(low1, fld_rows[2], turn(fld_rows[3]))]
        else:
            field = [jnp.where(low1, turn(fld_rows[0]), fld_rows[1]), jnp.where(low1, turn(fld_rows[2]), fld_rows[3])]
        field = jnp.concatenate(field, axis=1)
        half = halves(0, core_r, e) + 0.5 * over * field
        fock = half + jnp.transpose(half)
        size = size_sm[OWN * at_t + e]
        row_in = lax.rem(row_at + ROWS * at_t, BASIS) < size
        col_in = lax.rem(col_at + ROWS * at_t, BASIS) < size
        fock = jnp.where(row_in & col_in, fock, 0.0)
        total = jnp.sum(jnp.sum(fock * fock, axis=0, keepdims=True), axis=1, keepdims=True)
        fock = fock / jnp.sqrt(total + 1e-06)
        est[e] = fock + jnp.where(row_in, 0.0, eye)

    def sweep(step, carry):
        parts = [split(est[e]) for e in range(OWN)]
        squares = [split(dot3(parts[e], parts[e])) for e in range(OWN)]
        for e in range(OWN):
            est[e] = 1.5 * est[e] - 0.5 * dot3(squares[e], parts[e])
        return carry

    lax.fori_loop(0, ITERS, sweep, 0)

    loads[5].wait()
    first = PER + at_g * PER + OWN * at_t
    for e in range(OWN):
        dens = 0.5 * (eye - est[e])
        charge = jnp.sum(dens * over_f[e], axis=0, keepdims=True)
        charge = pltpu.roll(jnp.broadcast_to(charge, (8, BASIS)), forth, axis=1)[0:1]
        charge = charge - pop_v[pl.ds(OWN * at_t + e, 1), :]
        table[first + e] = charge

    for device in plane_devices:
        pltpu.make_async_remote_copy(
            src_ref=table.at[pl.ds(first, OWN)],
            dst_ref=table.at[pl.ds(first, OWN)],
            send_sem=tb_send,
            recv_sem=tb_recv,
            device_id=device,
            device_id_type=MESH,
        ).start()

    for e in range(OWN):
        dens = pltpu.roll(0.5 * (eye - est[e]), forth, axis=1)
        for r in range(TILES):
            dens_s[r, e] = dens[ROWS * r : ROWS * r + ROWS]
    slot = density_out.at[pl.ds(OWN * at_t, OWN)]
    den = [push(dens_s.at[r], slot, dn_send.at[r - 1], dn_recv.at[r - 1], tile_peer(r)) for r in (2, 1, 3)]
    keep = pltpu.make_async_copy(dens_s.at[0], slot, out_sem.at[0])
    keep.start()

    loads[6].wait()
    far_list = far_v[...].astype(f32)
    diag = lax.broadcasted_iota(jnp.int32, (LIST, LIST), 0) == lanes((LIST, LIST))
    far_at = [
        jnp.sum(jnp.where(diag, jnp.broadcast_to(far_list[f : f + 1], (LIST, LIST)), 0.0), axis=1, keepdims=True)
        for f in range(PER)
    ]
    far_at = jnp.broadcast_to(jnp.concatenate(far_at, axis=0), (PER * LIST, 128))
    lane64 = lanes((PER * LIST, 128))
    picks = []
    for z in range(planes):
        entry = jnp.where(lane64 < plane_frags, lane64 + z * plane_frags, -1).astype(f32)
        picks.append((far_at == entry).astype(f32))
    pick = jnp.concatenate(picks, axis=1).astype(bf16)
    pltpu.make_async_copy(
        place_t.at[pl.ds(0, planes - 1)], place_t.at[pl.ds(0, planes - 1)], pl_recv
    ).wait()
    far_place = pick_nt(
        pick, jnp.concatenate([place_t[z].reshape(3 * PC, 128) for z in range(planes)], axis=1)
    )
    spots = [
        jnp.concatenate([jnp.broadcast_to(near_c[1, d, f : f + 1, :], (LIST, BASIS)) for f in range(PER)], axis=0)
        for d in range(3)
    ]
    for p in range(PC):
        dist = 1.0
        for d in range(3):
            diff = spots[d] - far_place[:, d * PC + p : d * PC + p + 1]
            dist = dist + diff * diff
        kern_f[p] = lax.rsqrt(dist)

    lax.fori_loop(FIRST_PAIRS, NEXT_PAIRS, pair, 0)

    pltpu.make_async_copy(
        table.at[pl.ds(PER, plane_frags - OWN)], table.at[pl.ds(PER, plane_frags - OWN)], tb_recv
    ).wait()
    plane_charge = table[pl.ds(PER, plane_frags)].reshape(plane_frags, BASIS)
    block_t[at_z] = jnp.concatenate([pick_nt(sum_run, plane_charge), pad], axis=1)

    for device in z_devices:
        pltpu.make_async_remote_copy(
            src_ref=block_t.at[at_z],
            dst_ref=block_t.at[at_z],
            send_sem=bk_send,
            recv_sem=bk_recv,
            device_id=device,
            device_id_type=MESH,
        ).start()

    edge = [
        push(table.at[pl.ds(plane_frags, PER)], table.at[pl.ds(0, PER)], bd_send.at[0], bd_recv.at[0], z_peer(1)),
        push(table.at[pl.ds(PER, PER)], table.at[pl.ds(plane_frags + PER, PER)], bd_send.at[1], bd_recv.at[1], z_peer(-1)),
    ]

    lax.fori_loop(NEXT_PAIRS, PER * LIST, pair, 0)

    for copy in edge:
        copy.wait_recv()
    table_first = at_z * plane_frags - PER
    lane256 = lanes((BASIS, 128))
    near_cols = jnp.zeros((BASIS, 128), f32)

    def near_sum(f):
        acc = jnp.zeros((BASIS, 128), f32)
        for k in range(LIST):
            row = table[jnp.clip(near_sm[f, k] - table_first, 0, plane_frags + 2 * PER - 1)]
            acc = acc + kern_n[f * LIST + k, :, :128] * row[:, :128]
            acc = acc + kern_n[f * LIST + k, :, 128:] * row[:, 128:]
        return jnp.sum(acc, axis=1, keepdims=True)

    def near_step(f, cols):
        return jnp.where(lane256 == f, near_sum(f), cols)

    near_cols = lax.fori_loop(0, PER, near_step, near_cols)
    near_rows = jnp.transpose(near_cols)[:PER]

    pltpu.make_async_copy(
        block_t.at[pl.ds(0, planes - 1)], block_t.at[pl.ds(0, planes - 1)], bk_recv
    ).wait()
    far_charge = pick_nt(pick, jnp.concatenate([block_t[z] for z in range(planes)], axis=1))
    far_sum = jnp.zeros((PER * LIST, BASIS), f32)
    for p in range(PC):
        far_sum = far_sum + far_charge[:, p : p + 1] * kern_f[p]
    far_rows = jnp.sum(far_sum.reshape(PER, LIST, BASIS), axis=1)
    potential = 0.25 * (near_rows + far_rows)
    col_s[...] = jnp.transpose(jnp.concatenate([potential, jnp.zeros((128 - PER, BASIS), f32)], axis=0))
    mine = col_s[pl.ds(ROWS * at_t, ROWS), :]
    for f in range(PER):
        esp_out[f] = 0.5 * over_v[f] * (mine[:, f : f + 1] + potential[f : f + 1, :])

    for copy in den:
        copy.wait_recv()
    keep.wait()
    for copy in sends:
        copy.wait_send()
    for ref, count, sem in (
        (all_c, groups - 1, ac_send),
        (place_t, planes - 1, pl_send),
        (table, plane_frags - OWN, tb_send),
        (block_t, planes - 1, bk_send),
    ):
        pltpu.make_async_copy(ref.at[pl.ds(0, count)], ref.at[pl.ds(0, count)], sem).wait()


def per_device(
    planes,
    groups,
    core_fock,
    intersection,
    gamma_tile,
    charge_old,
    embed_old,
    core_pop,
    centres,
    frag_sizes,
    near_list,
    far_list,
):
    dma = pltpu.SemaphoreType.DMA
    smem = pl.BlockSpec(memory_space=pltpu.SMEM)
    hbm = pl.BlockSpec(memory_space=pltpu.HBM)
    vmem = pl.BlockSpec(memory_space=pltpu.VMEM)
    own = (PER, ROWS, BASIS)
    pieces = (ROWS, 128)
    plane_frags = groups * PER
    return pl.pallas_call(
        functools.partial(kernel, planes, groups),
        out_shape=(pltpu.VMEM(own, f32), pltpu.VMEM(own, f32)),
        in_specs=[hbm] * 7 + [smem, smem, hbm],
        out_specs=(vmem, vmem),
        scratch_shapes=[
            pltpu.VMEM(own, f32),
            pltpu.VMEM(own, f32),
            pltpu.VMEM(own, f32),
            pltpu.VMEM((PER, BASIS), f32),
            pltpu.VMEM((PER, BASIS), f32),
            pltpu.VMEM((PER, BASIS), f32),
            pltpu.VMEM((PER, LIST), jnp.int32),
            pltpu.VMEM(own, f32),
            pltpu.VMEM(own, f32),
            pltpu.VMEM((2, 3) + pieces, f32),
            pltpu.VMEM((2, 1) + pieces, f32),
            pltpu.VMEM((2, 2) + pieces, f32),
            pltpu.VMEM((2, 3) + pieces, f32),
            pltpu.VMEM((2, 1) + pieces, f32),
            pltpu.VMEM((2, 2) + pieces, f32),
            pltpu.VMEM((TILES, 1, 128), f32),
            pltpu.VMEM((TILES, 1, 128), f32),
            pltpu.VMEM((3, 3, PER, BASIS), f32),
            pltpu.VMEM((groups, 3, PER, BASIS), f32),
            pltpu.VMEM((planes, 3, PC, 128), f32),
            pltpu.VMEM((PER, 3, BASIS, 128), f32),
            pltpu.VMEM((PER * LIST, BASIS, BASIS), f32),
            pltpu.VMEM((PC, PER * LIST, BASIS), f32),
            pltpu.VMEM((OWN, BASIS, BASIS), f32),
            pltpu.VMEM((OWN, BASIS, BASIS), f32),
            pltpu.VMEM((TILES, OWN, ROWS, BASIS), f32),
            pltpu.VMEM((plane_frags + 2 * PER, 1, BASIS), f32),
            pltpu.VMEM((planes, PC, 128), f32),
            pltpu.VMEM((BASIS, 128), f32),
            dma((9,)),
            dma((3,)),
            dma((3,)),
            dma((3,)),
            dma((3,)),
            dma((2,)),
            dma((2,)),
            dma,
            dma,
            dma,
            dma,
            dma,
            dma,
            dma((2,)),
            dma((2,)),
            dma,
            dma,
            dma((3,)),
            dma((3,)),
            dma((1,)),
        ],
        compiler_params=pltpu.CompilerParams(
            collective_id=0, has_side_effects=True, vmem_limit_bytes=60 * 1024 * 1024
        ),
        name="scc_cycle",
    )(
        core_fock,
        intersection,
        gamma_tile,
        charge_old,
        embed_old,
        core_pop,
        jnp.transpose(centres, (1, 0, 2)),
        frag_sizes,
        near_list,
        far_list,
    )


def solution(mesh):
    groups = mesh.shape["frag"] // PLANES
    return build(mesh, PLANES, groups)


def build(mesh, planes, groups):
    in_specs = (
        P("frag", "tile", None),
        P("frag", "tile", None),
        P("frag", "tile", None),
        P("frag", None),
        P("frag", None),
        P("frag", None),
        P("frag", None, None),
        P("frag"),
        P("frag", None),
        P("frag", None),
    )
    out_specs = (P("frag", "tile", None), P("frag", "tile", None))
    return jax.shard_map(
        functools.partial(per_device, planes, groups),
        mesh=mesh,
        in_specs=in_specs,
        out_specs=out_specs,
        check_vma=False,
    )
```

```python
import functools
import jax
import jax.numpy as jnp
from jax import lax
from jax.experimental import pallas as pl
from jax.experimental.pallas import tpu as pltpu
from jax.sharding import PartitionSpec as P

ITERS = 12
TILES = 4
ROWS = 64
BASIS = 256
PER = 8
OWN = 2
PC = 8
LIST = 8
PLANES = 8
FIRST_PAIRS = 31
NEXT_PAIRS = 52

f32 = jnp.float32
bf16 = jnp.bfloat16
HI = lax.Precision.HIGHEST
MESH = pl.DeviceIdType.MESH


def dot_nt(a, b):
    return lax.dot_general(a, b, (((1,), (1,)), ((), ())), precision=HI, preferred_element_type=f32)


def split(x):
    high = x.astype(bf16)
    return high, (x - high.astype(f32)).astype(bf16)


def dot3(a, b):
    (ah, al), (bh, bl) = a, b
    mul = functools.partial(jnp.dot, preferred_element_type=f32)
    return mul(ah, bh) + mul(ah, bl) + mul(al, bh)


def pick_nt(sel, b):
    high = b.astype(bf16)
    rest = b - high.astype(f32)
    middle = rest.astype(bf16)
    least = (rest - middle.astype(f32)).astype(bf16)
    mul = functools.partial(
        lax.dot_general, dimension_numbers=(((1,), (1,)), ((), ())), preferred_element_type=f32
    )
    return mul(sel, high) + mul(sel, middle) + mul(sel, least)


def lanes(shape):
    return lax.broadcasted_iota(jnp.int32, shape, len(shape) - 1)


def turn(x):
    return pltpu.roll(x, ROWS, axis=1)


def kernel(
    planes,
    groups,
    core_hbm,
    over_hbm,
    gamma_hbm,
    charge_hbm,
    embed_hbm,
    pop_hbm,
    centre_hbm,
    size_sm,
    near_sm,
    far_hbm,
    density_out,
    esp_out,
    core_v,
    over_v,
    gamma_v,
    charge_v,
    embed_v,
    pop_v,
    far_v,
    core_r,
    over_r,
    send1,
    send2,
    send3,
    got1,
    got2,
    got3,
    field_s,
    field_g,
    near_c,
    all_c,
    place_t,
    col_b,
    kern_n,
    kern_f,
    est,
    over_f,
    dens_s,
    table,
    block_t,
    col_s,
    in_sem,
    raw_send,
    raw_recv,
    fld_send,
    fld_recv,
    nc_send,
    nc_recv,
    ac_send,
    ac_recv,
    pl_send,
    pl_recv,
    tb_send,
    tb_recv,
    bd_send,
    bd_recv,
    bk_send,
    bk_recv,
    dn_send,
    dn_recv,
    out_sem,
    ready,
):
    plane_frags = groups * PER
    at_f = lax.axis_index("frag")
    at_t = lax.axis_index("tile")
    at_z = at_f // groups
    at_g = lax.rem(at_f, groups)
    frag_devs = planes * groups

    def tile_peer(step):
        return (at_f, lax.rem(at_t + step, TILES))

    def frag_peer(step):
        return (lax.rem(at_f + frag_devs + step, frag_devs), at_t)

    deep = groups // 2
    ring = lambda n, size: min(n, size - n)
    steps = [(dx, dy, dc) for dx in range(TILES) for dy in range(deep) for dc in range(2)][1:]
    steps.sort(key=lambda s: (-ring(s[0], TILES) - ring(s[1], deep), -s[2]))
    at_c = lax.rem(at_g, 2)
    peer_x = [lax.rem(at_t + dx, TILES) for dx in range(TILES)]
    peer_g = [
        [at_z * groups + 2 * lax.rem(at_g // 2 + dy, deep) + (1 - at_c if dc else at_c) for dc in range(2)]
        for dy in range(deep)
    ]
    plane_devices = [(peer_g[dy][dc], peer_x[dx]) for dx, dy, dc in steps]

    def group_peer(step):
        return (at_z * groups + lax.rem(at_g + step, groups), at_t)

    def z_peer(step):
        return (lax.rem(at_z + planes + step, planes) * groups + at_g, at_t)

    loads = [
        pltpu.make_async_copy(src, dst, in_sem.at[n])
        for n, (src, dst) in enumerate(
            (
                (core_hbm, core_v),
                (over_hbm, over_v),
                (gamma_hbm, gamma_v),
                (charge_hbm, charge_v),
                (embed_hbm, embed_v),
                (pop_hbm, pop_v),
                (far_hbm, far_v),
                (centre_hbm, near_c.at[1]),
                (centre_hbm, all_c.at[at_g]),
            )
        )
    ]
    for load in loads:
        load.start()

    barrier = pltpu.get_barrier_semaphore()

    def signal(sem, device):
        pl.semaphore_signal(sem, inc=1, device_id=device, device_id_type=MESH)

    z_steps = sorted(range(1, planes), key=lambda n: -ring(n, planes))
    z_devices = [z_peer(step) for step in z_steps]
    tile_devices = [tile_peer(step) for step in (2, 1, 3)]
    first_devices = tile_devices + [frag_peer(1), frag_peer(-1), z_peer(1), z_peer(-1)]
    first_devices += [group_peer(step) for step in range(1, groups)]
    for device in first_devices:
        signal(barrier, device)

    back = lax.rem(BASIS - ROWS * at_t, BASIS)
    forth = ROWS * at_t
    lane128 = lanes((ROWS, 128))
    low = lane128 < ROWS
    to_prev = lax.rem(at_t + 3, TILES)
    to_opp = lax.rem(at_t + 2, TILES)
    to_next = lax.rem(at_t + 1, TILES)
    for n, (array, turned) in enumerate(((core_v, core_r), (over_v, over_r))):
        loads[n].wait()
        for f in range(PER):
            turned[f] = pltpu.roll(array[f], back, axis=1)
        firsts, pairs = [], []
        for e in range(OWN):
            mine = turned[OWN * to_prev + e]
            send1[n, e] = turn(mine[:, :128])
            firsts.append(mine[:, 128:])
            mine = turned[OWN * to_next + e]
            send3[n, e] = jnp.where(low, turn(mine[:, 128:]), turn(mine[:, :128]))
            pairs.append(turned[OWN * to_opp + e][:, :128])
        send1[n, 2] = jnp.where(low, firsts[0], turn(firsts[1]))
        send2[n, 0] = jnp.where(low, pairs[0], turn(pairs[1]))

    pl.semaphore_wait(barrier, len(first_devices))

    sends = []

    def push(src, dst, send_sem, recv_sem, device):
        copy = pltpu.make_async_remote_copy(
            src_ref=src,
            dst_ref=dst,
            send_sem=send_sem,
            recv_sem=recv_sem,
            device_id=device,
            device_id_type=MESH,
        )
        copy.start()
        sends.append(copy)
        return copy

    raw = [
        push(send2, got2, raw_send.at[1], raw_recv.at[1], tile_peer(2)),
        push(send1, got1, raw_send.at[0], raw_recv.at[0], tile_peer(3)),
        push(send3, got3, raw_send.at[2], raw_recv.at[2], tile_peer(1)),
    ]
    loads[7].wait()
    near = [
        push(near_c.at[1], near_c.at[0], nc_send.at[0], nc_recv.at[0], frag_peer(1)),
        push(near_c.at[1], near_c.at[2], nc_send.at[1], nc_recv.at[1], frag_peer(-1)),
    ]

    def spread_centres(step, carry):
        pltpu.make_async_remote_copy(
            src_ref=near_c.at[1],
            dst_ref=all_c.at[at_g],
            send_sem=ac_send,
            recv_sem=ac_recv,
            device_id=group_peer(step),
            device_id_type=MESH,
        ).start()
        return carry

    lax.fori_loop(1, groups, spread_centres, 0)
    for device in tile_devices:
        signal(ready.at[0], device)
    for step in (1, -1):
        signal(ready.at[1], z_peer(step))

    for n in (2, 3, 4):
        loads[n].wait()
    wide = (PER, PER * ROWS)
    prod = dot_nt(charge_v[...], gamma_v[...].reshape(PER * ROWS, BASIS))
    emb = pltpu.roll(embed_v[...], back, axis=1)[:, :128]
    emb = jnp.where(lanes((PER, 128)) < ROWS, emb, turn(emb))
    prod = prod + jnp.concatenate([emb] * 4, axis=1)
    same = lax.broadcasted_iota(jnp.int32, wide, 0) == lanes(wide) // ROWS
    fields = jnp.sum(jnp.where(same, prod, 0.0), axis=0, keepdims=True)
    for t in range(TILES):
        field_s[t] = fields[:, 128 * t : 128 * t + 128]
    fld = []
    for r in (2, 1, 3):
        dest = lax.rem(at_t + TILES - r, TILES)
        fld.append(
            push(field_s.at[dest], field_g.at[r], fld_send.at[r - 1], fld_recv.at[r - 1], (at_f, dest))
        )

    own = near_c[1].reshape(3 * PER, BASIS)
    cols = jnp.transpose(jnp.concatenate([own, jnp.zeros((128 - 3 * PER, BASIS), f32)], axis=0))
    for f in range(PER):
        for d in range(3):
            n = d * PER + f
            col_b[f, d] = jnp.broadcast_to(cols[:, n : n + 1], (BASIS, 128))
    for copy in near:
        copy.wait_recv()
    pl.semaphore_wait(ready.at[1], 2)
    for step in (2, -2):
        signal(ready.at[2], z_peer(step))

    near_first = at_f * PER - PER

    def pair(n, carry):
        f = n // LIST
        other = jnp.clip(near_sm[f, lax.rem(n, LIST)] - near_first, 0, 3 * PER - 1)
        slot = other // PER
        row = other - slot * PER
        src = [near_c[slot, d, pl.ds(row, 1), :] for d in range(3)]
        for r in range(4):
            rows = slice(64 * r, 64 * r + 64)
            for h in range(2):
                cut = slice(128 * h, 128 * h + 128)
                dist = 1.0
                for d in range(3):
                    diff = col_b[f, d, rows, :] - src[d][:, cut]
                    dist = dist + diff * diff
                kern_n[n, rows, cut] = lax.rsqrt(dist)
        return carry

    lax.fori_loop(0, FIRST_PAIRS, pair, 0)

    loads[8].wait()
    pltpu.make_async_copy(
        all_c.at[pl.ds(0, groups - 1)], all_c.at[pl.ds(0, groups - 1)], ac_recv
    ).wait()
    runs = lax.broadcasted_iota(jnp.int32, (PC, BASIS), 0) == lanes((PC, BASIS)) // (BASIS // PC)
    mean_run = (runs.astype(f32) * (PC / BASIS)).astype(bf16)
    sum_run = runs.astype(f32).astype(bf16)
    pad = jnp.zeros((PC, 128 - plane_frags), f32)
    for d in range(3):
        places = pick_nt(mean_run, all_c[:, d].reshape(plane_frags, BASIS))
        place_t[at_z, d] = jnp.concatenate([places, pad], axis=1)

    fld_rows = [field_s[at_t]]
    for copy in fld:
        copy.wait_recv()
    for r in (1, 2, 3):
        fld_rows.append(field_g[r])
    for copy in raw:
        copy.wait_recv()
    full_lanes = lanes((1, BASIS))
    low1 = lanes((1, 128)) < ROWS
    zero = jnp.zeros((ROWS, 128), f32)

    def halves(n, turned, e):
        top = turned[OWN * at_t + e]
        top = jnp.where(lanes((ROWS, BASIS)) < ROWS, 0.5 * top, top)
        one = got1[n, e]
        tail = got1[n, 2]
        tail = turn(tail) if e == 0 else tail
        opp = got2[n, 0]
        opp = opp if e == 0 else turn(opp)
        last = got3[n, e]
        return jnp.concatenate(
            [
                top,
                jnp.concatenate([jnp.where(low, 0.0, 0.5 * one), jnp.where(low, one, tail)], axis=1),
                jnp.concatenate([zero, jnp.where(low, 0.5 * opp, 0.0)], axis=1),
                jnp.concatenate([zero, jnp.where(low, last, 0.5 * last)], axis=1),
            ],
            axis=0,
        )

    square = (BASIS, BASIS)
    row_at = lax.broadcasted_iota(jnp.int32, square, 0)
    col_at = lanes(square)
    eye = (row_at == col_at).astype(f32)
    for e in range(OWN):
        half = halves(1, over_r, e)
        over = half + jnp.transpose(half)
        over_f[e] = over
        if e == 0:
            field = [jnp.where(low1, fld_rows[0], turn(fld_rows[1])), jnp.where(low1, fld_rows[2], turn(fld_rows[3]))]
        else:
            field = [jnp.where(low1, turn(fld_rows[0]), fld_rows[1]), jnp.where(low1, turn(fld_rows[2]), fld_rows[3])]
        field = jnp.concatenate(field, axis=1)
        half = halves(0, core_r, e) + 0.5 * over * field
        fock = half + jnp.transpose(half)
        size = size_sm[OWN * at_t + e]
        row_in = lax.rem(row_at + ROWS * at_t, BASIS) < size
        col_in = lax.rem(col_at + ROWS * at_t, BASIS) < size
        fock = jnp.where(row_in & col_in, fock, 0.0)
        total = jnp.sum(jnp.sum(fock * fock, axis=0, keepdims=True), axis=1, keepdims=True)
        fock = fock / jnp.sqrt(total + 1e-06)
        est[e] = fock + jnp.where(row_in, 0.0, eye)

    def sweep(step, carry):
        parts = [split(est[e]) for e in range(OWN)]
        squares = [split(dot3(parts[e], parts[e])) for e in range(OWN)]
        for e in range(OWN):
            est[e] = 1.5 * est[e] - 0.5 * dot3(squares[e], parts[e])
        return carry

    pl.semaphore_wait(ready.at[2], 2)

    def spread_places(step, carry):
        pltpu.make_async_remote_copy(
            src_ref=place_t.at[at_z],
            dst_ref=place_t.at[at_z],
            send_sem=pl_send,
            recv_sem=pl_recv,
            device_id=z_peer(step),
            device_id_type=MESH,
        ).start()
        return carry

    lax.fori_loop(1, planes, spread_places, 0)

    lax.fori_loop(0, ITERS, sweep, 0)

    loads[5].wait()
    first = PER + at_g * PER + OWN * at_t
    for e in range(OWN):
        dens = 0.5 * (eye - est[e])
        charge = jnp.sum(dens * over_f[e], axis=0, keepdims=True)
        charge = pltpu.roll(jnp.broadcast_to(charge, (8, BASIS)), forth, axis=1)[0:1]
        charge = charge - pop_v[pl.ds(OWN * at_t + e, 1), :]
        table[first + e] = charge

    pl.semaphore_wait(ready.at[0], len(tile_devices))
    for device in plane_devices:
        pltpu.make_async_remote_copy(
            src_ref=table.at[pl.ds(first, OWN)],
            dst_ref=table.at[pl.ds(first, OWN)],
            send_sem=tb_send,
            recv_sem=tb_recv,
            device_id=device,
            device_id_type=MESH,
        ).start()

    for e in range(OWN):
        dens = pltpu.roll(0.5 * (eye - est[e]), forth, axis=1)
        for r in range(TILES):
            dens_s[r, e] = dens[ROWS * r : ROWS * r + ROWS]
    slot = density_out.at[pl.ds(OWN * at_t, OWN)]
    den = [push(dens_s.at[r], slot, dn_send.at[r - 1], dn_recv.at[r - 1], tile_peer(r)) for r in (2, 1, 3)]
    keep = pltpu.make_async_copy(dens_s.at[0], slot, out_sem.at[0])
    keep.start()

    loads[6].wait()
    far_list = far_v[...].astype(f32)
    diag = lax.broadcasted_iota(jnp.int32, (LIST, LIST), 0) == lanes((LIST, LIST))
    far_at = [
        jnp.sum(jnp.where(diag, jnp.broadcast_to(far_list[f : f + 1], (LIST, LIST)), 0.0), axis=1, keepdims=True)
        for f in range(PER)
    ]
    far_at = jnp.broadcast_to(jnp.concatenate(far_at, axis=0), (PER * LIST, 128))
    lane64 = lanes((PER * LIST, 128))
    picks = []
    for z in range(planes):
        entry = jnp.where(lane64 < plane_frags, lane64 + z * plane_frags, -1).astype(f32)
        picks.append((far_at == entry).astype(f32))
    pick = jnp.concatenate(picks, axis=1).astype(bf16)
    pltpu.make_async_copy(
        place_t.at[pl.ds(0, planes - 1)], place_t.at[pl.ds(0, planes - 1)], pl_recv
    ).wait()
    far_place = pick_nt(
        pick, jnp.concatenate([place_t[z].reshape(3 * PC, 128) for z in range(planes)], axis=1)
    )
    spots = [
        jnp.concatenate([jnp.broadcast_to(near_c[1, d, f : f + 1, :], (LIST, BASIS)) for f in range(PER)], axis=0)
        for d in range(3)
    ]
    for p in range(PC):
        dist = 1.0
        for d in range(3):
            diff = spots[d] - far_place[:, d * PC + p : d * PC + p + 1]
            dist = dist + diff * diff
        kern_f[p] = lax.rsqrt(dist)

    lax.fori_loop(FIRST_PAIRS, NEXT_PAIRS, pair, 0)

    pltpu.make_async_copy(
        table.at[pl.ds(PER, plane_frags - OWN)], table.at[pl.ds(PER, plane_frags - OWN)], tb_recv
    ).wait()
    plane_charge = table[pl.ds(PER, plane_frags)].reshape(plane_frags, BASIS)
    block_t[at_z] = jnp.concatenate([pick_nt(sum_run, plane_charge), pad], axis=1)

    for device in z_devices:
        pltpu.make_async_remote_copy(
            src_ref=block_t.at[at_z],
            dst_ref=block_t.at[at_z],
            send_sem=bk_send,
            recv_sem=bk_recv,
            device_id=device,
            device_id_type=MESH,
        ).start()

    edge = [
        push(table.at[pl.ds(plane_frags, PER)], table.at[pl.ds(0, PER)], bd_send.at[0], bd_recv.at[0], z_peer(1)),
        push(table.at[pl.ds(PER, PER)], table.at[pl.ds(plane_frags + PER, PER)], bd_send.at[1], bd_recv.at[1], z_peer(-1)),
    ]

    lax.fori_loop(NEXT_PAIRS, PER * LIST, pair, 0)

    for copy in edge:
        copy.wait_recv()
    table_first = at_z * plane_frags - PER
    lane256 = lanes((BASIS, 128))
    near_cols = jnp.zeros((BASIS, 128), f32)

    def near_sum(f):
        acc = jnp.zeros((BASIS, 128), f32)
        for k in range(LIST):
            row = table[jnp.clip(near_sm[f, k] - table_first, 0, plane_frags + 2 * PER - 1)]
            acc = acc + kern_n[f * LIST + k, :, :128] * row[:, :128]
            acc = acc + kern_n[f * LIST + k, :, 128:] * row[:, 128:]
        return jnp.sum(acc, axis=1, keepdims=True)

    def near_step(f, cols):
        return jnp.where(lane256 == f, near_sum(f), cols)

    near_cols = lax.fori_loop(0, PER, near_step, near_cols)
    near_rows = jnp.transpose(near_cols)[:PER]

    pltpu.make_async_copy(
        block_t.at[pl.ds(0, planes - 1)], block_t.at[pl.ds(0, planes - 1)], bk_recv
    ).wait()
    far_charge = pick_nt(pick, jnp.concatenate([block_t[z] for z in range(planes)], axis=1))
    far_sum = jnp.zeros((PER * LIST, BASIS), f32)
    for p in range(PC):
        far_sum = far_sum + far_charge[:, p : p + 1] * kern_f[p]
    far_rows = jnp.sum(far_sum.reshape(PER, LIST, BASIS), axis=1)
    potential = 0.25 * (near_rows + far_rows)
    col_s[...] = jnp.transpose(jnp.concatenate([potential, jnp.zeros((128 - PER, BASIS), f32)], axis=0))
    mine = col_s[pl.ds(ROWS * at_t, ROWS), :]
    for f in range(PER):
        esp_out[f] = 0.5 * over_v[f] * (mine[:, f : f + 1] + potential[f : f + 1, :])

    for copy in den:
        copy.wait_recv()
    keep.wait()
    for copy in sends:
        copy.wait_send()
    for ref, count, sem in (
        (all_c, groups - 1, ac_send),
        (place_t, planes - 1, pl_send),
        (table, plane_frags - OWN, tb_send),
        (block_t, planes - 1, bk_send),
    ):
        pltpu.make_async_copy(ref.at[pl.ds(0, count)], ref.at[pl.ds(0, count)], sem).wait()


def store(density, esp, density_out, esp_out, sem):
    copies = [
        pltpu.make_async_copy(src, dst, sem.at[n])
        for n, (src, dst) in enumerate(((density, density_out), (esp, esp_out)))
    ]
    for copy in copies:
        copy.start()
    for copy in copies:
        copy.wait()


def per_device(
    planes,
    groups,
    core_fock,
    intersection,
    gamma_tile,
    charge_old,
    embed_old,
    core_pop,
    centres,
    frag_sizes,
    near_list,
    far_list,
):
    dma = pltpu.SemaphoreType.DMA
    smem = pl.BlockSpec(memory_space=pltpu.SMEM)
    hbm = pl.BlockSpec(memory_space=pltpu.HBM)
    vmem = pl.BlockSpec(memory_space=pltpu.VMEM)
    own = (PER, ROWS, BASIS)
    pieces = (ROWS, 128)
    plane_frags = groups * PER
    held = pl.pallas_call(
        functools.partial(kernel, planes, groups),
        out_shape=(pltpu.VMEM(own, f32), pltpu.VMEM(own, f32)),
        in_specs=[hbm] * 7 + [smem, smem, hbm],
        out_specs=(vmem, vmem),
        scratch_shapes=[
            pltpu.VMEM(own, f32),
            pltpu.VMEM(own, f32),
            pltpu.VMEM(own, f32),
            pltpu.VMEM((PER, BASIS), f32),
            pltpu.VMEM((PER, BASIS), f32),
            pltpu.VMEM((PER, BASIS), f32),
            pltpu.VMEM((PER, LIST), jnp.int32),
            pltpu.VMEM(own, f32),
            pltpu.VMEM(own, f32),
            pltpu.VMEM((2, 3) + pieces, f32),
            pltpu.VMEM((2, 1) + pieces, f32),
            pltpu.VMEM((2, 2) + pieces, f32),
            pltpu.VMEM((2, 3) + pieces, f32),
            pltpu.VMEM((2, 1) + pieces, f32),
            pltpu.VMEM((2, 2) + pieces, f32),
            pltpu.VMEM((TILES, 1, 128), f32),
            pltpu.VMEM((TILES, 1, 128), f32),
            pltpu.VMEM((3, 3, PER, BASIS), f32),
            pltpu.VMEM((groups, 3, PER, BASIS), f32),
            pltpu.VMEM((planes, 3, PC, 128), f32),
            pltpu.VMEM((PER, 3, BASIS, 128), f32),
            pltpu.VMEM((PER * LIST, BASIS, BASIS), f32),
            pltpu.VMEM((PC, PER * LIST, BASIS), f32),
            pltpu.VMEM((OWN, BASIS, BASIS), f32),
            pltpu.VMEM((OWN, BASIS, BASIS), f32),
            pltpu.VMEM((TILES, OWN, ROWS, BASIS), f32),
            pltpu.VMEM((plane_frags + 2 * PER, 1, BASIS), f32),
            pltpu.VMEM((planes, PC, 128), f32),
            pltpu.VMEM((BASIS, 128), f32),
            dma((9,)),
            dma((3,)),
            dma((3,)),
            dma((3,)),
            dma((3,)),
            dma((2,)),
            dma((2,)),
            dma,
            dma,
            dma,
            dma,
            dma,
            dma,
            dma((2,)),
            dma((2,)),
            dma,
            dma,
            dma((3,)),
            dma((3,)),
            dma((1,)),
            pltpu.SemaphoreType.REGULAR((3,)),
        ],
        compiler_params=pltpu.CompilerParams(
            collective_id=0, has_side_effects=True, vmem_limit_bytes=60 * 1024 * 1024
        ),
        name="scc_cycle",
    )(
        core_fock,
        intersection,
        gamma_tile,
        charge_old,
        embed_old,
        core_pop,
        jnp.transpose(centres, (1, 0, 2)),
        frag_sizes,
        near_list,
        far_list,
    )
    return pl.pallas_call(
        store,
        out_shape=(jax.ShapeDtypeStruct(own, f32), jax.ShapeDtypeStruct(own, f32)),
        in_specs=[vmem, vmem],
        out_specs=(pl.BlockSpec(memory_space=pl.ANY), pl.BlockSpec(memory_space=pl.ANY)),
        scratch_shapes=[dma((2,))],
        compiler_params=pltpu.CompilerParams(vmem_limit_bytes=1024 * 1024),
        name="store",
    )(*held)


def solution(mesh):
    groups = mesh.shape["frag"] // PLANES
    return build(mesh, PLANES, groups)


def build(mesh, planes, groups):
    in_specs = (
        P("frag", "tile", None),
        P("frag", "tile", None),
        P("frag", "tile", None),
        P("frag", None),
        P("frag", None),
        P("frag", None),
        P("frag", None, None),
        P("frag"),
        P("frag", None),
        P("frag", None),
    )
    out_specs = (P("frag", "tile", None), P("frag", "tile", None))
    return jax.shard_map(
        functools.partial(per_device, planes, groups),
        mesh=mesh,
        in_specs=in_specs,
        out_specs=out_specs,
        check_vma=False,
    )
```

```python
import functools
import jax
import jax.numpy as jnp
from jax import lax
from jax.experimental import pallas as pl
from jax.experimental.pallas import tpu as pltpu
from jax.sharding import PartitionSpec as P

ITERS = 12
TILES = 4
ROWS = 64
BASIS = 256
PER = 8
OWN = 2
PC = 8
LIST = 8
PLANES = 8
FIRST_PAIRS = 31
NEXT_PAIRS = 52

f32 = jnp.float32
bf16 = jnp.bfloat16
HI = lax.Precision.HIGHEST
MESH = pl.DeviceIdType.MESH


def dot_nt(a, b):
    return lax.dot_general(a, b, (((1,), (1,)), ((), ())), precision=HI, preferred_element_type=f32)


def split(x):
    high = x.astype(bf16)
    return high, (x - high.astype(f32)).astype(bf16)


def dot3(a, b):
    (ah, al), (bh, bl) = a, b
    mul = functools.partial(jnp.dot, preferred_element_type=f32)
    return mul(ah, bh) + mul(ah, bl) + mul(al, bh)


def pick_nt(sel, b):
    high = b.astype(bf16)
    rest = b - high.astype(f32)
    middle = rest.astype(bf16)
    least = (rest - middle.astype(f32)).astype(bf16)
    mul = functools.partial(
        lax.dot_general, dimension_numbers=(((1,), (1,)), ((), ())), preferred_element_type=f32
    )
    return mul(sel, high) + mul(sel, middle) + mul(sel, least)


def lanes(shape):
    return lax.broadcasted_iota(jnp.int32, shape, len(shape) - 1)


def turn(x):
    return pltpu.roll(x, ROWS, axis=1)


def kernel(
    planes,
    groups,
    core_hbm,
    over_hbm,
    gamma_hbm,
    charge_hbm,
    embed_hbm,
    pop_hbm,
    centre_hbm,
    size_sm,
    near_sm,
    far_hbm,
    density_out,
    esp_out,
    core_v,
    over_v,
    gamma_v,
    charge_v,
    embed_v,
    pop_v,
    far_v,
    core_r,
    over_r,
    send1,
    send2,
    send3,
    got1,
    got2,
    got3,
    field_s,
    field_g,
    near_c,
    all_c,
    place_t,
    col_b,
    kern_n,
    kern_f,
    est,
    over_f,
    dens_s,
    table,
    block_t,
    col_s,
    in_sem,
    raw_send,
    raw_recv,
    fld_send,
    fld_recv,
    nc_send,
    nc_recv,
    ac_send,
    ac_recv,
    pl_send,
    pl_recv,
    tb_send,
    tb_recv,
    bd_send,
    bd_recv,
    bk_send,
    bk_recv,
    dn_send,
    dn_recv,
    out_sem,
    ready,
):
    plane_frags = groups * PER
    at_f = lax.axis_index("frag")
    at_t = lax.axis_index("tile")
    at_z = at_f // groups
    at_g = lax.rem(at_f, groups)
    frag_devs = planes * groups

    def tile_peer(step):
        return (at_f, lax.rem(at_t + step, TILES))

    def frag_peer(step):
        return (lax.rem(at_f + frag_devs + step, frag_devs), at_t)

    deep = groups // 2
    ring = lambda n, size: min(n, size - n)
    steps = [(dx, dy, dc) for dx in range(TILES) for dy in range(deep) for dc in range(2)][1:]
    steps.sort(key=lambda s: (-ring(s[0], TILES) - ring(s[1], deep), -s[2]))
    at_c = lax.rem(at_g, 2)
    peer_x = [lax.rem(at_t + dx, TILES) for dx in range(TILES)]
    peer_g = [
        [at_z * groups + 2 * lax.rem(at_g // 2 + dy, deep) + (1 - at_c if dc else at_c) for dc in range(2)]
        for dy in range(deep)
    ]
    plane_devices = [(peer_g[dy][dc], peer_x[dx]) for dx, dy, dc in steps]

    def group_peer(step):
        return (at_z * groups + lax.rem(at_g + step, groups), at_t)

    def z_peer(step):
        return (lax.rem(at_z + planes + step, planes) * groups + at_g, at_t)

    loads = [
        pltpu.make_async_copy(src, dst, in_sem.at[n])
        for n, (src, dst) in enumerate(
            (
                (core_hbm, core_v),
                (over_hbm, over_v),
                (gamma_hbm, gamma_v),
                (charge_hbm, charge_v),
                (embed_hbm, embed_v),
                (pop_hbm, pop_v),
                (far_hbm, far_v),
                (centre_hbm, near_c.at[1]),
                (centre_hbm, all_c.at[at_g]),
            )
        )
    ]
    for load in loads:
        load.start()

    barrier = pltpu.get_barrier_semaphore()

    def signal(sem, device):
        pl.semaphore_signal(sem, inc=1, device_id=device, device_id_type=MESH)

    z_steps = sorted(range(1, planes), key=lambda n: -ring(n, planes))
    z_devices = [z_peer(step) for step in z_steps]
    tile_devices = [tile_peer(step) for step in (2, 1, 3)]
    first_devices = tile_devices + [frag_peer(1), frag_peer(-1), z_peer(1), z_peer(-1)]
    first_devices += [group_peer(step) for step in range(1, groups)]
    for device in first_devices:
        signal(barrier, device)

    back = lax.rem(BASIS - ROWS * at_t, BASIS)
    forth = ROWS * at_t
    lane128 = lanes((ROWS, 128))
    low = lane128 < ROWS
    to_prev = lax.rem(at_t + 3, TILES)
    to_opp = lax.rem(at_t + 2, TILES)
    to_next = lax.rem(at_t + 1, TILES)
    for n, (array, turned) in enumerate(((core_v, core_r), (over_v, over_r))):
        loads[n].wait()
        for f in range(PER):
            turned[f] = pltpu.roll(array[f], back, axis=1)
        firsts, pairs = [], []
        for e in range(OWN):
            mine = turned[OWN * to_prev + e]
            send1[n, e] = turn(mine[:, :128])
            firsts.append(mine[:, 128:])
            mine = turned[OWN * to_next + e]
            send3[n, e] = jnp.where(low, turn(mine[:, 128:]), turn(mine[:, :128]))
            pairs.append(turned[OWN * to_opp + e][:, :128])
        send1[n, 2] = jnp.where(low, firsts[0], turn(firsts[1]))
        send2[n, 0] = jnp.where(low, pairs[0], turn(pairs[1]))

    pl.semaphore_wait(barrier, len(first_devices))

    sends = []

    def push(src, dst, send_sem, recv_sem, device):
        copy = pltpu.make_async_remote_copy(
            src_ref=src,
            dst_ref=dst,
            send_sem=send_sem,
            recv_sem=recv_sem,
            device_id=device,
            device_id_type=MESH,
        )
        copy.start()
        sends.append(copy)
        return copy

    raw = [
        push(send2, got2, raw_send.at[1], raw_recv.at[1], tile_peer(2)),
        push(send1, got1, raw_send.at[0], raw_recv.at[0], tile_peer(3)),
        push(send3, got3, raw_send.at[2], raw_recv.at[2], tile_peer(1)),
    ]
    loads[7].wait()
    near = [
        push(near_c.at[1], near_c.at[0], nc_send.at[0], nc_recv.at[0], frag_peer(1)),
        push(near_c.at[1], near_c.at[2], nc_send.at[1], nc_recv.at[1], frag_peer(-1)),
    ]

    def spread_centres(step, carry):
        pltpu.make_async_remote_copy(
            src_ref=near_c.at[1],
            dst_ref=all_c.at[at_g],
            send_sem=ac_send,
            recv_sem=ac_recv,
            device_id=group_peer(step),
            device_id_type=MESH,
        ).start()
        return carry

    lax.fori_loop(1, groups, spread_centres, 0)
    for device in tile_devices:
        signal(ready.at[0], device)
    for step in (1, -1):
        signal(ready.at[1], z_peer(step))

    for n in (2, 3, 4):
        loads[n].wait()
    wide = (PER, PER * ROWS)
    prod = dot_nt(charge_v[...], gamma_v[...].reshape(PER * ROWS, BASIS))
    emb = pltpu.roll(embed_v[...], back, axis=1)[:, :128]
    emb = jnp.where(lanes((PER, 128)) < ROWS, emb, turn(emb))
    prod = prod + jnp.concatenate([emb] * 4, axis=1)
    same = lax.broadcasted_iota(jnp.int32, wide, 0) == lanes(wide) // ROWS
    fields = jnp.sum(jnp.where(same, prod, 0.0), axis=0, keepdims=True)
    for t in range(TILES):
        field_s[t] = fields[:, 128 * t : 128 * t + 128]
    fld = []
    for r in (2, 1, 3):
        dest = lax.rem(at_t + TILES - r, TILES)
        fld.append(
            push(field_s.at[dest], field_g.at[r], fld_send.at[r - 1], fld_recv.at[r - 1], (at_f, dest))
        )

    own = near_c[1].reshape(3 * PER, BASIS)
    cols = jnp.transpose(jnp.concatenate([own, jnp.zeros((128 - 3 * PER, BASIS), f32)], axis=0))
    for f in range(PER):
        for d in range(3):
            n = d * PER + f
            col_b[f, d] = jnp.broadcast_to(cols[:, n : n + 1], (BASIS, 128))
    for copy in near:
        copy.wait_recv()
    pl.semaphore_wait(ready.at[1], 2)
    for step in (2, -2):
        signal(ready.at[2], z_peer(step))

    near_first = at_f * PER - PER

    def pair(n, carry):
        f = n // LIST
        other = jnp.clip(near_sm[f, lax.rem(n, LIST)] - near_first, 0, 3 * PER - 1)
        slot = other // PER
        row = other - slot * PER
        src = [near_c[slot, d, pl.ds(row, 1), :] for d in range(3)]
        for r in range(4):
            rows = slice(64 * r, 64 * r + 64)
            for h in range(2):
                cut = slice(128 * h, 128 * h + 128)
                dist = 1.0
                for d in range(3):
                    diff = col_b[f, d, rows, :] - src[d][:, cut]
                    dist = dist + diff * diff
                kern_n[n, rows, cut] = lax.rsqrt(dist)
        return carry

    lax.fori_loop(0, FIRST_PAIRS, pair, 0)

    loads[8].wait()
    pltpu.make_async_copy(
        all_c.at[pl.ds(0, groups - 1)], all_c.at[pl.ds(0, groups - 1)], ac_recv
    ).wait()
    runs = lax.broadcasted_iota(jnp.int32, (PC, BASIS), 0) == lanes((PC, BASIS)) // (BASIS // PC)
    mean_run = (runs.astype(f32) * (PC / BASIS)).astype(bf16)
    sum_run = runs.astype(f32).astype(bf16)
    pad = jnp.zeros((PC, 128 - plane_frags), f32)
    for d in range(3):
        places = pick_nt(mean_run, all_c[:, d].reshape(plane_frags, BASIS))
        place_t[at_z, d] = jnp.concatenate([places, pad], axis=1)

    fld_rows = [field_s[at_t]]
    for copy in fld:
        copy.wait_recv()
    for r in (1, 2, 3):
        fld_rows.append(field_g[r])
    for copy in raw:
        copy.wait_recv()
    full_lanes = lanes((1, BASIS))
    low1 = lanes((1, 128)) < ROWS
    zero = jnp.zeros((ROWS, 128), f32)

    def halves(n, turned, e):
        top = turned[OWN * at_t + e]
        top = jnp.where(lanes((ROWS, BASIS)) < ROWS, 0.5 * top, top)
        one = got1[n, e]
        tail = got1[n, 2]
        tail = turn(tail) if e == 0 else tail
        opp = got2[n, 0]
        opp = opp if e == 0 else turn(opp)
        last = got3[n, e]
        return jnp.concatenate(
            [
                top,
                jnp.concatenate([jnp.where(low, 0.0, 0.5 * one), jnp.where(low, one, tail)], axis=1),
                jnp.concatenate([zero, jnp.where(low, 0.5 * opp, 0.0)], axis=1),
                jnp.concatenate([zero, jnp.where(low, last, 0.5 * last)], axis=1),
            ],
            axis=0,
        )

    square = (BASIS, BASIS)
    row_at = lax.broadcasted_iota(jnp.int32, square, 0)
    col_at = lanes(square)
    eye = (row_at == col_at).astype(f32)
    for e in range(OWN):
        half = halves(1, over_r, e)
        over = half + jnp.transpose(half)
        over_f[e] = over
        if e == 0:
            field = [jnp.where(low1, fld_rows[0], turn(fld_rows[1])), jnp.where(low1, fld_rows[2], turn(fld_rows[3]))]
        else:
            field = [jnp.where(low1, turn(fld_rows[0]), fld_rows[1]), jnp.where(low1, turn(fld_rows[2]), fld_rows[3])]
        field = jnp.concatenate(field, axis=1)
        half = halves(0, core_r, e) + 0.5 * over * field
        fock = half + jnp.transpose(half)
        size = size_sm[OWN * at_t + e]
        row_in = lax.rem(row_at + ROWS * at_t, BASIS) < size
        col_in = lax.rem(col_at + ROWS * at_t, BASIS) < size
        fock = jnp.where(row_in & col_in, fock, 0.0)
        total = jnp.sum(jnp.sum(fock * fock, axis=0, keepdims=True), axis=1, keepdims=True)
        fock = fock / jnp.sqrt(total + 1e-06)
        est[e] = fock + jnp.where(row_in, 0.0, eye)

    def near_product(a, b):
        mul = functools.partial(jnp.dot, preferred_element_type=f32)
        both = mul(jnp.concatenate(a, axis=0), b[0])
        rows = a[0].shape[0]
        return both[:rows] + both[rows:] + mul(a[0], b[1])

    def sweep(step, carry):
        now = [est[e] for e in range(OWN)]
        for _ in range(6):
            parts = [split(x) for x in now]
            cuts = [slice(r, r + 128) for r in range(0, BASIS, 128)]
            squares = [
                [split(near_product([p[cut] for p in part], part)) for cut in cuts] for part in parts
            ]
            now = [
                jnp.concatenate(
                    [1.5 * x[cut] - 0.5 * near_product(y, part) for cut, y in zip(cuts, square)], axis=0
                )
                for x, square, part in zip(now, squares, parts)
            ]
        for e in range(OWN):
            est[e] = now[e]
        return carry

    pl.semaphore_wait(ready.at[2], 2)

    def spread_places(step, carry):
        pltpu.make_async_remote_copy(
            src_ref=place_t.at[at_z],
            dst_ref=place_t.at[at_z],
            send_sem=pl_send,
            recv_sem=pl_recv,
            device_id=z_peer(step),
            device_id_type=MESH,
        ).start()
        return carry

    lax.fori_loop(1, planes, spread_places, 0)

    lax.fori_loop(0, ITERS // 6, sweep, 0)

    loads[5].wait()
    first = PER + at_g * PER + OWN * at_t
    for e in range(OWN):
        dens = 0.5 * (eye - est[e])
        charge = jnp.sum(dens * over_f[e], axis=0, keepdims=True)
        charge = pltpu.roll(jnp.broadcast_to(charge, (8, BASIS)), forth, axis=1)[0:1]
        charge = charge - pop_v[pl.ds(OWN * at_t + e, 1), :]
        table[first + e] = charge

    pl.semaphore_wait(ready.at[0], len(tile_devices))
    for device in plane_devices:
        pltpu.make_async_remote_copy(
            src_ref=table.at[pl.ds(first, OWN)],
            dst_ref=table.at[pl.ds(first, OWN)],
            send_sem=tb_send,
            recv_sem=tb_recv,
            device_id=device,
            device_id_type=MESH,
        ).start()

    for e in range(OWN):
        dens = pltpu.roll(0.5 * (eye - est[e]), forth, axis=1)
        for r in range(TILES):
            dens_s[r, e] = dens[ROWS * r : ROWS * r + ROWS]
    slot = density_out.at[pl.ds(OWN * at_t, OWN)]
    den = [push(dens_s.at[r], slot, dn_send.at[r - 1], dn_recv.at[r - 1], tile_peer(r)) for r in (2, 1, 3)]
    keep = pltpu.make_async_copy(dens_s.at[0], slot, out_sem.at[0])
    keep.start()

    loads[6].wait()
    far_list = far_v[...].astype(f32)
    diag = lax.broadcasted_iota(jnp.int32, (LIST, LIST), 0) == lanes((LIST, LIST))
    far_at = [
        jnp.sum(jnp.where(diag, jnp.broadcast_to(far_list[f : f + 1], (LIST, LIST)), 0.0), axis=1, keepdims=True)
        for f in range(PER)
    ]
    far_at = jnp.broadcast_to(jnp.concatenate(far_at, axis=0), (PER * LIST, 128))
    lane64 = lanes((PER * LIST, 128))
    picks = []
    for z in range(planes):
        entry = jnp.where(lane64 < plane_frags, lane64 + z * plane_frags, -1).astype(f32)
        picks.append((far_at == entry).astype(f32))
    pick = jnp.concatenate(picks, axis=1).astype(bf16)
    pltpu.make_async_copy(
        place_t.at[pl.ds(0, planes - 1)], place_t.at[pl.ds(0, planes - 1)], pl_recv
    ).wait()
    far_place = pick_nt(
        pick, jnp.concatenate([place_t[z].reshape(3 * PC, 128) for z in range(planes)], axis=1)
    )
    spots = [
        jnp.concatenate([jnp.broadcast_to(near_c[1, d, f : f + 1, :], (LIST, BASIS)) for f in range(PER)], axis=0)
        for d in range(3)
    ]
    for p in range(PC):
        dist = 1.0
        for d in range(3):
            diff = spots[d] - far_place[:, d * PC + p : d * PC + p + 1]
            dist = dist + diff * diff
        kern_f[p] = lax.rsqrt(dist)

    lax.fori_loop(FIRST_PAIRS, NEXT_PAIRS, pair, 0)

    pltpu.make_async_copy(
        table.at[pl.ds(PER, plane_frags - OWN)], table.at[pl.ds(PER, plane_frags - OWN)], tb_recv
    ).wait()
    plane_charge = table[pl.ds(PER, plane_frags)].reshape(plane_frags, BASIS)
    block_t[at_z] = jnp.concatenate([pick_nt(sum_run, plane_charge), pad], axis=1)

    for device in z_devices:
        pltpu.make_async_remote_copy(
            src_ref=block_t.at[at_z],
            dst_ref=block_t.at[at_z],
            send_sem=bk_send,
            recv_sem=bk_recv,
            device_id=device,
            device_id_type=MESH,
        ).start()

    edge = [
        push(table.at[pl.ds(plane_frags, PER)], table.at[pl.ds(0, PER)], bd_send.at[0], bd_recv.at[0], z_peer(1)),
        push(table.at[pl.ds(PER, PER)], table.at[pl.ds(plane_frags + PER, PER)], bd_send.at[1], bd_recv.at[1], z_peer(-1)),
    ]

    lax.fori_loop(NEXT_PAIRS, PER * LIST, pair, 0)

    for copy in edge:
        copy.wait_recv()
    table_first = at_z * plane_frags - PER
    lane256 = lanes((BASIS, 128))
    near_cols = jnp.zeros((BASIS, 128), f32)

    def near_sum(f):
        acc = jnp.zeros((BASIS, 128), f32)
        for k in range(LIST):
            row = table[jnp.clip(near_sm[f, k] - table_first, 0, plane_frags + 2 * PER - 1)]
            acc = acc + kern_n[f * LIST + k, :, :128] * row[:, :128]
            acc = acc + kern_n[f * LIST + k, :, 128:] * row[:, 128:]
        return jnp.sum(acc, axis=1, keepdims=True)

    def near_step(f, cols):
        return jnp.where(lane256 == f, near_sum(f), cols)

    near_cols = lax.fori_loop(0, PER, near_step, near_cols)
    near_rows = jnp.transpose(near_cols)[:PER]

    pltpu.make_async_copy(
        block_t.at[pl.ds(0, planes - 1)], block_t.at[pl.ds(0, planes - 1)], bk_recv
    ).wait()
    far_charge = pick_nt(pick, jnp.concatenate([block_t[z] for z in range(planes)], axis=1))
    far_sum = jnp.zeros((PER * LIST, BASIS), f32)
    for p in range(PC):
        far_sum = far_sum + far_charge[:, p : p + 1] * kern_f[p]
    far_rows = jnp.sum(far_sum.reshape(PER, LIST, BASIS), axis=1)
    potential = 0.25 * (near_rows + far_rows)
    col_s[...] = jnp.transpose(jnp.concatenate([potential, jnp.zeros((128 - PER, BASIS), f32)], axis=0))
    mine = col_s[pl.ds(ROWS * at_t, ROWS), :]
    for f in range(PER):
        esp_out[f] = 0.5 * over_v[f] * (mine[:, f : f + 1] + potential[f : f + 1, :])

    for copy in den:
        copy.wait_recv()
    keep.wait()
    for copy in sends:
        copy.wait_send()
    for ref, count, sem in (
        (all_c, groups - 1, ac_send),
        (place_t, planes - 1, pl_send),
        (table, plane_frags - OWN, tb_send),
        (block_t, planes - 1, bk_send),
    ):
        pltpu.make_async_copy(ref.at[pl.ds(0, count)], ref.at[pl.ds(0, count)], sem).wait()


def store(density, esp, density_out, esp_out, sem):
    copies = [
        pltpu.make_async_copy(src, dst, sem.at[n])
        for n, (src, dst) in enumerate(((density, density_out), (esp, esp_out)))
    ]
    for copy in copies:
        copy.start()
    for copy in copies:
        copy.wait()


def per_device(
    planes,
    groups,
    core_fock,
    intersection,
    gamma_tile,
    charge_old,
    embed_old,
    core_pop,
    centres,
    frag_sizes,
    near_list,
    far_list,
):
    dma = pltpu.SemaphoreType.DMA
    smem = pl.BlockSpec(memory_space=pltpu.SMEM)
    hbm = pl.BlockSpec(memory_space=pltpu.HBM)
    vmem = pl.BlockSpec(memory_space=pltpu.VMEM)
    own = (PER, ROWS, BASIS)
    pieces = (ROWS, 128)
    plane_frags = groups * PER
    held = pl.pallas_call(
        functools.partial(kernel, planes, groups),
        out_shape=(pltpu.VMEM(own, f32), pltpu.VMEM(own, f32)),
        in_specs=[hbm] * 7 + [smem, smem, hbm],
        out_specs=(vmem, vmem),
        scratch_shapes=[
            pltpu.VMEM(own, f32),
            pltpu.VMEM(own, f32),
            pltpu.VMEM(own, f32),
            pltpu.VMEM((PER, BASIS), f32),
            pltpu.VMEM((PER, BASIS), f32),
            pltpu.VMEM((PER, BASIS), f32),
            pltpu.VMEM((PER, LIST), jnp.int32),
            pltpu.VMEM(own, f32),
            pltpu.VMEM(own, f32),
            pltpu.VMEM((2, 3) + pieces, f32),
            pltpu.VMEM((2, 1) + pieces, f32),
            pltpu.VMEM((2, 2) + pieces, f32),
            pltpu.VMEM((2, 3) + pieces, f32),
            pltpu.VMEM((2, 1) + pieces, f32),
            pltpu.VMEM((2, 2) + pieces, f32),
            pltpu.VMEM((TILES, 1, 128), f32),
            pltpu.VMEM((TILES, 1, 128), f32),
            pltpu.VMEM((3, 3, PER, BASIS), f32),
            pltpu.VMEM((groups, 3, PER, BASIS), f32),
            pltpu.VMEM((planes, 3, PC, 128), f32),
            pltpu.VMEM((PER, 3, BASIS, 128), f32),
            pltpu.VMEM((PER * LIST, BASIS, BASIS), f32),
            pltpu.VMEM((PC, PER * LIST, BASIS), f32),
            pltpu.VMEM((OWN, BASIS, BASIS), f32),
            pltpu.VMEM((OWN, BASIS, BASIS), f32),
            pltpu.VMEM((TILES, OWN, ROWS, BASIS), f32),
            pltpu.VMEM((plane_frags + 2 * PER, 1, BASIS), f32),
            pltpu.VMEM((planes, PC, 128), f32),
            pltpu.VMEM((BASIS, 128), f32),
            dma((9,)),
            dma((3,)),
            dma((3,)),
            dma((3,)),
            dma((3,)),
            dma((2,)),
            dma((2,)),
            dma,
            dma,
            dma,
            dma,
            dma,
            dma,
            dma((2,)),
            dma((2,)),
            dma,
            dma,
            dma((3,)),
            dma((3,)),
            dma((1,)),
            pltpu.SemaphoreType.REGULAR((3,)),
        ],
        compiler_params=pltpu.CompilerParams(
            collective_id=0, has_side_effects=True, vmem_limit_bytes=60 * 1024 * 1024
        ),
        name="scc_cycle",
    )(
        core_fock,
        intersection,
        gamma_tile,
        charge_old,
        embed_old,
        core_pop,
        jnp.transpose(centres, (1, 0, 2)),
        frag_sizes,
        near_list,
        far_list,
    )
    return pl.pallas_call(
        store,
        out_shape=(jax.ShapeDtypeStruct(own, f32), jax.ShapeDtypeStruct(own, f32)),
        in_specs=[vmem, vmem],
        out_specs=(pl.BlockSpec(memory_space=pl.ANY), pl.BlockSpec(memory_space=pl.ANY)),
        scratch_shapes=[dma((2,))],
        compiler_params=pltpu.CompilerParams(vmem_limit_bytes=1024 * 1024),
        name="store",
    )(*held)


def solution(mesh):
    groups = mesh.shape["frag"] // PLANES
    return build(mesh, PLANES, groups)


def build(mesh, planes, groups):
    in_specs = (
        P("frag", "tile", None),
        P("frag", "tile", None),
        P("frag", "tile", None),
        P("frag", None),
        P("frag", None),
        P("frag", None),
        P("frag", None, None),
        P("frag"),
        P("frag", None),
        P("frag", None),
    )
    out_specs = (P("frag", "tile", None), P("frag", "tile", None))
    return jax.shard_map(
        functools.partial(per_device, planes, groups),
        mesh=mesh,
        in_specs=in_specs,
        out_specs=out_specs,
        check_vma=False,
    )
```

```python
import functools
import jax
import jax.numpy as jnp
from jax import lax
from jax.experimental import pallas as pl
from jax.experimental.pallas import tpu as pltpu
from jax.sharding import PartitionSpec as P

ITERS = 12
TILES = 4
ROWS = 64
BASIS = 256
PER = 8
OWN = 2
PC = 8
LIST = 8
PLANES = 8
FIRST_PAIRS = 34

f32 = jnp.float32
bf16 = jnp.bfloat16
HI = lax.Precision.HIGHEST
MESH = pl.DeviceIdType.MESH


def dot_nt(a, b):
    return lax.dot_general(a, b, (((1,), (1,)), ((), ())), precision=HI, preferred_element_type=f32)


def split(x):
    high = x.astype(bf16)
    return high, (x - high.astype(f32)).astype(bf16)


def dot3(a, b):
    (ah, al), (bh, bl) = a, b
    mul = functools.partial(jnp.dot, preferred_element_type=f32)
    return mul(ah, bh) + mul(ah, bl) + mul(al, bh)


def pick_nt(sel, b):
    high = b.astype(bf16)
    rest = b - high.astype(f32)
    middle = rest.astype(bf16)
    least = (rest - middle.astype(f32)).astype(bf16)
    mul = functools.partial(
        lax.dot_general, dimension_numbers=(((1,), (1,)), ((), ())), preferred_element_type=f32
    )
    return mul(sel, high) + mul(sel, middle) + mul(sel, least)


def lanes(shape):
    return lax.broadcasted_iota(jnp.int32, shape, len(shape) - 1)


def turn(x):
    return pltpu.roll(x, ROWS, axis=1)


def kernel(
    planes,
    groups,
    core_hbm,
    over_hbm,
    gamma_hbm,
    charge_hbm,
    embed_hbm,
    pop_hbm,
    centre_hbm,
    size_sm,
    near_sm,
    far_hbm,
    density_out,
    esp_out,
    core_v,
    over_v,
    gamma_v,
    charge_v,
    embed_v,
    pop_v,
    far_v,
    core_r,
    over_r,
    send1,
    send2,
    send3,
    got1,
    got2,
    got3,
    field_s,
    field_g,
    near_c,
    all_c,
    place_t,
    col_b,
    kern_n,
    kern_f,
    est,
    over_f,
    dens_s,
    table,
    block_t,
    col_s,
    in_sem,
    raw_send,
    raw_recv,
    fld_send,
    fld_recv,
    nc_send,
    nc_recv,
    ac_send,
    ac_recv,
    pl_send,
    pl_recv,
    tb_send,
    tb_recv,
    bd_send,
    bd_recv,
    bk_send,
    bk_recv,
    dn_send,
    dn_recv,
    out_sem,
    ready,
):
    plane_frags = groups * PER
    at_f = lax.axis_index("frag")
    at_t = lax.axis_index("tile")
    at_z = at_f // groups
    at_g = lax.rem(at_f, groups)
    frag_devs = planes * groups

    def tile_peer(step):
        return (at_f, lax.rem(at_t + step, TILES))

    def frag_peer(step):
        return (lax.rem(at_f + frag_devs + step, frag_devs), at_t)

    deep = groups // 2
    ring = lambda n, size: min(n, size - n)
    steps = [(dx, dy, dc) for dx in range(TILES) for dy in range(deep) for dc in range(2)][1:]
    steps.sort(key=lambda s: (-ring(s[0], TILES) - ring(s[1], deep), -s[2]))
    at_c = lax.rem(at_g, 2)
    peer_x = [lax.rem(at_t + dx, TILES) for dx in range(TILES)]
    peer_g = [
        [at_z * groups + 2 * lax.rem(at_g // 2 + dy, deep) + (1 - at_c if dc else at_c) for dc in range(2)]
        for dy in range(deep)
    ]
    plane_devices = [(peer_g[dy][dc], peer_x[dx]) for dx, dy, dc in steps]

    def group_peer(step):
        return (at_z * groups + lax.rem(at_g + step, groups), at_t)

    def z_peer(step):
        return (lax.rem(at_z + planes + step, planes) * groups + at_g, at_t)

    loads = [
        pltpu.make_async_copy(src, dst, in_sem.at[n])
        for n, (src, dst) in enumerate(
            (
                (core_hbm, core_v),
                (over_hbm, over_v),
                (gamma_hbm, gamma_v),
                (charge_hbm, charge_v),
                (embed_hbm, embed_v),
                (pop_hbm, pop_v),
                (far_hbm, far_v),
                (centre_hbm, near_c.at[1]),
                (centre_hbm, all_c.at[at_g]),
            )
        )
    ]
    for load in loads:
        load.start()

    barrier = pltpu.get_barrier_semaphore()

    def signal(sem, device):
        pl.semaphore_signal(sem, inc=1, device_id=device, device_id_type=MESH)

    z_steps = sorted(range(1, planes), key=lambda n: -ring(n, planes))
    z_devices = [z_peer(step) for step in z_steps]
    tile_devices = [tile_peer(step) for step in (2, 1, 3)]
    first_devices = tile_devices + [frag_peer(1), frag_peer(-1), z_peer(1), z_peer(-1)]
    first_devices += [group_peer(step) for step in range(1, groups)]
    for device in first_devices:
        signal(barrier, device)

    back = lax.rem(BASIS - ROWS * at_t, BASIS)
    forth = ROWS * at_t
    lane128 = lanes((ROWS, 128))
    low = lane128 < ROWS
    to_prev = lax.rem(at_t + 3, TILES)
    to_opp = lax.rem(at_t + 2, TILES)
    to_next = lax.rem(at_t + 1, TILES)
    for n, (array, turned) in enumerate(((core_v, core_r), (over_v, over_r))):
        loads[n].wait()
        for f in range(PER):
            turned[f] = pltpu.roll(array[f], back, axis=1)
        firsts, pairs = [], []
        for e in range(OWN):
            mine = turned[OWN * to_prev + e]
            send1[n, e] = turn(mine[:, :128])
            firsts.append(mine[:, 128:])
            mine = turned[OWN * to_next + e]
            send3[n, e] = jnp.where(low, turn(mine[:, 128:]), turn(mine[:, :128]))
            pairs.append(turned[OWN * to_opp + e][:, :128])
        send1[n, 2] = jnp.where(low, firsts[0], turn(firsts[1]))
        send2[n, 0] = jnp.where(low, pairs[0], turn(pairs[1]))

    pl.semaphore_wait(barrier, len(first_devices))

    sends = []

    def push(src, dst, send_sem, recv_sem, device):
        copy = pltpu.make_async_remote_copy(
            src_ref=src,
            dst_ref=dst,
            send_sem=send_sem,
            recv_sem=recv_sem,
            device_id=device,
            device_id_type=MESH,
        )
        copy.start()
        sends.append(copy)
        return copy

    raw = [
        push(send2, got2, raw_send.at[1], raw_recv.at[1], tile_peer(2)),
        push(send1, got1, raw_send.at[0], raw_recv.at[0], tile_peer(3)),
        push(send3, got3, raw_send.at[2], raw_recv.at[2], tile_peer(1)),
    ]
    loads[7].wait()
    near = [
        push(near_c.at[1], near_c.at[0], nc_send.at[0], nc_recv.at[0], frag_peer(1)),
        push(near_c.at[1], near_c.at[2], nc_send.at[1], nc_recv.at[1], frag_peer(-1)),
    ]

    def spread_centres(step, carry):
        pltpu.make_async_remote_copy(
            src_ref=near_c.at[1],
            dst_ref=all_c.at[at_g],
            send_sem=ac_send,
            recv_sem=ac_recv,
            device_id=group_peer(step),
            device_id_type=MESH,
        ).start()
        return carry

    lax.fori_loop(1, groups, spread_centres, 0)
    for device in tile_devices:
        signal(ready.at[0], device)
    for step in (1, -1):
        signal(ready.at[1], z_peer(step))

    for n in (2, 3, 4):
        loads[n].wait()
    wide = (PER, PER * ROWS)
    prod = dot_nt(charge_v[...], gamma_v[...].reshape(PER * ROWS, BASIS))
    emb = pltpu.roll(embed_v[...], back, axis=1)[:, :128]
    emb = jnp.where(lanes((PER, 128)) < ROWS, emb, turn(emb))
    prod = prod + jnp.concatenate([emb] * 4, axis=1)
    same = lax.broadcasted_iota(jnp.int32, wide, 0) == lanes(wide) // ROWS
    fields = jnp.sum(jnp.where(same, prod, 0.0), axis=0, keepdims=True)
    for t in range(TILES):
        field_s[t] = fields[:, 128 * t : 128 * t + 128]
    fld = []
    for r in (2, 1, 3):
        dest = lax.rem(at_t + TILES - r, TILES)
        fld.append(
            push(field_s.at[dest], field_g.at[r], fld_send.at[r - 1], fld_recv.at[r - 1], (at_f, dest))
        )

    own = near_c[1].reshape(3 * PER, BASIS)
    cols = jnp.transpose(jnp.concatenate([own, jnp.zeros((128 - 3 * PER, BASIS), f32)], axis=0))
    for f in range(PER):
        for d in range(3):
            n = d * PER + f
            col_b[f, d] = jnp.broadcast_to(cols[:, n : n + 1], (BASIS, 128))
    for copy in near:
        copy.wait_recv()
    pl.semaphore_wait(ready.at[1], 2)
    for step in (2, -2):
        signal(ready.at[2], z_peer(step))

    near_first = at_f * PER - PER

    def pair(n, carry):
        f = n // LIST
        other = jnp.clip(near_sm[f, lax.rem(n, LIST)] - near_first, 0, 3 * PER - 1)
        slot = other // PER
        row = other - slot * PER
        src = [near_c[slot, d, pl.ds(row, 1), :] for d in range(3)]
        for r in range(4):
            rows = slice(64 * r, 64 * r + 64)
            for h in range(2):
                cut = slice(128 * h, 128 * h + 128)
                dist = 1.0
                for d in range(3):
                    diff = col_b[f, d, rows, :] - src[d][:, cut]
                    dist = dist + diff * diff
                kern_n[n, rows, cut] = lax.rsqrt(dist)
        return carry

    lax.fori_loop(0, FIRST_PAIRS, pair, 0)

    loads[8].wait()
    pltpu.make_async_copy(
        all_c.at[pl.ds(0, groups - 1)], all_c.at[pl.ds(0, groups - 1)], ac_recv
    ).wait()
    runs = lax.broadcasted_iota(jnp.int32, (PC, BASIS), 0) == lanes((PC, BASIS)) // (BASIS // PC)
    mean_run = (runs.astype(f32) * (PC / BASIS)).astype(bf16)
    sum_run = runs.astype(f32).astype(bf16)
    pad = jnp.zeros((PC, 128 - plane_frags), f32)
    for d in range(3):
        places = pick_nt(mean_run, all_c[:, d].reshape(plane_frags, BASIS))
        place_t[at_z, d] = jnp.concatenate([places, pad], axis=1)

    fld_rows = [field_s[at_t]]
    for copy in fld:
        copy.wait_recv()
    for r in (1, 2, 3):
        fld_rows.append(field_g[r])
    for copy in raw:
        copy.wait_recv()
    full_lanes = lanes((1, BASIS))
    low1 = lanes((1, 128)) < ROWS
    zero = jnp.zeros((ROWS, 128), f32)

    def halves(n, turned, e):
        top = turned[OWN * at_t + e]
        top = jnp.where(lanes((ROWS, BASIS)) < ROWS, 0.5 * top, top)
        one = got1[n, e]
        tail = got1[n, 2]
        tail = turn(tail) if e == 0 else tail
        opp = got2[n, 0]
        opp = opp if e == 0 else turn(opp)
        last = got3[n, e]
        return jnp.concatenate(
            [
                top,
                jnp.concatenate([jnp.where(low, 0.0, 0.5 * one), jnp.where(low, one, tail)], axis=1),
                jnp.concatenate([zero, jnp.where(low, 0.5 * opp, 0.0)], axis=1),
                jnp.concatenate([zero, jnp.where(low, last, 0.5 * last)], axis=1),
            ],
            axis=0,
        )

    square = (BASIS, BASIS)
    row_at = lax.broadcasted_iota(jnp.int32, square, 0)
    col_at = lanes(square)
    eye = (row_at == col_at).astype(f32)
    for e in range(OWN):
        half = halves(1, over_r, e)
        over = half + jnp.transpose(half)
        over_f[e] = over
        if e == 0:
            field = [jnp.where(low1, fld_rows[0], turn(fld_rows[1])), jnp.where(low1, fld_rows[2], turn(fld_rows[3]))]
        else:
            field = [jnp.where(low1, turn(fld_rows[0]), fld_rows[1]), jnp.where(low1, turn(fld_rows[2]), fld_rows[3])]
        field = jnp.concatenate(field, axis=1)
        half = halves(0, core_r, e) + 0.5 * over * field
        fock = half + jnp.transpose(half)
        size = size_sm[OWN * at_t + e]
        row_in = lax.rem(row_at + ROWS * at_t, BASIS) < size
        col_in = lax.rem(col_at + ROWS * at_t, BASIS) < size
        fock = jnp.where(row_in & col_in, fock, 0.0)
        total = jnp.sum(jnp.sum(fock * fock, axis=0, keepdims=True), axis=1, keepdims=True)
        fock = fock / jnp.sqrt(total + 1e-06)
        est[e] = fock + jnp.where(row_in, 0.0, eye)

    def near_product(a, b):
        mul = functools.partial(jnp.dot, preferred_element_type=f32)
        both = mul(jnp.concatenate(a, axis=0), b[0])
        rows = a[0].shape[0]
        return both[:rows] + both[rows:] + mul(a[0], b[1])

    def sweep(step, carry):
        now = [est[e] for e in range(OWN)]
        for _ in range(6):
            parts = [split(x) for x in now]
            cuts = [slice(r, r + 128) for r in range(0, BASIS, 128)]
            squares = [
                [split(near_product([p[cut] for p in part], part)) for cut in cuts] for part in parts
            ]
            now = [
                jnp.concatenate(
                    [1.5 * x[cut] - 0.5 * near_product(y, part) for cut, y in zip(cuts, square)], axis=0
                )
                for x, square, part in zip(now, squares, parts)
            ]
        for e in range(OWN):
            est[e] = now[e]
        return carry

    pl.semaphore_wait(ready.at[2], 2)

    def spread_places(step, carry):
        pltpu.make_async_remote_copy(
            src_ref=place_t.at[at_z],
            dst_ref=place_t.at[at_z],
            send_sem=pl_send,
            recv_sem=pl_recv,
            device_id=z_peer(step),
            device_id_type=MESH,
        ).start()
        return carry

    lax.fori_loop(1, planes, spread_places, 0)

    lax.fori_loop(0, ITERS // 6, sweep, 0)

    loads[5].wait()
    first = PER + at_g * PER + OWN * at_t
    for e in range(OWN):
        dens = 0.5 * (eye - est[e])
        charge = jnp.sum(dens * over_f[e], axis=0, keepdims=True)
        charge = pltpu.roll(jnp.broadcast_to(charge, (8, BASIS)), forth, axis=1)[0:1]
        charge = charge - pop_v[pl.ds(OWN * at_t + e, 1), :]
        table[first + e] = charge

    pl.semaphore_wait(ready.at[0], len(tile_devices))
    def to_next_plane(end, step, row):
        @pl.when(at_g == end)
        def _():
            for t in range(TILES):
                pltpu.make_async_remote_copy(
                    src_ref=table.at[pl.ds(first, OWN)],
                    dst_ref=table.at[pl.ds(row + OWN * at_t, OWN)],
                    send_sem=bd_send.at[step],
                    recv_sem=bd_recv.at[step],
                    device_id=(frag_peer(1 if step == 0 else -1)[0], t),
                    device_id_type=MESH,
                ).start()

    to_next_plane(groups - 1, 0, 0)
    to_next_plane(0, 1, plane_frags + PER)
    for device in plane_devices:
        pltpu.make_async_remote_copy(
            src_ref=table.at[pl.ds(first, OWN)],
            dst_ref=table.at[pl.ds(first, OWN)],
            send_sem=tb_send,
            recv_sem=tb_recv,
            device_id=device,
            device_id_type=MESH,
        ).start()

    for e in range(OWN):
        dens = pltpu.roll(0.5 * (eye - est[e]), forth, axis=1)
        for r in range(TILES):
            dens_s[r, e] = dens[ROWS * r : ROWS * r + ROWS]
    slot = density_out.at[pl.ds(OWN * at_t, OWN)]
    den = [push(dens_s.at[r], slot, dn_send.at[r - 1], dn_recv.at[r - 1], tile_peer(r)) for r in (2, 1, 3)]
    keep = pltpu.make_async_copy(dens_s.at[0], slot, out_sem.at[0])
    keep.start()

    loads[6].wait()
    far_list = far_v[...].astype(f32)
    diag = lax.broadcasted_iota(jnp.int32, (LIST, LIST), 0) == lanes((LIST, LIST))
    far_at = [
        jnp.sum(jnp.where(diag, jnp.broadcast_to(far_list[f : f + 1], (LIST, LIST)), 0.0), axis=1, keepdims=True)
        for f in range(PER)
    ]
    far_at = jnp.broadcast_to(jnp.concatenate(far_at, axis=0), (PER * LIST, 128))
    lane64 = lanes((PER * LIST, 128))
    picks = []
    for z in range(planes):
        entry = jnp.where(lane64 < plane_frags, lane64 + z * plane_frags, -1).astype(f32)
        picks.append((far_at == entry).astype(f32))
    pick = jnp.concatenate(picks, axis=1).astype(bf16)
    pltpu.make_async_copy(
        place_t.at[pl.ds(0, planes - 1)], place_t.at[pl.ds(0, planes - 1)], pl_recv
    ).wait()
    far_place = pick_nt(
        pick, jnp.concatenate([place_t[z].reshape(3 * PC, 128) for z in range(planes)], axis=1)
    )
    spots = [
        jnp.concatenate([jnp.broadcast_to(near_c[1, d, f : f + 1, :], (LIST, BASIS)) for f in range(PER)], axis=0)
        for d in range(3)
    ]
    for p in range(PC):
        dist = 1.0
        for d in range(3):
            diff = spots[d] - far_place[:, d * PC + p : d * PC + p + 1]
            dist = dist + diff * diff
        kern_f[p] = lax.rsqrt(dist)

    lax.fori_loop(FIRST_PAIRS, PER * LIST, pair, 0)

    pltpu.make_async_copy(
        table.at[pl.ds(PER, plane_frags - OWN)], table.at[pl.ds(PER, plane_frags - OWN)], tb_recv
    ).wait()
    plane_charge = table[pl.ds(PER, plane_frags)].reshape(plane_frags, BASIS)
    block_t[at_z] = jnp.concatenate([pick_nt(sum_run, plane_charge), pad], axis=1)

    for device in z_devices:
        pltpu.make_async_remote_copy(
            src_ref=block_t.at[at_z],
            dst_ref=block_t.at[at_z],
            send_sem=bk_send,
            recv_sem=bk_recv,
            device_id=device,
            device_id_type=MESH,
        ).start()

    below = table.at[pl.ds(0, PER)]
    above = table.at[pl.ds(plane_frags + PER, PER)]

    @pl.when(at_g == 0)
    def _():
        pltpu.make_async_copy(below, below, bd_recv.at[0]).wait()

    @pl.when(at_g == groups - 1)
    def _():
        pltpu.make_async_copy(above, above, bd_recv.at[1]).wait()

    table_first = at_z * plane_frags - PER
    lane256 = lanes((BASIS, 128))
    near_cols = jnp.zeros((BASIS, 128), f32)

    def near_sum(f):
        acc = jnp.zeros((BASIS, 128), f32)
        for k in range(LIST):
            row = table[jnp.clip(near_sm[f, k] - table_first, 0, plane_frags + 2 * PER - 1)]
            acc = acc + kern_n[f * LIST + k, :, :128] * row[:, :128]
            acc = acc + kern_n[f * LIST + k, :, 128:] * row[:, 128:]
        return jnp.sum(acc, axis=1, keepdims=True)

    def near_step(f, cols):
        return jnp.where(lane256 == f, near_sum(f), cols)

    near_cols = lax.fori_loop(0, PER, near_step, near_cols)
    near_rows = jnp.transpose(near_cols)[:PER]

    pltpu.make_async_copy(
        block_t.at[pl.ds(0, planes - 1)], block_t.at[pl.ds(0, planes - 1)], bk_recv
    ).wait()
    far_charge = pick_nt(pick, jnp.concatenate([block_t[z] for z in range(planes)], axis=1))
    far_sum = jnp.zeros((PER * LIST, BASIS), f32)
    for p in range(PC):
        far_sum = far_sum + far_charge[:, p : p + 1] * kern_f[p]
    far_rows = jnp.sum(far_sum.reshape(PER, LIST, BASIS), axis=1)
    potential = 0.25 * (near_rows + far_rows)
    col_s[...] = jnp.transpose(jnp.concatenate([potential, jnp.zeros((128 - PER, BASIS), f32)], axis=0))
    mine = col_s[pl.ds(ROWS * at_t, ROWS), :]
    for f in range(PER):
        esp_out[f] = 0.5 * over_v[f] * (mine[:, f : f + 1] + potential[f : f + 1, :])

    for copy in den:
        copy.wait_recv()
    keep.wait()
    for copy in sends:
        copy.wait_send()
    for end, step in ((groups - 1, 0), (0, 1)):

        @pl.when(at_g == end)
        def _():
            pltpu.make_async_copy(below, below, bd_send.at[step]).wait()

    for ref, count, sem in (
        (all_c, groups - 1, ac_send),
        (place_t, planes - 1, pl_send),
        (table, plane_frags - OWN, tb_send),
        (block_t, planes - 1, bk_send),
    ):
        pltpu.make_async_copy(ref.at[pl.ds(0, count)], ref.at[pl.ds(0, count)], sem).wait()


def store(density, esp, density_out, esp_out, sem):
    copies = [
        pltpu.make_async_copy(src, dst, sem.at[n])
        for n, (src, dst) in enumerate(((density, density_out), (esp, esp_out)))
    ]
    for copy in copies:
        copy.start()
    for copy in copies:
        copy.wait()


def per_device(
    planes,
    groups,
    core_fock,
    intersection,
    gamma_tile,
    charge_old,
    embed_old,
    core_pop,
    centres,
    frag_sizes,
    near_list,
    far_list,
):
    dma = pltpu.SemaphoreType.DMA
    smem = pl.BlockSpec(memory_space=pltpu.SMEM)
    hbm = pl.BlockSpec(memory_space=pltpu.HBM)
    vmem = pl.BlockSpec(memory_space=pltpu.VMEM)
    own = (PER, ROWS, BASIS)
    pieces = (ROWS, 128)
    plane_frags = groups * PER
    held = pl.pallas_call(
        functools.partial(kernel, planes, groups),
        out_shape=(pltpu.VMEM(own, f32), pltpu.VMEM(own, f32)),
        in_specs=[hbm] * 7 + [smem, smem, hbm],
        out_specs=(vmem, vmem),
        scratch_shapes=[
            pltpu.VMEM(own, f32),
            pltpu.VMEM(own, f32),
            pltpu.VMEM(own, f32),
            pltpu.VMEM((PER, BASIS), f32),
            pltpu.VMEM((PER, BASIS), f32),
            pltpu.VMEM((PER, BASIS), f32),
            pltpu.VMEM((PER, LIST), jnp.int32),
            pltpu.VMEM(own, f32),
            pltpu.VMEM(own, f32),
            pltpu.VMEM((2, 3) + pieces, f32),
            pltpu.VMEM((2, 1) + pieces, f32),
            pltpu.VMEM((2, 2) + pieces, f32),
            pltpu.VMEM((2, 3) + pieces, f32),
            pltpu.VMEM((2, 1) + pieces, f32),
            pltpu.VMEM((2, 2) + pieces, f32),
            pltpu.VMEM((TILES, 1, 128), f32),
            pltpu.VMEM((TILES, 1, 128), f32),
            pltpu.VMEM((3, 3, PER, BASIS), f32),
            pltpu.VMEM((groups, 3, PER, BASIS), f32),
            pltpu.VMEM((planes, 3, PC, 128), f32),
            pltpu.VMEM((PER, 3, BASIS, 128), f32),
            pltpu.VMEM((PER * LIST, BASIS, BASIS), f32),
            pltpu.VMEM((PC, PER * LIST, BASIS), f32),
            pltpu.VMEM((OWN, BASIS, BASIS), f32),
            pltpu.VMEM((OWN, BASIS, BASIS), f32),
            pltpu.VMEM((TILES, OWN, ROWS, BASIS), f32),
            pltpu.VMEM((plane_frags + 2 * PER, 1, BASIS), f32),
            pltpu.VMEM((planes, PC, 128), f32),
            pltpu.VMEM((BASIS, 128), f32),
            dma((9,)),
            dma((3,)),
            dma((3,)),
            dma((3,)),
            dma((3,)),
            dma((2,)),
            dma((2,)),
            dma,
            dma,
            dma,
            dma,
            dma,
            dma,
            dma((2,)),
            dma((2,)),
            dma,
            dma,
            dma((3,)),
            dma((3,)),
            dma((1,)),
            pltpu.SemaphoreType.REGULAR((3,)),
        ],
        compiler_params=pltpu.CompilerParams(
            collective_id=0, has_side_effects=True, vmem_limit_bytes=60 * 1024 * 1024
        ),
        name="scc_cycle",
    )(
        core_fock,
        intersection,
        gamma_tile,
        charge_old,
        embed_old,
        core_pop,
        jnp.transpose(centres, (1, 0, 2)),
        frag_sizes,
        near_list,
        far_list,
    )
    return pl.pallas_call(
        store,
        out_shape=(jax.ShapeDtypeStruct(own, f32), jax.ShapeDtypeStruct(own, f32)),
        in_specs=[vmem, vmem],
        out_specs=(pl.BlockSpec(memory_space=pl.ANY), pl.BlockSpec(memory_space=pl.ANY)),
        scratch_shapes=[dma((2,))],
        compiler_params=pltpu.CompilerParams(vmem_limit_bytes=1024 * 1024),
        name="store",
    )(*held)


def solution(mesh):
    groups = mesh.shape["frag"] // PLANES
    return build(mesh, PLANES, groups)


def build(mesh, planes, groups):
    in_specs = (
        P("frag", "tile", None),
        P("frag", "tile", None),
        P("frag", "tile", None),
        P("frag", None),
        P("frag", None),
        P("frag", None),
        P("frag", None, None),
        P("frag"),
        P("frag", None),
        P("frag", None),
    )
    out_specs = (P("frag", "tile", None), P("frag", "tile", None))
    return jax.shard_map(
        functools.partial(per_device, planes, groups),
        mesh=mesh,
        in_specs=in_specs,
        out_specs=out_specs,
        check_vma=False,
    )
```

```python
import functools
import jax
import jax.numpy as jnp
from jax import lax
from jax.experimental import pallas as pl
from jax.experimental.pallas import tpu as pltpu
from jax.sharding import PartitionSpec as P

ITERS = 12
TILES = 4
ROWS = 64
BASIS = 256
PER = 8
OWN = 2
PC = 8
LIST = 8
PLANES = 8
FIRST_PAIRS = 28
NEXT_PAIRS = 56

f32 = jnp.float32
bf16 = jnp.bfloat16
HI = lax.Precision.HIGHEST
MESH = pl.DeviceIdType.MESH


def dot_nt(a, b):
    return lax.dot_general(a, b, (((1,), (1,)), ((), ())), precision=HI, preferred_element_type=f32)


def split(x):
    high = x.astype(bf16)
    return high, (x - high.astype(f32)).astype(bf16)


def dot3(a, b):
    (ah, al), (bh, bl) = a, b
    mul = functools.partial(jnp.dot, preferred_element_type=f32)
    return mul(ah, bh) + mul(ah, bl) + mul(al, bh)


def pick_nt(sel, b):
    high = b.astype(bf16)
    rest = b - high.astype(f32)
    middle = rest.astype(bf16)
    least = (rest - middle.astype(f32)).astype(bf16)
    mul = functools.partial(
        lax.dot_general, dimension_numbers=(((1,), (1,)), ((), ())), preferred_element_type=f32
    )
    return mul(sel, high) + mul(sel, middle) + mul(sel, least)


def lanes(shape):
    return lax.broadcasted_iota(jnp.int32, shape, len(shape) - 1)


def turn(x):
    return pltpu.roll(x, ROWS, axis=1)


def kernel(
    planes,
    groups,
    core_hbm,
    over_hbm,
    gamma_hbm,
    charge_hbm,
    embed_hbm,
    pop_hbm,
    centre_hbm,
    size_sm,
    near_sm,
    far_hbm,
    density_out,
    esp_out,
    core_v,
    over_v,
    gamma_v,
    charge_v,
    embed_v,
    pop_v,
    far_v,
    core_r,
    over_r,
    send1,
    send2,
    send3,
    got1,
    got2,
    got3,
    field_s,
    field_g,
    near_c,
    all_c,
    place_t,
    col_b,
    pick_v,
    kern_n,
    kern_f,
    est,
    over_f,
    dens_s,
    table,
    block_t,
    col_s,
    in_sem,
    raw_send,
    raw_recv,
    fld_send,
    fld_recv,
    nc_send,
    nc_recv,
    ac_send,
    ac_recv,
    pl_send,
    pl_recv,
    tb_send,
    tb_recv,
    bd_send,
    bd_recv,
    bk_send,
    bk_recv,
    dn_send,
    dn_recv,
    out_sem,
    ready,
):
    plane_frags = groups * PER
    at_f = lax.axis_index("frag")
    at_t = lax.axis_index("tile")
    at_z = at_f // groups
    at_g = lax.rem(at_f, groups)
    frag_devs = planes * groups

    def tile_peer(step):
        return (at_f, lax.rem(at_t + step, TILES))

    def frag_peer(step):
        return (lax.rem(at_f + frag_devs + step, frag_devs), at_t)

    deep = groups // 2
    ring = lambda n, size: min(n, size - n)
    steps = [(dx, dy, dc) for dx in range(TILES) for dy in range(deep) for dc in range(2)][1:]
    steps.sort(key=lambda s: (-ring(s[0], TILES) - ring(s[1], deep), -s[2]))
    at_c = lax.rem(at_g, 2)
    peer_x = [lax.rem(at_t + dx, TILES) for dx in range(TILES)]
    peer_g = [
        [at_z * groups + 2 * lax.rem(at_g // 2 + dy, deep) + (1 - at_c if dc else at_c) for dc in range(2)]
        for dy in range(deep)
    ]
    plane_devices = [(peer_g[dy][dc], peer_x[dx]) for dx, dy, dc in steps]

    def group_peer(step):
        return (at_z * groups + lax.rem(at_g + step, groups), at_t)

    def z_peer(step):
        return (lax.rem(at_z + planes + step, planes) * groups + at_g, at_t)

    loads = [
        pltpu.make_async_copy(src, dst, in_sem.at[n])
        for n, (src, dst) in enumerate(
            (
                (core_hbm, core_v),
                (over_hbm, over_v),
                (gamma_hbm, gamma_v),
                (charge_hbm, charge_v),
                (embed_hbm, embed_v),
                (pop_hbm, pop_v),
                (far_hbm, far_v),
                (centre_hbm, near_c.at[1]),
                (centre_hbm, all_c.at[at_g]),
            )
        )
    ]
    for load in loads:
        load.start()

    barrier = pltpu.get_barrier_semaphore()

    def signal(sem, device):
        pl.semaphore_signal(sem, inc=1, device_id=device, device_id_type=MESH)

    z_steps = sorted(range(1, planes), key=lambda n: -ring(n, planes))
    z_devices = [z_peer(step) for step in z_steps]
    tile_devices = [tile_peer(step) for step in (2, 1, 3)]
    first_devices = tile_devices + [frag_peer(1), frag_peer(-1), z_peer(1), z_peer(-1)]
    first_devices += [group_peer(step) for step in range(1, groups)]
    for device in first_devices:
        signal(barrier, device)

    back = lax.rem(BASIS - ROWS * at_t, BASIS)
    forth = ROWS * at_t
    lane128 = lanes((ROWS, 128))
    low = lane128 < ROWS
    to_prev = lax.rem(at_t + 3, TILES)
    to_opp = lax.rem(at_t + 2, TILES)
    to_next = lax.rem(at_t + 1, TILES)
    for n, (array, turned) in enumerate(((core_v, core_r), (over_v, over_r))):
        loads[n].wait()
        for f in range(PER):
            turned[f] = pltpu.roll(array[f], back, axis=1)
        firsts, pairs = [], []
        for e in range(OWN):
            mine = turned[OWN * to_prev + e]
            send1[n, e] = turn(mine[:, :128])
            firsts.append(mine[:, 128:])
            mine = turned[OWN * to_next + e]
            send3[n, e] = jnp.where(low, turn(mine[:, 128:]), turn(mine[:, :128]))
            pairs.append(turned[OWN * to_opp + e][:, :128])
        send1[n, 2] = jnp.where(low, firsts[0], turn(firsts[1]))
        send2[n, 0] = jnp.where(low, pairs[0], turn(pairs[1]))

    pl.semaphore_wait(barrier, len(first_devices))

    sends = []

    def push(src, dst, send_sem, recv_sem, device):
        copy = pltpu.make_async_remote_copy(
            src_ref=src,
            dst_ref=dst,
            send_sem=send_sem,
            recv_sem=recv_sem,
            device_id=device,
            device_id_type=MESH,
        )
        copy.start()
        sends.append(copy)
        return copy

    raw = [
        push(send2, got2, raw_send.at[1], raw_recv.at[1], tile_peer(2)),
        push(send1, got1, raw_send.at[0], raw_recv.at[0], tile_peer(3)),
        push(send3, got3, raw_send.at[2], raw_recv.at[2], tile_peer(1)),
    ]
    loads[7].wait()
    near = [
        push(near_c.at[1], near_c.at[0], nc_send.at[0], nc_recv.at[0], frag_peer(1)),
        push(near_c.at[1], near_c.at[2], nc_send.at[1], nc_recv.at[1], frag_peer(-1)),
    ]

    def spread_centres(step, carry):
        pltpu.make_async_remote_copy(
            src_ref=near_c.at[1],
            dst_ref=all_c.at[at_g],
            send_sem=ac_send,
            recv_sem=ac_recv,
            device_id=group_peer(step),
            device_id_type=MESH,
        ).start()
        return carry

    lax.fori_loop(1, groups, spread_centres, 0)
    for device in tile_devices:
        signal(ready.at[0], device)
    for step in (1, -1):
        signal(ready.at[1], z_peer(step))

    for n in (2, 3, 4):
        loads[n].wait()
    wide = (PER, PER * ROWS)
    prod = dot_nt(charge_v[...], gamma_v[...].reshape(PER * ROWS, BASIS))
    emb = pltpu.roll(embed_v[...], back, axis=1)[:, :128]
    emb = jnp.where(lanes((PER, 128)) < ROWS, emb, turn(emb))
    prod = prod + jnp.concatenate([emb] * 4, axis=1)
    same = lax.broadcasted_iota(jnp.int32, wide, 0) == lanes(wide) // ROWS
    fields = jnp.sum(jnp.where(same, prod, 0.0), axis=0, keepdims=True)
    for t in range(TILES):
        field_s[t] = fields[:, 128 * t : 128 * t + 128]
    fld = []
    for r in (2, 1, 3):
        dest = lax.rem(at_t + TILES - r, TILES)
        fld.append(
            push(field_s.at[dest], field_g.at[r], fld_send.at[r - 1], fld_recv.at[r - 1], (at_f, dest))
        )

    own = near_c[1]
    length = own[0] * own[0] + own[1] * own[1] + own[2] * own[2] + 1.0
    own = own.reshape(3 * PER, BASIS)
    cols = jnp.transpose(
        jnp.concatenate([own, length, jnp.zeros((128 - 4 * PER, BASIS), f32)], axis=0)
    )
    for f in range(PER):
        for d in range(3):
            n = d * PER + f
            col_b[f, d] = jnp.broadcast_to(cols[:, n : n + 1], (BASIS, 128))
        n = 3 * PER + f
        col_b[f, 3] = jnp.broadcast_to(cols[:, n : n + 1], (BASIS, 128))
    loads[6].wait()
    far_list = far_v[...].astype(f32)
    diag = lax.broadcasted_iota(jnp.int32, (LIST, LIST), 0) == lanes((LIST, LIST))
    far_at = [
        jnp.sum(jnp.where(diag, jnp.broadcast_to(far_list[f : f + 1], (LIST, LIST)), 0.0), axis=1, keepdims=True)
        for f in range(PER)
    ]
    far_at = jnp.broadcast_to(jnp.concatenate(far_at, axis=0), (PER * LIST, 128))
    lane64 = lanes((PER * LIST, 128))
    picks = []
    for z in range(planes):
        entry = jnp.where(lane64 < plane_frags, lane64 + z * plane_frags, -1).astype(f32)
        picks.append((far_at == entry).astype(f32))
    pick_v[...] = jnp.concatenate(picks, axis=1).astype(bf16)

    for copy in near:
        copy.wait_recv()
    pl.semaphore_wait(ready.at[1], 2)
    for step in (2, -2):
        signal(ready.at[2], z_peer(step))

    near_first = at_f * PER - PER

    def pair(n, carry):
        f = n // LIST
        other = jnp.clip(near_sm[f, lax.rem(n, LIST)] - near_first, 0, 3 * PER - 1)
        slot = other // PER
        row = other - slot * PER
        src = [near_c[slot, d, pl.ds(row, 1), :] for d in range(3)]
        src_length = src[0] * src[0] + src[1] * src[1] + src[2] * src[2]
        src = [-2.0 * x for x in src]
        for r in range(4):
            rows = slice(64 * r, 64 * r + 64)
            for h in range(2):
                cut = slice(128 * h, 128 * h + 128)
                dist = col_b[f, 3, rows, :] + src_length[:, cut]
                dot = col_b[f, 0, rows, :] * src[0][:, cut]
                for d in (1, 2):
                    dot = dot + col_b[f, d, rows, :] * src[d][:, cut]
                kern_n[n, rows, cut] = lax.rsqrt(dist + dot)
        return carry

    lax.fori_loop(0, FIRST_PAIRS, pair, 0)

    loads[8].wait()
    pltpu.make_async_copy(
        all_c.at[pl.ds(0, groups - 1)], all_c.at[pl.ds(0, groups - 1)], ac_recv
    ).wait()
    runs = lax.broadcasted_iota(jnp.int32, (PC, BASIS), 0) == lanes((PC, BASIS)) // (BASIS // PC)
    mean_run = (runs.astype(f32) * (PC / BASIS)).astype(bf16)
    sum_run = runs.astype(f32).astype(bf16)
    pad = jnp.zeros((PC, 128 - plane_frags), f32)
    for d in range(3):
        places = pick_nt(mean_run, all_c[:, d].reshape(plane_frags, BASIS))
        place_t[at_z, d] = jnp.concatenate([places, pad], axis=1)

    fld_rows = [field_s[at_t]]
    for copy in fld:
        copy.wait_recv()
    for r in (1, 2, 3):
        fld_rows.append(field_g[r])
    for copy in raw:
        copy.wait_recv()
    full_lanes = lanes((1, BASIS))
    low1 = lanes((1, 128)) < ROWS
    zero = jnp.zeros((ROWS, 128), f32)

    def halves(n, turned, e):
        top = turned[OWN * at_t + e]
        top = jnp.where(lanes((ROWS, BASIS)) < ROWS, 0.5 * top, top)
        one = got1[n, e]
        tail = got1[n, 2]
        tail = turn(tail) if e == 0 else tail
        opp = got2[n, 0]
        opp = opp if e == 0 else turn(opp)
        last = got3[n, e]
        return jnp.concatenate(
            [
                top,
                jnp.concatenate([jnp.where(low, 0.0, 0.5 * one), jnp.where(low, one, tail)], axis=1),
                jnp.concatenate([zero, jnp.where(low, 0.5 * opp, 0.0)], axis=1),
                jnp.concatenate([zero, jnp.where(low, last, 0.5 * last)], axis=1),
            ],
            axis=0,
        )

    square = (BASIS, BASIS)
    row_at = lax.broadcasted_iota(jnp.int32, square, 0)
    col_at = lanes(square)
    eye = (row_at == col_at).astype(f32)
    for e in range(OWN):
        half = halves(1, over_r, e)
        over = half + jnp.transpose(half)
        over_f[e] = over
        if e == 0:
            field = [jnp.where(low1, fld_rows[0], turn(fld_rows[1])), jnp.where(low1, fld_rows[2], turn(fld_rows[3]))]
        else:
            field = [jnp.where(low1, turn(fld_rows[0]), fld_rows[1]), jnp.where(low1, turn(fld_rows[2]), fld_rows[3])]
        field = jnp.concatenate(field, axis=1)
        half = halves(0, core_r, e) + 0.5 * over * field
        fock = half + jnp.transpose(half)
        size = size_sm[OWN * at_t + e]
        row_in = lax.rem(row_at + ROWS * at_t, BASIS) < size
        col_in = lax.rem(col_at + ROWS * at_t, BASIS) < size
        fock = jnp.where(row_in & col_in, fock, 0.0)
        total = jnp.sum(jnp.sum(fock * fock, axis=0, keepdims=True), axis=1, keepdims=True)
        fock = fock / jnp.sqrt(total + 1e-06)
        est[e] = fock + jnp.where(row_in, 0.0, eye)

    def near_product(a, b):
        mul = functools.partial(jnp.dot, preferred_element_type=f32)
        both = mul(jnp.concatenate(a, axis=0), b[0])
        rows = a[0].shape[0]
        return both[:rows] + both[rows:] + mul(a[0], b[1])

    def sweep(step, carry):
        now = [est[e] for e in range(OWN)]
        for _ in range(6):
            parts = [split(x) for x in now]
            cuts = [slice(r, r + 128) for r in range(0, BASIS, 128)]
            squares = [
                [split(near_product([p[cut] for p in part], part)) for cut in cuts] for part in parts
            ]
            now = [
                jnp.concatenate(
                    [1.5 * x[cut] - 0.5 * near_product(y, part) for cut, y in zip(cuts, square)], axis=0
                )
                for x, square, part in zip(now, squares, parts)
            ]
        for e in range(OWN):
            est[e] = now[e]
        return carry

    pl.semaphore_wait(ready.at[2], 2)

    def spread_places(step, carry):
        pltpu.make_async_remote_copy(
            src_ref=place_t.at[at_z],
            dst_ref=place_t.at[at_z],
            send_sem=pl_send,
            recv_sem=pl_recv,
            device_id=z_peer(step),
            device_id_type=MESH,
        ).start()
        return carry

    lax.fori_loop(1, planes, spread_places, 0)

    lax.fori_loop(0, ITERS // 6, sweep, 0)

    loads[5].wait()
    first = PER + at_g * PER + OWN * at_t
    for e in range(OWN):
        dens = 0.5 * (eye - est[e])
        charge = jnp.sum(dens * over_f[e], axis=0, keepdims=True)
        charge = pltpu.roll(jnp.broadcast_to(charge, (8, BASIS)), forth, axis=1)[0:1]
        charge = charge - pop_v[pl.ds(OWN * at_t + e, 1), :]
        table[first + e] = charge

    pl.semaphore_wait(ready.at[0], len(tile_devices))
    def to_next_plane(end, step, row):
        @pl.when(at_g == end)
        def _():
            for t in range(TILES):
                pltpu.make_async_remote_copy(
                    src_ref=table.at[pl.ds(first, OWN)],
                    dst_ref=table.at[pl.ds(row + OWN * at_t, OWN)],
                    send_sem=bd_send.at[step],
                    recv_sem=bd_recv.at[step],
                    device_id=(frag_peer(1 if step == 0 else -1)[0], t),
                    device_id_type=MESH,
                ).start()

    to_next_plane(groups - 1, 0, 0)
    to_next_plane(0, 1, plane_frags + PER)
    for device in plane_devices:
        pltpu.make_async_remote_copy(
            src_ref=table.at[pl.ds(first, OWN)],
            dst_ref=table.at[pl.ds(first, OWN)],
            send_sem=tb_send,
            recv_sem=tb_recv,
            device_id=device,
            device_id_type=MESH,
        ).start()

    for e in range(OWN):
        dens = pltpu.roll(0.5 * (eye - est[e]), forth, axis=1)
        for r in range(TILES):
            dens_s[r, e] = dens[ROWS * r : ROWS * r + ROWS]
    slot = density_out.at[pl.ds(OWN * at_t, OWN)]
    den = [push(dens_s.at[r], slot, dn_send.at[r - 1], dn_recv.at[r - 1], tile_peer(r)) for r in (2, 1, 3)]
    keep = pltpu.make_async_copy(dens_s.at[0], slot, out_sem.at[0])
    keep.start()

    pick = pick_v[...]
    pltpu.make_async_copy(
        place_t.at[pl.ds(0, planes - 1)], place_t.at[pl.ds(0, planes - 1)], pl_recv
    ).wait()
    far_place = pick_nt(
        pick, jnp.concatenate([place_t[z].reshape(3 * PC, 128) for z in range(planes)], axis=1)
    )
    spots = [
        jnp.concatenate([jnp.broadcast_to(near_c[1, d, f : f + 1, :], (LIST, BASIS)) for f in range(PER)], axis=0)
        for d in range(3)
    ]
    for p in range(PC):
        dist = 1.0
        for d in range(3):
            diff = spots[d] - far_place[:, d * PC + p : d * PC + p + 1]
            dist = dist + diff * diff
        kern_f[p] = lax.rsqrt(dist)

    lax.fori_loop(FIRST_PAIRS, NEXT_PAIRS, pair, 0)

    pltpu.make_async_copy(
        table.at[pl.ds(PER, plane_frags - OWN)], table.at[pl.ds(PER, plane_frags - OWN)], tb_recv
    ).wait()
    plane_charge = table[pl.ds(PER, plane_frags)].reshape(plane_frags, BASIS)
    block_t[at_z] = jnp.concatenate([pick_nt(sum_run, plane_charge), pad], axis=1)

    for device in z_devices:
        pltpu.make_async_remote_copy(
            src_ref=block_t.at[at_z],
            dst_ref=block_t.at[at_z],
            send_sem=bk_send,
            recv_sem=bk_recv,
            device_id=device,
            device_id_type=MESH,
        ).start()

    lax.fori_loop(NEXT_PAIRS, PER * LIST, pair, 0)

    below = table.at[pl.ds(0, PER)]
    above = table.at[pl.ds(plane_frags + PER, PER)]

    @pl.when(at_g == 0)
    def _():
        pltpu.make_async_copy(below, below, bd_recv.at[0]).wait()

    @pl.when(at_g == groups - 1)
    def _():
        pltpu.make_async_copy(above, above, bd_recv.at[1]).wait()

    table_first = at_z * plane_frags - PER
    lane256 = lanes((BASIS, 128))
    near_cols = jnp.zeros((BASIS, 128), f32)

    def near_sum(f):
        acc = jnp.zeros((BASIS, 128), f32)
        for k in range(LIST):
            row = table[jnp.clip(near_sm[f, k] - table_first, 0, plane_frags + 2 * PER - 1)]
            acc = acc + kern_n[f * LIST + k, :, :128] * row[:, :128]
            acc = acc + kern_n[f * LIST + k, :, 128:] * row[:, 128:]
        return jnp.sum(acc, axis=1, keepdims=True)

    def near_step(f, cols):
        return jnp.where(lane256 == f, near_sum(f), cols)

    near_cols = lax.fori_loop(0, PER, near_step, near_cols)
    near_rows = jnp.transpose(near_cols)[:PER]

    pltpu.make_async_copy(
        block_t.at[pl.ds(0, planes - 1)], block_t.at[pl.ds(0, planes - 1)], bk_recv
    ).wait()
    far_charge = pick_nt(pick, jnp.concatenate([block_t[z] for z in range(planes)], axis=1))
    far_sum = jnp.zeros((PER * LIST, BASIS), f32)
    for p in range(PC):
        far_sum = far_sum + far_charge[:, p : p + 1] * kern_f[p]
    far_rows = jnp.sum(far_sum.reshape(PER, LIST, BASIS), axis=1)
    potential = 0.25 * (near_rows + far_rows)
    col_s[...] = jnp.transpose(jnp.concatenate([potential, jnp.zeros((128 - PER, BASIS), f32)], axis=0))
    mine = col_s[pl.ds(ROWS * at_t, ROWS), :]
    for f in range(PER):
        esp_out[f] = 0.5 * over_v[f] * (mine[:, f : f + 1] + potential[f : f + 1, :])

    for copy in den:
        copy.wait_recv()
    keep.wait()
    for copy in sends:
        copy.wait_send()
    for end, step in ((groups - 1, 0), (0, 1)):

        @pl.when(at_g == end)
        def _():
            pltpu.make_async_copy(below, below, bd_send.at[step]).wait()

    for ref, count, sem in (
        (all_c, groups - 1, ac_send),
        (place_t, planes - 1, pl_send),
        (table, plane_frags - OWN, tb_send),
        (block_t, planes - 1, bk_send),
    ):
        pltpu.make_async_copy(ref.at[pl.ds(0, count)], ref.at[pl.ds(0, count)], sem).wait()


def store(density, esp, density_out, esp_out, sem):
    copies = [
        pltpu.make_async_copy(src, dst, sem.at[n])
        for n, (src, dst) in enumerate(((density, density_out), (esp, esp_out)))
    ]
    for copy in copies:
        copy.start()
    for copy in copies:
        copy.wait()


def per_device(
    planes,
    groups,
    core_fock,
    intersection,
    gamma_tile,
    charge_old,
    embed_old,
    core_pop,
    centres,
    frag_sizes,
    near_list,
    far_list,
):
    dma = pltpu.SemaphoreType.DMA
    smem = pl.BlockSpec(memory_space=pltpu.SMEM)
    hbm = pl.BlockSpec(memory_space=pltpu.HBM)
    vmem = pl.BlockSpec(memory_space=pltpu.VMEM)
    own = (PER, ROWS, BASIS)
    pieces = (ROWS, 128)
    plane_frags = groups * PER
    held = pl.pallas_call(
        functools.partial(kernel, planes, groups),
        out_shape=(pltpu.VMEM(own, f32), pltpu.VMEM(own, f32)),
        in_specs=[hbm] * 7 + [smem, smem, hbm],
        out_specs=(vmem, vmem),
        scratch_shapes=[
            pltpu.VMEM(own, f32),
            pltpu.VMEM(own, f32),
            pltpu.VMEM(own, f32),
            pltpu.VMEM((PER, BASIS), f32),
            pltpu.VMEM((PER, BASIS), f32),
            pltpu.VMEM((PER, BASIS), f32),
            pltpu.VMEM((PER, LIST), jnp.int32),
            pltpu.VMEM(own, f32),
            pltpu.VMEM(own, f32),
            pltpu.VMEM((2, 3) + pieces, f32),
            pltpu.VMEM((2, 1) + pieces, f32),
            pltpu.VMEM((2, 2) + pieces, f32),
            pltpu.VMEM((2, 3) + pieces, f32),
            pltpu.VMEM((2, 1) + pieces, f32),
            pltpu.VMEM((2, 2) + pieces, f32),
            pltpu.VMEM((TILES, 1, 128), f32),
            pltpu.VMEM((TILES, 1, 128), f32),
            pltpu.VMEM((3, 3, PER, BASIS), f32),
            pltpu.VMEM((groups, 3, PER, BASIS), f32),
            pltpu.VMEM((planes, 3, PC, 128), f32),
            pltpu.VMEM((PER, 4, BASIS, 128), f32),
            pltpu.VMEM((PER * LIST, planes * 128), bf16),
            pltpu.VMEM((PER * LIST, BASIS, BASIS), f32),
            pltpu.VMEM((PC, PER * LIST, BASIS), f32),
            pltpu.VMEM((OWN, BASIS, BASIS), f32),
            pltpu.VMEM((OWN, BASIS, BASIS), f32),
            pltpu.VMEM((TILES, OWN, ROWS, BASIS), f32),
            pltpu.VMEM((plane_frags + 2 * PER, 1, BASIS), f32),
            pltpu.VMEM((planes, PC, 128), f32),
            pltpu.VMEM((BASIS, 128), f32),
            dma((9,)),
            dma((3,)),
            dma((3,)),
            dma((3,)),
            dma((3,)),
            dma((2,)),
            dma((2,)),
            dma,
            dma,
            dma,
            dma,
            dma,
            dma,
            dma((2,)),
            dma((2,)),
            dma,
            dma,
            dma((3,)),
            dma((3,)),
            dma((1,)),
            pltpu.SemaphoreType.REGULAR((3,)),
        ],
        compiler_params=pltpu.CompilerParams(
            collective_id=0, has_side_effects=True, vmem_limit_bytes=60 * 1024 * 1024
        ),
        name="scc_cycle",
    )(
        core_fock,
        intersection,
        gamma_tile,
        charge_old,
        embed_old,
        core_pop,
        jnp.transpose(centres, (1, 0, 2)),
        frag_sizes,
        near_list,
        far_list,
    )
    return pl.pallas_call(
        store,
        out_shape=(jax.ShapeDtypeStruct(own, f32), jax.ShapeDtypeStruct(own, f32)),
        in_specs=[vmem, vmem],
        out_specs=(pl.BlockSpec(memory_space=pl.ANY), pl.BlockSpec(memory_space=pl.ANY)),
        scratch_shapes=[dma((2,))],
        compiler_params=pltpu.CompilerParams(vmem_limit_bytes=1024 * 1024),
        name="store",
    )(*held)


def solution(mesh):
    groups = mesh.shape["frag"] // PLANES
    return build(mesh, PLANES, groups)


def build(mesh, planes, groups):
    in_specs = (
        P("frag", "tile", None),
        P("frag", "tile", None),
        P("frag", "tile", None),
        P("frag", None),
        P("frag", None),
        P("frag", None),
        P("frag", None, None),
        P("frag"),
        P("frag", None),
        P("frag", None),
    )
    out_specs = (P("frag", "tile", None), P("frag", "tile", None))
    return jax.shard_map(
        functools.partial(per_device, planes, groups),
        mesh=mesh,
        in_specs=in_specs,
        out_specs=out_specs,
        check_vma=False,
    )
```

```python
import functools
import jax
import jax.numpy as jnp
from jax import lax
from jax.experimental import pallas as pl
from jax.experimental.pallas import tpu as pltpu
from jax.sharding import PartitionSpec as P

ITERS = 12
TILES = 4
ROWS = 64
BASIS = 256
PER = 8
OWN = 2
PC = 8
LIST = 8
PLANES = 8
FIRST_PAIRS = 35

f32 = jnp.float32
bf16 = jnp.bfloat16
HI = lax.Precision.HIGHEST
MESH = pl.DeviceIdType.MESH


def dot_nt(a, b):
    return lax.dot_general(a, b, (((1,), (1,)), ((), ())), precision=HI, preferred_element_type=f32)


def split(x):
    high = x.astype(bf16)
    return high, (x - high.astype(f32)).astype(bf16)


def dot3(a, b):
    (ah, al), (bh, bl) = a, b
    mul = functools.partial(jnp.dot, preferred_element_type=f32)
    return mul(ah, bh) + mul(ah, bl) + mul(al, bh)


def pick_nt(sel, b):
    high = b.astype(bf16)
    rest = b - high.astype(f32)
    middle = rest.astype(bf16)
    least = (rest - middle.astype(f32)).astype(bf16)
    mul = functools.partial(
        lax.dot_general, dimension_numbers=(((1,), (1,)), ((), ())), preferred_element_type=f32
    )
    return mul(sel, high) + mul(sel, middle) + mul(sel, least)


def lanes(shape):
    return lax.broadcasted_iota(jnp.int32, shape, len(shape) - 1)


def turn(x):
    return pltpu.roll(x, ROWS, axis=1)


def kernel(
    planes,
    groups,
    core_hbm,
    over_hbm,
    gamma_hbm,
    charge_hbm,
    embed_hbm,
    pop_hbm,
    centre_hbm,
    size_sm,
    near_sm,
    far_hbm,
    density_out,
    esp_out,
    core_v,
    over_v,
    gamma_v,
    charge_v,
    embed_v,
    pop_v,
    far_v,
    core_r,
    over_r,
    send1,
    send2,
    send3,
    got1,
    got2,
    got3,
    field_s,
    field_g,
    near_c,
    all_c,
    place_t,
    col_b,
    pick_v,
    kern_n,
    kern_f,
    est,
    over_f,
    dens_s,
    table,
    block_t,
    col_s,
    in_sem,
    raw_send,
    raw_recv,
    fld_send,
    fld_recv,
    nc_send,
    nc_recv,
    ac_send,
    ac_recv,
    pl_send,
    pl_recv,
    tb_send,
    tb_recv,
    bd_send,
    bd_recv,
    bk_send,
    bk_recv,
    dn_send,
    dn_recv,
    out_sem,
    ready,
):
    plane_frags = groups * PER
    at_f = lax.axis_index("frag")
    at_t = lax.axis_index("tile")
    at_z = at_f // groups
    at_g = lax.rem(at_f, groups)
    frag_devs = planes * groups

    def tile_peer(step):
        return (at_f, lax.rem(at_t + step, TILES))

    def frag_peer(step):
        return (lax.rem(at_f + frag_devs + step, frag_devs), at_t)

    deep = groups // 2
    ring = lambda n, size: min(n, size - n)
    steps = [(dx, dy, dc) for dx in range(TILES) for dy in range(deep) for dc in range(2)][1:]
    steps.sort(key=lambda s: (-ring(s[0], TILES) - ring(s[1], deep), -s[2]))
    at_c = lax.rem(at_g, 2)
    peer_x = [lax.rem(at_t + dx, TILES) for dx in range(TILES)]
    peer_g = [
        [at_z * groups + 2 * lax.rem(at_g // 2 + dy, deep) + (1 - at_c if dc else at_c) for dc in range(2)]
        for dy in range(deep)
    ]
    plane_devices = [(peer_g[dy][dc], peer_x[dx]) for dx, dy, dc in steps]

    def group_peer(step):
        return (at_z * groups + lax.rem(at_g + step, groups), at_t)

    def z_peer(step):
        return (lax.rem(at_z + planes + step, planes) * groups + at_g, at_t)

    loads = [
        pltpu.make_async_copy(src, dst, in_sem.at[n])
        for n, (src, dst) in enumerate(
            (
                (core_hbm, core_v),
                (over_hbm, over_v),
                (gamma_hbm, gamma_v),
                (charge_hbm, charge_v),
                (embed_hbm, embed_v),
                (pop_hbm, pop_v),
                (far_hbm, far_v),
                (centre_hbm, near_c.at[1]),
                (centre_hbm, all_c.at[at_g]),
            )
        )
    ]
    for load in loads:
        load.start()

    barrier = pltpu.get_barrier_semaphore()

    def signal(sem, device):
        pl.semaphore_signal(sem, inc=1, device_id=device, device_id_type=MESH)

    z_steps = sorted(range(1, planes), key=lambda n: -ring(n, planes))
    z_devices = [z_peer(step) for step in z_steps]
    tile_devices = [tile_peer(step) for step in (2, 1, 3)]
    first_devices = tile_devices + [frag_peer(1), frag_peer(-1), z_peer(1), z_peer(-1)]
    first_devices += [group_peer(step) for step in range(1, groups)]
    for device in first_devices:
        signal(barrier, device)

    back = lax.rem(BASIS - ROWS * at_t, BASIS)
    forth = ROWS * at_t
    lane128 = lanes((ROWS, 128))
    low = lane128 < ROWS
    to_prev = lax.rem(at_t + 3, TILES)
    to_opp = lax.rem(at_t + 2, TILES)
    to_next = lax.rem(at_t + 1, TILES)
    sends = []

    def push(src, dst, send_sem, recv_sem, device):
        copy = pltpu.make_async_remote_copy(
            src_ref=src,
            dst_ref=dst,
            send_sem=send_sem,
            recv_sem=recv_sem,
            device_id=device,
            device_id_type=MESH,
        )
        copy.start()
        sends.append(copy)
        return copy

    def pack(n, array, turned):
        loads[n].wait()
        for f in range(PER):
            turned[f] = pltpu.roll(array[f], back, axis=1)
        firsts, pairs = [], []
        for e in range(OWN):
            mine = turned[OWN * to_prev + e]
            send1[n, e] = turn(mine[:, :128])
            firsts.append(mine[:, 128:])
            mine = turned[OWN * to_next + e]
            send3[n, e] = jnp.where(low, turn(mine[:, 128:]), turn(mine[:, :128]))
            pairs.append(turned[OWN * to_opp + e][:, :128])
        send1[n, 2] = jnp.where(low, firsts[0], turn(firsts[1]))
        send2[n, 0] = jnp.where(low, pairs[0], turn(pairs[1]))

    def send_packed(n):
        return [
            push(send2.at[n], got2.at[n], raw_send.at[n, 1], raw_recv.at[n, 1], tile_peer(2)),
            push(send1.at[n], got1.at[n], raw_send.at[n, 0], raw_recv.at[n, 0], tile_peer(3)),
            push(send3.at[n], got3.at[n], raw_send.at[n, 2], raw_recv.at[n, 2], tile_peer(1)),
        ]

    pack(0, core_v, core_r)

    pl.semaphore_wait(barrier, len(first_devices))

    raw = send_packed(0)
    loads[7].wait()
    near = [
        push(near_c.at[1], near_c.at[0], nc_send.at[0], nc_recv.at[0], frag_peer(1)),
        push(near_c.at[1], near_c.at[2], nc_send.at[1], nc_recv.at[1], frag_peer(-1)),
    ]

    pack(1, over_v, over_r)
    raw += send_packed(1)

    def spread_centres(step, carry):
        pltpu.make_async_remote_copy(
            src_ref=near_c.at[1],
            dst_ref=all_c.at[at_g],
            send_sem=ac_send,
            recv_sem=ac_recv,
            device_id=group_peer(step),
            device_id_type=MESH,
        ).start()
        return carry

    lax.fori_loop(1, groups, spread_centres, 0)
    for device in tile_devices:
        signal(ready.at[0], device)
    for step in (1, -1):
        signal(ready.at[1], z_peer(step))

    for n in (2, 3, 4):
        loads[n].wait()
    wide = (PER, PER * ROWS)
    prod = dot_nt(charge_v[...], gamma_v[...].reshape(PER * ROWS, BASIS))
    emb = pltpu.roll(embed_v[...], back, axis=1)[:, :128]
    emb = jnp.where(lanes((PER, 128)) < ROWS, emb, turn(emb))
    prod = prod + jnp.concatenate([emb] * 4, axis=1)
    same = lax.broadcasted_iota(jnp.int32, wide, 0) == lanes(wide) // ROWS
    fields = jnp.sum(jnp.where(same, prod, 0.0), axis=0, keepdims=True)
    for t in range(TILES):
        field_s[t] = fields[:, 128 * t : 128 * t + 128]
    fld = []
    for r in (2, 1, 3):
        dest = lax.rem(at_t + TILES - r, TILES)
        fld.append(
            push(field_s.at[dest], field_g.at[r], fld_send.at[r - 1], fld_recv.at[r - 1], (at_f, dest))
        )

    own = near_c[1]
    length = own[0] * own[0] + own[1] * own[1] + own[2] * own[2] + 1.0
    own = own.reshape(3 * PER, BASIS)
    cols = jnp.transpose(
        jnp.concatenate([own, length, jnp.zeros((128 - 4 * PER, BASIS), f32)], axis=0)
    )
    for f in range(PER):
        for d in range(3):
            n = d * PER + f
            col_b[f, d] = jnp.broadcast_to(cols[:, n : n + 1], (BASIS, 128))
        n = 3 * PER + f
        col_b[f, 3] = jnp.broadcast_to(cols[:, n : n + 1], (BASIS, 128))
    loads[6].wait()
    far_list = far_v[...].astype(f32)
    diag = lax.broadcasted_iota(jnp.int32, (LIST, LIST), 0) == lanes((LIST, LIST))
    far_at = [
        jnp.sum(jnp.where(diag, jnp.broadcast_to(far_list[f : f + 1], (LIST, LIST)), 0.0), axis=1, keepdims=True)
        for f in range(PER)
    ]
    far_at = jnp.broadcast_to(jnp.concatenate(far_at, axis=0), (PER * LIST, 128))
    lane64 = lanes((PER * LIST, 128))
    picks = []
    for z in range(planes):
        entry = jnp.where(lane64 < plane_frags, lane64 + z * plane_frags, -1).astype(f32)
        picks.append((far_at == entry).astype(f32))
    pick_v[...] = jnp.concatenate(picks, axis=1).astype(bf16)

    for copy in near:
        copy.wait_recv()
    pl.semaphore_wait(ready.at[1], 2)
    for step in (2, -2):
        signal(ready.at[2], z_peer(step))

    near_first = at_f * PER - PER

    def pair(n, carry):
        f = n // LIST
        other = jnp.clip(near_sm[f, lax.rem(n, LIST)] - near_first, 0, 3 * PER - 1)
        slot = other // PER
        row = other - slot * PER
        src = [near_c[slot, d, pl.ds(row, 1), :] for d in range(3)]
        src_length = src[0] * src[0] + src[1] * src[1] + src[2] * src[2]
        src = [-2.0 * x for x in src]
        for r in range(4):
            rows = slice(64 * r, 64 * r + 64)
            for h in range(2):
                cut = slice(128 * h, 128 * h + 128)
                dist = col_b[f, 3, rows, :] + src_length[:, cut]
                dot = col_b[f, 0, rows, :] * src[0][:, cut]
                for d in (1, 2):
                    dot = dot + col_b[f, d, rows, :] * src[d][:, cut]
                kern_n[n, rows, cut] = lax.rsqrt(dist + dot)
        return carry

    lax.fori_loop(0, FIRST_PAIRS, pair, 0)

    loads[8].wait()
    pltpu.make_async_copy(
        all_c.at[pl.ds(0, groups - 1)], all_c.at[pl.ds(0, groups - 1)], ac_recv
    ).wait()
    runs = lax.broadcasted_iota(jnp.int32, (PC, BASIS), 0) == lanes((PC, BASIS)) // (BASIS // PC)
    mean_run = (runs.astype(f32) * (PC / BASIS)).astype(bf16)
    sum_run = runs.astype(f32).astype(bf16)
    pad = jnp.zeros((PC, 128 - plane_frags), f32)
    for d in range(3):
        places = pick_nt(mean_run, all_c[:, d].reshape(plane_frags, BASIS))
        place_t[at_z, d] = jnp.concatenate([places, pad], axis=1)

    fld_rows = [field_s[at_t]]
    for copy in fld:
        copy.wait_recv()
    for r in (1, 2, 3):
        fld_rows.append(field_g[r])
    for copy in raw:
        copy.wait_recv()
    full_lanes = lanes((1, BASIS))
    low1 = lanes((1, 128)) < ROWS
    zero = jnp.zeros((ROWS, 128), f32)

    def halves(n, turned, e):
        top = turned[OWN * at_t + e]
        top = jnp.where(lanes((ROWS, BASIS)) < ROWS, 0.5 * top, top)
        one = got1[n, e]
        tail = got1[n, 2]
        tail = turn(tail) if e == 0 else tail
        opp = got2[n, 0]
        opp = opp if e == 0 else turn(opp)
        last = got3[n, e]
        return jnp.concatenate(
            [
                top,
                jnp.concatenate([jnp.where(low, 0.0, 0.5 * one), jnp.where(low, one, tail)], axis=1),
                jnp.concatenate([zero, jnp.where(low, 0.5 * opp, 0.0)], axis=1),
                jnp.concatenate([zero, jnp.where(low, last, 0.5 * last)], axis=1),
            ],
            axis=0,
        )

    square = (BASIS, BASIS)
    row_at = lax.broadcasted_iota(jnp.int32, square, 0)
    col_at = lanes(square)
    eye = (row_at == col_at).astype(f32)
    for e in range(OWN):
        half = halves(1, over_r, e)
        over = half + jnp.transpose(half)
        over_f[e] = over
        if e == 0:
            field = [jnp.where(low1, fld_rows[0], turn(fld_rows[1])), jnp.where(low1, fld_rows[2], turn(fld_rows[3]))]
        else:
            field = [jnp.where(low1, turn(fld_rows[0]), fld_rows[1]), jnp.where(low1, turn(fld_rows[2]), fld_rows[3])]
        field = jnp.concatenate(field, axis=1)
        half = halves(0, core_r, e) + 0.5 * over * field
        fock = half + jnp.transpose(half)
        size = size_sm[OWN * at_t + e]
        row_in = lax.rem(row_at + ROWS * at_t, BASIS) < size
        col_in = lax.rem(col_at + ROWS * at_t, BASIS) < size
        fock = jnp.where(row_in & col_in, fock, 0.0)
        total = jnp.sum(jnp.sum(fock * fock, axis=0, keepdims=True), axis=1, keepdims=True)
        fock = fock / jnp.sqrt(total + 1e-06)
        est[e] = fock + jnp.where(row_in, 0.0, eye)

    def near_product(a, b):
        mul = functools.partial(jnp.dot, preferred_element_type=f32)
        both = mul(jnp.concatenate(a, axis=0), b[0])
        rows = a[0].shape[0]
        return both[:rows] + both[rows:] + mul(a[0], b[1])

    def sweep(step, carry):
        now = [est[e] for e in range(OWN)]
        for _ in range(6):
            parts = [split(x) for x in now]
            cuts = [slice(r, r + 128) for r in range(0, BASIS, 128)]
            squares = [
                [split(near_product([p[cut] for p in part], part)) for cut in cuts] for part in parts
            ]
            now = [
                jnp.concatenate(
                    [1.5 * x[cut] - 0.5 * near_product(y, part) for cut, y in zip(cuts, square)], axis=0
                )
                for x, square, part in zip(now, squares, parts)
            ]
        for e in range(OWN):
            est[e] = now[e]
        return carry

    pl.semaphore_wait(ready.at[2], 2)

    def spread_places(step, carry):
        pltpu.make_async_remote_copy(
            src_ref=place_t.at[at_z],
            dst_ref=place_t.at[at_z],
            send_sem=pl_send,
            recv_sem=pl_recv,
            device_id=z_peer(step),
            device_id_type=MESH,
        ).start()
        return carry

    lax.fori_loop(1, planes, spread_places, 0)

    lax.fori_loop(0, ITERS // 6, sweep, 0)

    loads[5].wait()
    first = PER + at_g * PER + OWN * at_t
    for e in range(OWN):
        dens = 0.5 * (eye - est[e])
        charge = jnp.sum(dens * over_f[e], axis=0, keepdims=True)
        charge = pltpu.roll(jnp.broadcast_to(charge, (8, BASIS)), forth, axis=1)[0:1]
        charge = charge - pop_v[pl.ds(OWN * at_t + e, 1), :]
        table[first + e] = charge

    pl.semaphore_wait(ready.at[0], len(tile_devices))
    def to_next_plane(end, step, row):
        @pl.when(at_g == end)
        def _():
            for t in range(TILES):
                pltpu.make_async_remote_copy(
                    src_ref=table.at[pl.ds(first, OWN)],
                    dst_ref=table.at[pl.ds(row + OWN * at_t, OWN)],
                    send_sem=bd_send.at[step],
                    recv_sem=bd_recv.at[step],
                    device_id=(frag_peer(1 if step == 0 else -1)[0], t),
                    device_id_type=MESH,
                ).start()

    to_next_plane(groups - 1, 0, 0)
    to_next_plane(0, 1, plane_frags + PER)
    for device in plane_devices:
        pltpu.make_async_remote_copy(
            src_ref=table.at[pl.ds(first, OWN)],
            dst_ref=table.at[pl.ds(first, OWN)],
            send_sem=tb_send,
            recv_sem=tb_recv,
            device_id=device,
            device_id_type=MESH,
        ).start()

    for e in range(OWN):
        dens = pltpu.roll(0.5 * (eye - est[e]), forth, axis=1)
        for r in range(TILES):
            dens_s[r, e] = dens[ROWS * r : ROWS * r + ROWS]
    slot = density_out.at[pl.ds(OWN * at_t, OWN)]
    den = [push(dens_s.at[r], slot, dn_send.at[r - 1], dn_recv.at[r - 1], tile_peer(r)) for r in (2, 1, 3)]
    keep = pltpu.make_async_copy(dens_s.at[0], slot, out_sem.at[0])
    keep.start()

    pick = pick_v[...]
    pltpu.make_async_copy(
        place_t.at[pl.ds(0, planes - 1)], place_t.at[pl.ds(0, planes - 1)], pl_recv
    ).wait()
    far_place = pick_nt(
        pick, jnp.concatenate([place_t[z].reshape(3 * PC, 128) for z in range(planes)], axis=1)
    )
    spots = [
        jnp.concatenate([jnp.broadcast_to(near_c[1, d, f : f + 1, :], (LIST, BASIS)) for f in range(PER)], axis=0)
        for d in range(3)
    ]
    for p in range(PC):
        dist = 1.0
        for d in range(3):
            diff = spots[d] - far_place[:, d * PC + p : d * PC + p + 1]
            dist = dist + diff * diff
        kern_f[p] = lax.rsqrt(dist)

    lax.fori_loop(FIRST_PAIRS, PER * LIST, pair, 0)

    pltpu.make_async_copy(
        table.at[pl.ds(PER, plane_frags - OWN)], table.at[pl.ds(PER, plane_frags - OWN)], tb_recv
    ).wait()
    plane_charge = table[pl.ds(PER, plane_frags)].reshape(plane_frags, BASIS)
    block_t[at_z] = jnp.concatenate([pick_nt(sum_run, plane_charge), pad], axis=1)

    for device in z_devices:
        pltpu.make_async_remote_copy(
            src_ref=block_t.at[at_z],
            dst_ref=block_t.at[at_z],
            send_sem=bk_send,
            recv_sem=bk_recv,
            device_id=device,
            device_id_type=MESH,
        ).start()

    below = table.at[pl.ds(0, PER)]
    above = table.at[pl.ds(plane_frags + PER, PER)]

    @pl.when(at_g == 0)
    def _():
        pltpu.make_async_copy(below, below, bd_recv.at[0]).wait()

    @pl.when(at_g == groups - 1)
    def _():
        pltpu.make_async_copy(above, above, bd_recv.at[1]).wait()

    table_first = at_z * plane_frags - PER
    lane256 = lanes((BASIS, 128))
    near_cols = jnp.zeros((BASIS, 128), f32)

    def near_sum(f):
        acc = jnp.zeros((BASIS, 128), f32)
        for k in range(LIST):
            row = table[jnp.clip(near_sm[f, k] - table_first, 0, plane_frags + 2 * PER - 1)]
            acc = acc + kern_n[f * LIST + k, :, :128] * row[:, :128]
            acc = acc + kern_n[f * LIST + k, :, 128:] * row[:, 128:]
        return jnp.sum(acc, axis=1, keepdims=True)

    def near_step(f, cols):
        return jnp.where(lane256 == f, near_sum(f), cols)

    near_cols = lax.fori_loop(0, PER, near_step, near_cols)
    near_rows = jnp.transpose(near_cols)[:PER]

    pltpu.make_async_copy(
        block_t.at[pl.ds(0, planes - 1)], block_t.at[pl.ds(0, planes - 1)], bk_recv
    ).wait()
    far_charge = pick_nt(pick, jnp.concatenate([block_t[z] for z in range(planes)], axis=1))
    far_sum = jnp.zeros((PER * LIST, BASIS), f32)
    for p in range(PC):
        far_sum = far_sum + far_charge[:, p : p + 1] * kern_f[p]
    far_rows = jnp.sum(far_sum.reshape(PER, LIST, BASIS), axis=1)
    potential = 0.25 * (near_rows + far_rows)
    col_s[...] = jnp.transpose(jnp.concatenate([potential, jnp.zeros((128 - PER, BASIS), f32)], axis=0))
    mine = col_s[pl.ds(ROWS * at_t, ROWS), :]
    for f in range(PER):
        esp_out[f] = 0.5 * over_v[f] * (mine[:, f : f + 1] + potential[f : f + 1, :])

    for copy in den:
        copy.wait_recv()
    keep.wait()
    for copy in sends:
        copy.wait_send()
    for end, step in ((groups - 1, 0), (0, 1)):

        @pl.when(at_g == end)
        def _():
            pltpu.make_async_copy(below, below, bd_send.at[step]).wait()

    for ref, count, sem in (
        (all_c, groups - 1, ac_send),
        (place_t, planes - 1, pl_send),
        (table, plane_frags - OWN, tb_send),
        (block_t, planes - 1, bk_send),
    ):
        pltpu.make_async_copy(ref.at[pl.ds(0, count)], ref.at[pl.ds(0, count)], sem).wait()


def store(density, esp, density_out, esp_out, sem):
    copies = [
        pltpu.make_async_copy(src, dst, sem.at[n])
        for n, (src, dst) in enumerate(((density, density_out), (esp, esp_out)))
    ]
    for copy in copies:
        copy.start()
    for copy in copies:
        copy.wait()


def per_device(
    planes,
    groups,
    core_fock,
    intersection,
    gamma_tile,
    charge_old,
    embed_old,
    core_pop,
    centres,
    frag_sizes,
    near_list,
    far_list,
):
    dma = pltpu.SemaphoreType.DMA
    smem = pl.BlockSpec(memory_space=pltpu.SMEM)
    hbm = pl.BlockSpec(memory_space=pltpu.HBM)
    vmem = pl.BlockSpec(memory_space=pltpu.VMEM)
    own = (PER, ROWS, BASIS)
    pieces = (ROWS, 128)
    plane_frags = groups * PER
    held = pl.pallas_call(
        functools.partial(kernel, planes, groups),
        out_shape=(pltpu.VMEM(own, f32), pltpu.VMEM(own, f32)),
        in_specs=[hbm] * 7 + [smem, smem, hbm],
        out_specs=(vmem, vmem),
        scratch_shapes=[
            pltpu.VMEM(own, f32),
            pltpu.VMEM(own, f32),
            pltpu.VMEM(own, f32),
            pltpu.VMEM((PER, BASIS), f32),
            pltpu.VMEM((PER, BASIS), f32),
            pltpu.VMEM((PER, BASIS), f32),
            pltpu.VMEM((PER, LIST), jnp.int32),
            pltpu.VMEM(own, f32),
            pltpu.VMEM(own, f32),
            pltpu.VMEM((2, 3) + pieces, f32),
            pltpu.VMEM((2, 1) + pieces, f32),
            pltpu.VMEM((2, 2) + pieces, f32),
            pltpu.VMEM((2, 3) + pieces, f32),
            pltpu.VMEM((2, 1) + pieces, f32),
            pltpu.VMEM((2, 2) + pieces, f32),
            pltpu.VMEM((TILES, 1, 128), f32),
            pltpu.VMEM((TILES, 1, 128), f32),
            pltpu.VMEM((3, 3, PER, BASIS), f32),
            pltpu.VMEM((groups, 3, PER, BASIS), f32),
            pltpu.VMEM((planes, 3, PC, 128), f32),
            pltpu.VMEM((PER, 4, BASIS, 128), f32),
            pltpu.VMEM((PER * LIST, planes * 128), bf16),
            pltpu.VMEM((PER * LIST, BASIS, BASIS), f32),
            pltpu.VMEM((PC, PER * LIST, BASIS), f32),
            pltpu.VMEM((OWN, BASIS, BASIS), f32),
            pltpu.VMEM((OWN, BASIS, BASIS), f32),
            pltpu.VMEM((TILES, OWN, ROWS, BASIS), f32),
            pltpu.VMEM((plane_frags + 2 * PER, 1, BASIS), f32),
            pltpu.VMEM((planes, PC, 128), f32),
            pltpu.VMEM((BASIS, 128), f32),
            dma((9,)),
            dma((2, 3)),
            dma((2, 3)),
            dma((3,)),
            dma((3,)),
            dma((2,)),
            dma((2,)),
            dma,
            dma,
            dma,
            dma,
            dma,
            dma,
            dma((2,)),
            dma((2,)),
            dma,
            dma,
            dma((3,)),
            dma((3,)),
            dma((1,)),
            pltpu.SemaphoreType.REGULAR((3,)),
        ],
        compiler_params=pltpu.CompilerParams(
            collective_id=0, has_side_effects=True, vmem_limit_bytes=60 * 1024 * 1024
        ),
        name="scc_cycle",
    )(
        core_fock,
        intersection,
        gamma_tile,
        charge_old,
        embed_old,
        core_pop,
        jnp.transpose(centres, (1, 0, 2)),
        frag_sizes,
        near_list,
        far_list,
    )
    return pl.pallas_call(
        store,
        out_shape=(jax.ShapeDtypeStruct(own, f32), jax.ShapeDtypeStruct(own, f32)),
        in_specs=[vmem, vmem],
        out_specs=(pl.BlockSpec(memory_space=pl.ANY), pl.BlockSpec(memory_space=pl.ANY)),
        scratch_shapes=[dma((2,))],
        compiler_params=pltpu.CompilerParams(vmem_limit_bytes=1024 * 1024),
        name="store",
    )(*held)


def solution(mesh):
    groups = mesh.shape["frag"] // PLANES
    return build(mesh, PLANES, groups)


def build(mesh, planes, groups):
    in_specs = (
        P("frag", "tile", None),
        P("frag", "tile", None),
        P("frag", "tile", None),
        P("frag", None),
        P("frag", None),
        P("frag", None),
        P("frag", None, None),
        P("frag"),
        P("frag", None),
        P("frag", None),
    )
    out_specs = (P("frag", "tile", None), P("frag", "tile", None))
    return jax.shard_map(
        functools.partial(per_device, planes, groups),
        mesh=mesh,
        in_specs=in_specs,
        out_specs=out_specs,
        check_vma=False,
    )
```

```python
import functools
import jax
import jax.numpy as jnp
from jax import lax
from jax.experimental import pallas as pl
from jax.experimental.pallas import tpu as pltpu
from jax.sharding import PartitionSpec as P

ITERS = 12
TILES = 4
ROWS = 64
BASIS = 256
PER = 8
OWN = 2
PC = 8
LIST = 8
PLANES = 8
FIRST_PAIRS = 30

f32 = jnp.float32
bf16 = jnp.bfloat16
HI = lax.Precision.HIGHEST
MESH = pl.DeviceIdType.MESH


def dot_nt(a, b):
    return lax.dot_general(a, b, (((1,), (1,)), ((), ())), precision=HI, preferred_element_type=f32)


def split(x):
    high = x.astype(bf16)
    return high, (x - high.astype(f32)).astype(bf16)


def dot3(a, b):
    (ah, al), (bh, bl) = a, b
    mul = functools.partial(jnp.dot, preferred_element_type=f32)
    return mul(ah, bh) + mul(ah, bl) + mul(al, bh)


def pick_nt(sel, b):
    high = b.astype(bf16)
    rest = b - high.astype(f32)
    middle = rest.astype(bf16)
    least = (rest - middle.astype(f32)).astype(bf16)
    mul = functools.partial(
        lax.dot_general, dimension_numbers=(((1,), (1,)), ((), ())), preferred_element_type=f32
    )
    return mul(sel, high) + mul(sel, middle) + mul(sel, least)


def lanes(shape):
    return lax.broadcasted_iota(jnp.int32, shape, len(shape) - 1)


def turn(x):
    return pltpu.roll(x, ROWS, axis=1)


def kernel(
    planes,
    groups,
    core_hbm,
    over_hbm,
    gamma_hbm,
    charge_hbm,
    embed_hbm,
    pop_hbm,
    centre_hbm,
    size_sm,
    near_sm,
    far_hbm,
    density_out,
    esp_out,
    core_v,
    over_v,
    gamma_v,
    charge_v,
    embed_v,
    pop_v,
    far_v,
    core_r,
    over_r,
    send1,
    send2,
    send3,
    got1,
    got2,
    got3,
    field_s,
    field_g,
    near_c,
    all_c,
    place_t,
    col_b,
    pick_v,
    kern_n,
    kern_f,
    est,
    over_f,
    dens_s,
    table,
    block_t,
    col_s,
    in_sem,
    raw_send,
    raw_recv,
    fld_send,
    fld_recv,
    nc_send,
    nc_recv,
    ac_send,
    ac_recv,
    pl_send,
    pl_recv,
    tb_send,
    tb_recv,
    bd_send,
    bd_recv,
    bk_send,
    bk_recv,
    dn_send,
    dn_recv,
    out_sem,
    ready,
):
    plane_frags = groups * PER
    at_f = lax.axis_index("frag")
    at_t = lax.axis_index("tile")
    at_z = at_f // groups
    at_g = lax.rem(at_f, groups)
    frag_devs = planes * groups

    def tile_peer(step):
        return (at_f, lax.rem(at_t + step, TILES))

    def frag_peer(step):
        return (lax.rem(at_f + frag_devs + step, frag_devs), at_t)

    deep = groups // 2
    ring = lambda n, size: min(n, size - n)
    steps = [(dx, dy, dc) for dx in range(TILES) for dy in range(deep) for dc in range(2)][1:]
    steps.sort(key=lambda s: (-ring(s[0], TILES) - ring(s[1], deep), -s[2]))
    at_c = lax.rem(at_g, 2)
    peer_x = [lax.rem(at_t + dx, TILES) for dx in range(TILES)]
    peer_g = [
        [at_z * groups + 2 * lax.rem(at_g // 2 + dy, deep) + (1 - at_c if dc else at_c) for dc in range(2)]
        for dy in range(deep)
    ]
    plane_devices = [(peer_g[dy][dc], peer_x[dx]) for dx, dy, dc in steps]

    def group_peer(step):
        return (at_z * groups + lax.rem(at_g + step, groups), at_t)

    def z_peer(step):
        return (lax.rem(at_z + planes + step, planes) * groups + at_g, at_t)

    loads = [
        pltpu.make_async_copy(src, dst, in_sem.at[n])
        for n, (src, dst) in enumerate(
            (
                (core_hbm, core_v),
                (over_hbm, over_v),
                (gamma_hbm, gamma_v),
                (charge_hbm, charge_v),
                (embed_hbm, embed_v),
                (pop_hbm, pop_v),
                (far_hbm, far_v),
                (centre_hbm, near_c.at[1]),
                (centre_hbm, all_c.at[at_g]),
            )
        )
    ]
    for load in loads:
        load.start()

    barrier = pltpu.get_barrier_semaphore()

    def signal(sem, device):
        pl.semaphore_signal(sem, inc=1, device_id=device, device_id_type=MESH)

    z_steps = sorted(range(1, planes), key=lambda n: -ring(n, planes))
    z_devices = [z_peer(step) for step in z_steps]
    tile_devices = [tile_peer(step) for step in (2, 1, 3)]
    first_devices = tile_devices + [frag_peer(1), frag_peer(-1), z_peer(1), z_peer(-1)]
    first_devices += [group_peer(step) for step in range(1, groups)]
    for device in first_devices:
        signal(barrier, device)

    back = lax.rem(BASIS - ROWS * at_t, BASIS)
    forth = ROWS * at_t
    lane128 = lanes((ROWS, 128))
    low = lane128 < ROWS
    to_prev = lax.rem(at_t + 3, TILES)
    to_opp = lax.rem(at_t + 2, TILES)
    to_next = lax.rem(at_t + 1, TILES)
    for n, (array, turned) in enumerate(((core_v, core_r), (over_v, over_r))):
        loads[n].wait()
        for f in range(PER):
            turned[f] = pltpu.roll(array[f], back, axis=1)
        firsts, pairs = [], []
        for e in range(OWN):
            mine = turned[OWN * to_prev + e]
            send1[n, e] = turn(mine[:, :128])
            firsts.append(mine[:, 128:])
            mine = turned[OWN * to_next + e]
            send3[n, e] = jnp.where(low, turn(mine[:, 128:]), turn(mine[:, :128]))
            pairs.append(turned[OWN * to_opp + e][:, :128])
        send1[n, 2] = jnp.where(low, firsts[0], turn(firsts[1]))
        send2[n, 0] = jnp.where(low, pairs[0], turn(pairs[1]))

    pl.semaphore_wait(barrier, len(first_devices))

    sends = []

    def push(src, dst, send_sem, recv_sem, device):
        copy = pltpu.make_async_remote_copy(
            src_ref=src,
            dst_ref=dst,
            send_sem=send_sem,
            recv_sem=recv_sem,
            device_id=device,
            device_id_type=MESH,
        )
        copy.start()
        sends.append(copy)
        return copy

    raw = [
        push(send2, got2, raw_send.at[1], raw_recv.at[1], tile_peer(2)),
        push(send1, got1, raw_send.at[0], raw_recv.at[0], tile_peer(3)),
        push(send3, got3, raw_send.at[2], raw_recv.at[2], tile_peer(1)),
    ]
    loads[7].wait()
    near = [
        push(near_c.at[1], near_c.at[0], nc_send.at[0], nc_recv.at[0], frag_peer(1)),
        push(near_c.at[1], near_c.at[2], nc_send.at[1], nc_recv.at[1], frag_peer(-1)),
    ]

    def spread_centres(step, carry):
        pltpu.make_async_remote_copy(
            src_ref=near_c.at[1],
            dst_ref=all_c.at[at_g],
            send_sem=ac_send,
            recv_sem=ac_recv,
            device_id=group_peer(step),
            device_id_type=MESH,
        ).start()
        return carry

    lax.fori_loop(1, groups, spread_centres, 0)
    for device in tile_devices:
        signal(ready.at[0], device)
    for step in (1, -1):
        signal(ready.at[1], z_peer(step))

    for n in (2, 3, 4):
        loads[n].wait()
    wide = (PER, PER * ROWS)
    prod = dot_nt(charge_v[...], gamma_v[...].reshape(PER * ROWS, BASIS))
    emb = pltpu.roll(embed_v[...], back, axis=1)[:, :128]
    emb = jnp.where(lanes((PER, 128)) < ROWS, emb, turn(emb))
    prod = prod + jnp.concatenate([emb] * 4, axis=1)
    same = lax.broadcasted_iota(jnp.int32, wide, 0) == lanes(wide) // ROWS
    fields = jnp.sum(jnp.where(same, prod, 0.0), axis=0, keepdims=True)
    for t in range(TILES):
        field_s[t] = fields[:, 128 * t : 128 * t + 128]
    fld = []
    for r in (2, 1, 3):
        dest = lax.rem(at_t + TILES - r, TILES)
        fld.append(
            push(field_s.at[dest], field_g.at[r], fld_send.at[r - 1], fld_recv.at[r - 1], (at_f, dest))
        )

    own = near_c[1]
    length = own[0] * own[0] + own[1] * own[1] + own[2] * own[2] + 1.0
    own = own.reshape(3 * PER, BASIS)
    cols = jnp.transpose(
        jnp.concatenate([own, length, jnp.zeros((128 - 4 * PER, BASIS), f32)], axis=0)
    )
    for f in range(PER):
        for d in range(3):
            n = d * PER + f
            col_b[f, d] = jnp.broadcast_to(cols[:, n : n + 1], (BASIS, 128))
        n = 3 * PER + f
        col_b[f, 3] = jnp.broadcast_to(cols[:, n : n + 1], (BASIS, 128))
    loads[6].wait()
    far_list = far_v[...].astype(f32)
    diag = lax.broadcasted_iota(jnp.int32, (LIST, LIST), 0) == lanes((LIST, LIST))
    far_at = [
        jnp.sum(jnp.where(diag, jnp.broadcast_to(far_list[f : f + 1], (LIST, LIST)), 0.0), axis=1, keepdims=True)
        for f in range(PER)
    ]
    far_at = jnp.broadcast_to(jnp.concatenate(far_at, axis=0), (PER * LIST, 128))
    lane64 = lanes((PER * LIST, 128))
    picks = []
    for z in range(planes):
        entry = jnp.where(lane64 < plane_frags, lane64 + z * plane_frags, -1).astype(f32)
        picks.append((far_at == entry).astype(f32))
    pick_v[...] = jnp.concatenate(picks, axis=1).astype(bf16)

    for copy in near:
        copy.wait_recv()
    pl.semaphore_wait(ready.at[1], 2)
    for step in (2, -2):
        signal(ready.at[2], z_peer(step))

    near_first = at_f * PER - PER

    def pair(n, carry):
        f = n // LIST
        other = jnp.clip(near_sm[f, lax.rem(n, LIST)] - near_first, 0, 3 * PER - 1)
        slot = other // PER
        row = other - slot * PER
        src = [near_c[slot, d, pl.ds(row, 1), :] for d in range(3)]
        src_length = src[0] * src[0] + src[1] * src[1] + src[2] * src[2]
        src = [-2.0 * x for x in src]
        for r in range(4):
            rows = slice(64 * r, 64 * r + 64)
            for h in range(2):
                cut = slice(128 * h, 128 * h + 128)
                dist = col_b[f, 3, rows, :] + src_length[:, cut]
                dot = col_b[f, 0, rows, :] * src[0][:, cut]
                for d in (1, 2):
                    dot = dot + col_b[f, d, rows, :] * src[d][:, cut]
                kern_n[n, rows, cut] = lax.rsqrt(dist + dot)
        return carry

    lax.fori_loop(0, FIRST_PAIRS, pair, 0)

    loads[8].wait()
    pltpu.make_async_copy(
        all_c.at[pl.ds(0, groups - 1)], all_c.at[pl.ds(0, groups - 1)], ac_recv
    ).wait()
    runs = lax.broadcasted_iota(jnp.int32, (PC, BASIS), 0) == lanes((PC, BASIS)) // (BASIS // PC)
    mean_run = (runs.astype(f32) * (PC / BASIS)).astype(bf16)
    sum_run = runs.astype(f32).astype(bf16)
    pad = jnp.zeros((PC, 128 - plane_frags), f32)
    for d in range(3):
        places = pick_nt(mean_run, all_c[:, d].reshape(plane_frags, BASIS))
        place_t[at_z, d] = jnp.concatenate([places, pad], axis=1)

    fld_rows = [field_s[at_t]]
    for copy in fld:
        copy.wait_recv()
    for r in (1, 2, 3):
        fld_rows.append(field_g[r])
    for copy in raw:
        copy.wait_recv()
    full_lanes = lanes((1, BASIS))
    low1 = lanes((1, 128)) < ROWS
    zero = jnp.zeros((ROWS, 128), f32)

    def halves(n, turned, e):
        top = turned[OWN * at_t + e]
        top = jnp.where(lanes((ROWS, BASIS)) < ROWS, 0.5 * top, top)
        one = got1[n, e]
        tail = got1[n, 2]
        tail = turn(tail) if e == 0 else tail
        opp = got2[n, 0]
        opp = opp if e == 0 else turn(opp)
        last = got3[n, e]
        return jnp.concatenate(
            [
                top,
                jnp.concatenate([jnp.where(low, 0.0, 0.5 * one), jnp.where(low, one, tail)], axis=1),
                jnp.concatenate([zero, jnp.where(low, 0.5 * opp, 0.0)], axis=1),
                jnp.concatenate([zero, jnp.where(low, last, 0.5 * last)], axis=1),
            ],
            axis=0,
        )

    square = (BASIS, BASIS)
    row_at = lax.broadcasted_iota(jnp.int32, square, 0)
    col_at = lanes(square)
    eye = (row_at == col_at).astype(f32)
    for e in range(OWN):
        half = halves(1, over_r, e)
        over = half + jnp.transpose(half)
        over_f[e] = over
        if e == 0:
            field = [jnp.where(low1, fld_rows[0], turn(fld_rows[1])), jnp.where(low1, fld_rows[2], turn(fld_rows[3]))]
        else:
            field = [jnp.where(low1, turn(fld_rows[0]), fld_rows[1]), jnp.where(low1, turn(fld_rows[2]), fld_rows[3])]
        field = jnp.concatenate(field, axis=1)
        half = halves(0, core_r, e) + 0.5 * over * field
        fock = half + jnp.transpose(half)
        size = size_sm[OWN * at_t + e]
        row_in = lax.rem(row_at + ROWS * at_t, BASIS) < size
        col_in = lax.rem(col_at + ROWS * at_t, BASIS) < size
        fock = jnp.where(row_in & col_in, fock, 0.0)
        total = jnp.sum(jnp.sum(fock * fock, axis=0, keepdims=True), axis=1, keepdims=True)
        fock = fock / jnp.sqrt(total + 1e-06)
        est[e] = fock + jnp.where(row_in, 0.0, eye)

    def near_product(a, b):
        mul = functools.partial(jnp.dot, preferred_element_type=f32)
        both = mul(jnp.concatenate(a, axis=0), b[0])
        rows = a[0].shape[0]
        return both[:rows] + both[rows:] + mul(a[0], b[1])

    def sweep(step, carry):
        now = [est[e] for e in range(OWN)]
        for _ in range(12):
            parts = [split(x) for x in now]
            cuts = [slice(r, r + 128) for r in range(0, BASIS, 128)]
            squares = [
                [split(near_product([p[cut] for p in part], part)) for cut in cuts] for part in parts
            ]
            now = [
                jnp.concatenate(
                    [1.5 * x[cut] - 0.5 * near_product(y, part) for cut, y in zip(cuts, square)], axis=0
                )
                for x, square, part in zip(now, squares, parts)
            ]
        for e in range(OWN):
            est[e] = now[e]
        return carry

    pl.semaphore_wait(ready.at[2], 2)

    def spread_places(step, carry):
        pltpu.make_async_remote_copy(
            src_ref=place_t.at[at_z],
            dst_ref=place_t.at[at_z],
            send_sem=pl_send,
            recv_sem=pl_recv,
            device_id=z_peer(step),
            device_id_type=MESH,
        ).start()
        return carry

    lax.fori_loop(1, planes, spread_places, 0)

    lax.fori_loop(0, ITERS // 12, sweep, 0)

    loads[5].wait()
    first = PER + at_g * PER + OWN * at_t
    for e in range(OWN):
        dens = 0.5 * (eye - est[e])
        charge = jnp.sum(dens * over_f[e], axis=0, keepdims=True)
        charge = pltpu.roll(jnp.broadcast_to(charge, (8, BASIS)), forth, axis=1)[0:1]
        charge = charge - pop_v[pl.ds(OWN * at_t + e, 1), :]
        table[first + e] = charge

    pl.semaphore_wait(ready.at[0], len(tile_devices))
    def to_next_plane(end, step, row):
        @pl.when(at_g == end)
        def _():
            for t in range(TILES):
                pltpu.make_async_remote_copy(
                    src_ref=table.at[pl.ds(first, OWN)],
                    dst_ref=table.at[pl.ds(row + OWN * at_t, OWN)],
                    send_sem=bd_send.at[step],
                    recv_sem=bd_recv.at[step],
                    device_id=(frag_peer(1 if step == 0 else -1)[0], t),
                    device_id_type=MESH,
                ).start()

    to_next_plane(groups - 1, 0, 0)
    to_next_plane(0, 1, plane_frags + PER)
    for device in plane_devices:
        pltpu.make_async_remote_copy(
            src_ref=table.at[pl.ds(first, OWN)],
            dst_ref=table.at[pl.ds(first, OWN)],
            send_sem=tb_send,
            recv_sem=tb_recv,
            device_id=device,
            device_id_type=MESH,
        ).start()

    for e in range(OWN):
        dens = pltpu.roll(0.5 * (eye - est[e]), forth, axis=1)
        for r in range(TILES):
            dens_s[r, e] = dens[ROWS * r : ROWS * r + ROWS]
    slot = density_out.at[pl.ds(OWN * at_t, OWN)]
    den = [push(dens_s.at[r], slot, dn_send.at[r - 1], dn_recv.at[r - 1], tile_peer(r)) for r in (2, 1, 3)]
    keep = pltpu.make_async_copy(dens_s.at[0], slot, out_sem.at[0])
    keep.start()

    pick = pick_v[...]
    pltpu.make_async_copy(
        place_t.at[pl.ds(0, planes - 1)], place_t.at[pl.ds(0, planes - 1)], pl_recv
    ).wait()
    far_place = pick_nt(
        pick, jnp.concatenate([place_t[z].reshape(3 * PC, 128) for z in range(planes)], axis=1)
    )
    spots = [
        jnp.concatenate([jnp.broadcast_to(near_c[1, d, f : f + 1, :], (LIST, BASIS)) for f in range(PER)], axis=0)
        for d in range(3)
    ]
    for p in range(PC):
        dist = 1.0
        for d in range(3):
            diff = spots[d] - far_place[:, d * PC + p : d * PC + p + 1]
            dist = dist + diff * diff
        kern_f[p] = lax.rsqrt(dist)

    lax.fori_loop(FIRST_PAIRS, PER * LIST, pair, 0)

    pltpu.make_async_copy(
        table.at[pl.ds(PER, plane_frags - OWN)], table.at[pl.ds(PER, plane_frags - OWN)], tb_recv
    ).wait()
    plane_charge = table[pl.ds(PER, plane_frags)].reshape(plane_frags, BASIS)
    block_t[at_z] = jnp.concatenate([pick_nt(sum_run, plane_charge), pad], axis=1)

    for device in z_devices:
        pltpu.make_async_remote_copy(
            src_ref=block_t.at[at_z],
            dst_ref=block_t.at[at_z],
            send_sem=bk_send,
            recv_sem=bk_recv,
            device_id=device,
            device_id_type=MESH,
        ).start()

    below = table.at[pl.ds(0, PER)]
    above = table.at[pl.ds(plane_frags + PER, PER)]

    @pl.when(at_g == 0)
    def _():
        pltpu.make_async_copy(below, below, bd_recv.at[0]).wait()

    @pl.when(at_g == groups - 1)
    def _():
        pltpu.make_async_copy(above, above, bd_recv.at[1]).wait()

    table_first = at_z * plane_frags - PER
    lane256 = lanes((BASIS, 128))
    near_cols = jnp.zeros((BASIS, 128), f32)

    def near_sum(f):
        acc = jnp.zeros((BASIS, 128), f32)
        for k in range(LIST):
            row = table[jnp.clip(near_sm[f, k] - table_first, 0, plane_frags + 2 * PER - 1)]
            acc = acc + kern_n[f * LIST + k, :, :128] * row[:, :128]
            acc = acc + kern_n[f * LIST + k, :, 128:] * row[:, 128:]
        return jnp.sum(acc, axis=1, keepdims=True)

    def near_step(f, cols):
        return jnp.where(lane256 == f, near_sum(f), cols)

    near_cols = lax.fori_loop(0, PER, near_step, near_cols)
    near_rows = jnp.transpose(near_cols)[:PER]

    pltpu.make_async_copy(
        block_t.at[pl.ds(0, planes - 1)], block_t.at[pl.ds(0, planes - 1)], bk_recv
    ).wait()
    far_charge = pick_nt(pick, jnp.concatenate([block_t[z] for z in range(planes)], axis=1))
    far_sum = jnp.zeros((PER * LIST, BASIS), f32)
    for p in range(PC):
        far_sum = far_sum + far_charge[:, p : p + 1] * kern_f[p]
    far_rows = jnp.sum(far_sum.reshape(PER, LIST, BASIS), axis=1)
    potential = 0.25 * (near_rows + far_rows)
    col_s[...] = jnp.transpose(jnp.concatenate([potential, jnp.zeros((128 - PER, BASIS), f32)], axis=0))
    mine = col_s[pl.ds(ROWS * at_t, ROWS), :]
    for f in range(PER):
        esp_out[f] = 0.5 * over_v[f] * (mine[:, f : f + 1] + potential[f : f + 1, :])

    for copy in den:
        copy.wait_recv()
    keep.wait()
    for copy in sends:
        copy.wait_send()
    for end, step in ((groups - 1, 0), (0, 1)):

        @pl.when(at_g == end)
        def _():
            pltpu.make_async_copy(below, below, bd_send.at[step]).wait()

    for ref, count, sem in (
        (all_c, groups - 1, ac_send),
        (place_t, planes - 1, pl_send),
        (table, plane_frags - OWN, tb_send),
        (block_t, planes - 1, bk_send),
    ):
        pltpu.make_async_copy(ref.at[pl.ds(0, count)], ref.at[pl.ds(0, count)], sem).wait()


def store(density, esp, density_out, esp_out, sem):
    copies = [
        pltpu.make_async_copy(src, dst, sem.at[n])
        for n, (src, dst) in enumerate(((density, density_out), (esp, esp_out)))
    ]
    for copy in copies:
        copy.start()
    for copy in copies:
        copy.wait()


def per_device(
    planes,
    groups,
    core_fock,
    intersection,
    gamma_tile,
    charge_old,
    embed_old,
    core_pop,
    centres,
    frag_sizes,
    near_list,
    far_list,
):
    dma = pltpu.SemaphoreType.DMA
    smem = pl.BlockSpec(memory_space=pltpu.SMEM)
    hbm = pl.BlockSpec(memory_space=pltpu.HBM)
    vmem = pl.BlockSpec(memory_space=pltpu.VMEM)
    own = (PER, ROWS, BASIS)
    pieces = (ROWS, 128)
    plane_frags = groups * PER
    held = pl.pallas_call(
        functools.partial(kernel, planes, groups),
        out_shape=(pltpu.VMEM(own, f32), pltpu.VMEM(own, f32)),
        in_specs=[hbm] * 7 + [smem, smem, hbm],
        out_specs=(vmem, vmem),
        scratch_shapes=[
            pltpu.VMEM(own, f32),
            pltpu.VMEM(own, f32),
            pltpu.VMEM(own, f32),
            pltpu.VMEM((PER, BASIS), f32),
            pltpu.VMEM((PER, BASIS), f32),
            pltpu.VMEM((PER, BASIS), f32),
            pltpu.VMEM((PER, LIST), jnp.int32),
            pltpu.VMEM(own, f32),
            pltpu.VMEM(own, f32),
            pltpu.VMEM((2, 3) + pieces, f32),
            pltpu.VMEM((2, 1) + pieces, f32),
            pltpu.VMEM((2, 2) + pieces, f32),
            pltpu.VMEM((2, 3) + pieces, f32),
            pltpu.VMEM((2, 1) + pieces, f32),
            pltpu.VMEM((2, 2) + pieces, f32),
            pltpu.VMEM((TILES, 1, 128), f32),
            pltpu.VMEM((TILES, 1, 128), f32),
            pltpu.VMEM((3, 3, PER, BASIS), f32),
            pltpu.VMEM((groups, 3, PER, BASIS), f32),
            pltpu.VMEM((planes, 3, PC, 128), f32),
            pltpu.VMEM((PER, 4, BASIS, 128), f32),
            pltpu.VMEM((PER * LIST, planes * 128), bf16),
            pltpu.VMEM((PER * LIST, BASIS, BASIS), f32),
            pltpu.VMEM((PC, PER * LIST, BASIS), f32),
            pltpu.VMEM((OWN, BASIS, BASIS), f32),
            pltpu.VMEM((OWN, BASIS, BASIS), f32),
            pltpu.VMEM((TILES, OWN, ROWS, BASIS), f32),
            pltpu.VMEM((plane_frags + 2 * PER, 1, BASIS), f32),
            pltpu.VMEM((planes, PC, 128), f32),
            pltpu.VMEM((BASIS, 128), f32),
            dma((9,)),
            dma((3,)),
            dma((3,)),
            dma((3,)),
            dma((3,)),
            dma((2,)),
            dma((2,)),
            dma,
            dma,
            dma,
            dma,
            dma,
            dma,
            dma((2,)),
            dma((2,)),
            dma,
            dma,
            dma((3,)),
            dma((3,)),
            dma((1,)),
            pltpu.SemaphoreType.REGULAR((3,)),
        ],
        compiler_params=pltpu.CompilerParams(
            collective_id=0, has_side_effects=True, vmem_limit_bytes=60 * 1024 * 1024
        ),
        name="scc_cycle",
    )(
        core_fock,
        intersection,
        gamma_tile,
        charge_old,
        embed_old,
        core_pop,
        jnp.transpose(centres, (1, 0, 2)),
        frag_sizes,
        near_list,
        far_list,
    )
    return pl.pallas_call(
        store,
        out_shape=(jax.ShapeDtypeStruct(own, f32), jax.ShapeDtypeStruct(own, f32)),
        in_specs=[vmem, vmem],
        out_specs=(pl.BlockSpec(memory_space=pl.ANY), pl.BlockSpec(memory_space=pl.ANY)),
        scratch_shapes=[dma((2,))],
        compiler_params=pltpu.CompilerParams(vmem_limit_bytes=1024 * 1024),
        name="store",
    )(*held)


def solution(mesh):
    groups = mesh.shape["frag"] // PLANES
    return build(mesh, PLANES, groups)


def build(mesh, planes, groups):
    in_specs = (
        P("frag", "tile", None),
        P("frag", "tile", None),
        P("frag", "tile", None),
        P("frag", None),
        P("frag", None),
        P("frag", None),
        P("frag", None, None),
        P("frag"),
        P("frag", None),
        P("frag", None),
    )
    out_specs = (P("frag", "tile", None), P("frag", "tile", None))
    return jax.shard_map(
        functools.partial(per_device, planes, groups),
        mesh=mesh,
        in_specs=in_specs,
        out_specs=out_specs,
        check_vma=False,
    )
```
